32 devices in a mesh: batch: 8 (over z, y), seq: 4 (over x, core).
Axes of the slice: x: 2, y: 2, z: 4, core: 2. Of those that a mesh axis runs over, the one named last changes fastest.
Arguments:
- source_tokens: bfloat16 [8, 1024, 1024], P('batch', 'seq'), may hold values from -6 to 6
- target_tokens: bfloat16 [8, 1024, 1024], P('batch', 'seq'), may hold values from -6 to 6
- source_lengths: int32 [8, 16], P('batch'), may hold values from 1 to 512, 1024 in all within a row
- target_lengths: int32 [8, 16], P('batch'), may hold values from 1 to 512, 1024 in all within a row
- projections: bfloat16 [3, 1024, 3072], P(None, 'batch'), may hold values from -0.1875 to 0.1875
- combiners: bfloat16 [3, 1024, 1024], P(None, 'batch'), may hold values from -0.75 to 0.75
- expanders: bfloat16 [2, 1024, 4096], P(None, 'batch'), may hold values from -0.1875 to 0.1875
- reducers: bfloat16 [2, 4096, 1024], P(None, 'batch'), may hold values from -0.09375 to 0.09375
- norm_gains: float32 [5, 1024], replicated, may hold values from 0.5 to 1.5
- norm_shifts: float32 [5, 1024], replicated, may hold values from -1.2 to 1.2
- attention_biases: float32 [3, 3, 1024], replicated, may hold values from -0.6 to 0.6
- expander_biases: float32 [2, 4096], replicated, may hold values from -1.2 to 1.2
- reducer_biases: float32 [2, 1024], replicated, may hold values from -1.2 to 1.2
- source_cotangent: bfloat16 [8, 1024, 1024], P('batch', 'seq'), may hold values from -6 to 6
- target_cotangent: bfloat16 [8, 1024, 1024], P('batch', 'seq'), may hold values from -6 to 6
Outputs:
- encoder_output: bfloat16 [8, 1024, 1024], P('batch', 'seq')
- decoder_output: bfloat16 [8, 1024, 1024], P('batch', 'seq')
- source_gradient: float32 [8, 1024, 1024], P('batch', 'seq')
- target_gradient: float32 [8, 1024, 1024], P('batch', 'seq')
- projections_gradient: float32 [3, 1024, 3072], P(None, 'batch')
- combiners_gradient: float32 [3, 1024, 1024], P(None, 'batch')
- expanders_gradient: float32 [2, 1024, 4096], P(None, 'batch')
- reducers_gradient: float32 [2, 4096, 1024], P(None, 'batch')
- gains_gradient: float32 [5, 1024], replicated
- shifts_gradient: float32 [5, 1024], replicated
- attention_biases_gradient: float32 [3, 3, 1024], replicated
- expander_biases_gradient: float32 [2, 4096], replicated
- reducer_biases_gradient: float32 [2, 1024], replicated
The draws below stay inside these ranges and needn't reach their ends.
Inputs may be any that keep to these rules, and one draw needn't show every extreme that they name: `source_lengths`: in every row the 16 entries sum to 1024; the last entry counts the padding tokens at the row's end; the largest entry is 512. `target_lengths`: in every row the 16 entries sum to 1024; the last entry counts the padding tokens at the row's end; the largest entry is 512.
All inputs are finite; a program needn't handle non-finite values.
Results may differ from the reference program's by a relative error of at most 0.025.
Values may be sent and summed in bfloat16 or wider, within the bound.
No kernel may reach another device: no remote copies, remote signals or barrier semaphores. Data moves between devices by JAX's collectives and lax.ppermute only.
A program may use at most 384 MiB of HBM per device.

```python
import math
import jax
import jax.numpy as jnp
import numpy as np
from jax import lax

D = 1024
FF = 4096
HEADS = 16
HEAD_DIM = 64
SEGS = 16
ROW_LEN = 1024
SEG_MOST = 512
ROWS = 8


def shard_levels(stream_key, extent, cuts, low, top_value):
    loudness, own = 1.0, jax.random.fold_in(stream_key, 6)
    for axis_at, blocks in cuts:
        draws = jnp.exp(jax.random.uniform(jax.random.fold_in(own, axis_at), (blocks,), jnp.float32, low / len(cuts), top_value / len(cuts)))
        loudness = loudness * jnp.repeat(draws, extent[axis_at] // blocks).reshape([-1 if axis == axis_at else 1 for axis in range(len(extent))])
    return loudness


def length_profile(amount, total, reach, slope):
    loads = [(1 << 20) // math.isqrt(grade ** slope) + 1 for grade in range(2, amount + 1)]
    spare, holding = total - reach - (amount - 1), [1] * (amount - 1)
    while spare > 0:
        movable = [i for i in range(amount - 1) if holding[i] < reach]
        whole, left = sum([loads[i] for i in movable]), spare
        for i in movable:
            addition = min(reach - holding[i], max(1, left * loads[i] // whole), spare)
            holding[i] = holding[i] + addition
            spare = spare - addition
    return np.array([reach] + holding)


def ragged_sizes(rng, count, total, reach, lean):
    if count == 2:
        one = jax.random.randint(rng, (), max(1, total - reach), min(reach, total - 1) + 1)
        return jnp.stack([one, total - one])
    tallies = jnp.asarray(length_profile(count, total, reach, lean), jnp.int32)
    twos = (count - 1) // 2
    donor, receiver = tallies[1:1 + 2 * twos:2], tallies[2:2 + 2 * twos:2]
    margin = jnp.minimum(donor - 1, reach - receiver)
    moved = jax.random.randint(jax.random.fold_in(rng, 1), (twos,), 0, 1 << 20) % (margin + 1)
    tallies = tallies.at[1:1 + 2 * twos:2].set(donor - moved).at[2:2 + 2 * twos:2].set(receiver + moved)
    return tallies[jax.random.permutation(jax.random.fold_in(rng, 2), count)]


def bell_draw(key, extent, scale, reach, cuts=(), kind=jnp.bfloat16):
    values = jax.random.normal(key, extent, jnp.float32) * scale
    if len(cuts) > 0:
        values = shard_levels(key, extent, cuts, -0.22, 0.18) * values
    return jnp.clip(values, min=-reach, max=reach).astype(kind)


def setup_inputs(seed: int = 0) -> dict:
    seeds = jax.random.split(jax.random.key(seed), 16)
    return {
        "source_tokens": bell_draw(seeds[0], (ROWS, ROW_LEN, D), 1.0, 6.0, ((0, 8), (1, 4))),
        "target_tokens": bell_draw(seeds[1], (ROWS, ROW_LEN, D), 1.0, 6.0, ((0, 8), (1, 4))),
        "source_lengths": jax.vmap(lambda own: ragged_sizes(own, SEGS, ROW_LEN, SEG_MOST, 2))(jax.random.split(seeds[2], ROWS)).reshape((ROWS, SEGS)).astype(jnp.int32),
        "target_lengths": jax.vmap(lambda own: ragged_sizes(own, SEGS, ROW_LEN, SEG_MOST, 2))(jax.random.split(seeds[3], ROWS)).reshape((ROWS, SEGS)).astype(jnp.int32),
        "projections": bell_draw(seeds[4], (3, D, 3 * D), D ** -0.5, 0.1875, ((1, 8),)),
        "combiners": bell_draw(seeds[5], (3, D, D), (D // 16) ** -0.5, 0.75, ((1, 8),)),
        "expanders": bell_draw(seeds[6], (2, D, FF), D ** -0.5, 0.1875, ((1, 8),)),
        "reducers": bell_draw(seeds[7], (2, FF, D), FF ** -0.5, 0.09375, ((1, 8),)),
        "norm_gains": jnp.clip(1.0 + 0.1 * jax.random.normal(seeds[8], (5, D), jnp.float32), 0.5, 1.5),
        "norm_shifts": bell_draw(seeds[9], (5, D), 0.2, 1.2, (), jnp.float32),
        "attention_biases": bell_draw(seeds[10], (3, 3, D), 0.1, 0.6, (), jnp.float32),
        "expander_biases": bell_draw(seeds[11], (2, FF), 0.2, 1.2, (), jnp.float32),
        "reducer_biases": bell_draw(seeds[12], (2, D), 0.2, 1.2, (), jnp.float32),
        "source_cotangent": bell_draw(seeds[13], (ROWS, ROW_LEN, D), 1.0, 6.0, ((0, 8), (1, 4))),
        "target_cotangent": bell_draw(seeds[14], (ROWS, ROW_LEN, D), 1.0, 6.0, ((0, 8), (1, 4))),
    }


epsilon = 1e-05
masked_score = -1e+30
highest = lax.Precision.HIGHEST

@jax.custom_vjp
def low(v):
    return lax.optimization_barrier(v.astype(jnp.bfloat16)).astype(jnp.float32)

@jax.custom_vjp
def low_back(v):
    return v

def low_keep(v):
    return (low(v), None)

def low_pass(kept, grad):
    return (grad,)

def back_keep(v):
    return (v, None)

def back_low(kept, grad):
    return (low(grad),)
low.defvjp(low_keep, low_pass)
low_back.defvjp(back_keep, back_low)

def layer_norm(values, gain_vec, offset):
    middle = lax.optimization_barrier(jnp.mean(values, -1, keepdims=True))
    centred = values - middle
    spread = lax.optimization_barrier(jnp.mean(centred * centred, -1, keepdims=True))
    return centred * lax.rsqrt(spread + epsilon) * gain_vec + offset

def product(left, right):
    return jnp.dot(left, right, precision=highest)

def segment_ids(lengths, row_count):
    ends = jnp.cumsum(lengths, axis=-1, dtype=jnp.int32)
    places = jnp.arange(row_count, dtype=jnp.int32)
    return lax.optimization_barrier(jnp.sum((places[None, :, None] >= ends[:, None, :]).astype(jnp.int32), axis=-1, dtype=jnp.int32))

def split_heads(values):
    return values.reshape(values.shape[0], HEADS, HEAD_DIM).transpose(1, 0, 2)

def attend(queries, key_rows, value_rows, key_mask):
    factor = float(HEAD_DIM) ** (-0.5)

    def one_head(head_parts):
        query_head, key_head, value_head = head_parts
        scores = low_back(jnp.dot(query_head, key_head.T, precision=highest) * factor)
        weights = jax.nn.softmax(jnp.where(key_mask, scores, masked_score), axis=-1)
        return jnp.dot(low(weights), value_head, precision=highest)
    mixture = lax.map(jax.checkpoint(one_head), (split_heads(queries), split_heads(key_rows), split_heads(value_rows)))
    return mixture.transpose(1, 0, 2).reshape(queries.shape)

def finish_attention(inputs, queries, key_rows, value_rows, key_mask, exit_matrix, biases):
    mixture = low_back(low(attend(queries, key_rows, value_rows, key_mask)))
    return inputs + low_back(product(mixture, exit_matrix)) + biases[2]

def self_block(inputs, key_mask, gain_vec, offset, entry_matrix, exit_matrix, biases):
    normed = low(layer_norm(inputs, gain_vec, offset))
    queries = low(low_back(product(normed, entry_matrix[:, :D])) + biases[0])
    key_rows = low(low_back(product(normed, entry_matrix[:, D:2 * D])))
    value_rows = low(low_back(product(normed, entry_matrix[:, 2 * D:])) + biases[1])
    return finish_attention(inputs, queries, key_rows, value_rows, key_mask, exit_matrix, biases)

def cross_block(inputs, memory, key_mask, gain_vec, offset, entry_matrix, exit_matrix, biases):
    normed = low(layer_norm(inputs, gain_vec, offset))
    source = low(memory)
    queries = low(low_back(product(normed, entry_matrix[:, :D])) + biases[0])
    key_rows = low(low_back(product(source, entry_matrix[:, D:2 * D])))
    value_rows = low(low_back(product(source, entry_matrix[:, 2 * D:])) + biases[1])
    return finish_attention(inputs, queries, key_rows, value_rows, key_mask, exit_matrix, biases)

def feedforward_block(inputs, gain_vec, offset, entry_matrix, exit_matrix, entry_bias, exit_bias):
    normed = low(layer_norm(inputs, gain_vec, offset))
    hidden = low_back(product(normed, entry_matrix)) + entry_bias
    active = low(jax.nn.gelu(hidden, approximate=False))
    return inputs + low_back(product(active, exit_matrix)) + exit_bias

def layer_pair(params, source, target, encoder_mask, self_mask, cross_mask):
    projections, combiners, expanders, reducers, gains, shifts, attention_biases, expander_biases, reducer_biases = params
    middle = self_block(source, encoder_mask, gains[0], shifts[0], projections[0], combiners[0], attention_biases[0])
    memory = feedforward_block(middle, gains[1], shifts[1], expanders[0], reducers[0], expander_biases[0], reducer_biases[0])
    self_out = self_block(target, self_mask, gains[2], shifts[2], projections[1], combiners[1], attention_biases[1])
    cross_out = cross_block(self_out, memory, cross_mask, gains[3], shifts[3], projections[2], combiners[2], attention_biases[2])
    decoded = feedforward_block(cross_out, gains[4], shifts[4], expanders[1], reducers[1], expander_biases[1], reducer_biases[1])
    return (memory, decoded)

def reference(source_tokens, target_tokens, source_lengths, target_lengths, projections, combiners, expanders, reducers, norm_gains, norm_shifts, attention_biases, expander_biases, reducer_biases, source_cotangent, target_cotangent):
    params = (projections.astype(jnp.float32), combiners.astype(jnp.float32), expanders.astype(jnp.float32), reducers.astype(jnp.float32), norm_gains.astype(jnp.float32), norm_shifts.astype(jnp.float32), attention_biases.astype(jnp.float32), expander_biases.astype(jnp.float32), reducer_biases.astype(jnp.float32))
    places = jnp.arange(ROW_LEN, dtype=jnp.int32)
    causal = places[:, None] >= places[None, :]

    def row_step(totals, row):
        source, target, source_len, target_len, source_cot, target_cot = row
        source_segment = segment_ids(source_len[None], ROW_LEN)[0]
        target_segment = segment_ids(target_len[None], ROW_LEN)[0]
        encoder_mask = source_segment[:, None] == source_segment[None, :]
        self_mask = (target_segment[:, None] == target_segment[None, :]) & causal
        cross_mask = target_segment[:, None] == source_segment[None, :]

        def forward(weights, source_in, target_in):
            return layer_pair(weights, source_in, target_in, encoder_mask, self_mask, cross_mask)
        outputs, pullback = jax.vjp(forward, params, source.astype(jnp.float32), target.astype(jnp.float32))
        keep_source = (source_segment < SEGS - 1).astype(jnp.float32)[:, None]
        keep_target = (target_segment < SEGS - 1).astype(jnp.float32)[:, None]
        grads, source_grad, target_grad = pullback((source_cot.astype(jnp.float32) * keep_source, target_cot.astype(jnp.float32) * keep_target))
        totals = jax.tree.map(jnp.add, totals, grads)
        return (totals, (outputs[0].astype(jnp.bfloat16), outputs[1].astype(jnp.bfloat16), source_grad, target_grad))
    start = jax.tree.map(jnp.zeros_like, params)
    totals, (encoder_output, decoder_output, source_gradient, target_gradient) = lax.scan(row_step, start, (source_tokens, target_tokens, source_lengths, target_lengths, source_cotangent, target_cotangent))
    return (encoder_output, decoder_output, source_gradient, target_gradient, totals[0], totals[1], totals[2], totals[3], totals[4], totals[5], totals[6], totals[7], totals[8])
```

```python
import jax
import jax.numpy as jnp
from jax import lax
from jax.sharding import PartitionSpec as P

HEADS = 16


epsilon = 1e-05
masked_score = -1e30
low = jnp.bfloat16


def layer_norm(values, gain_vec, offset):
    middle = jnp.mean(values, -1, keepdims=True)
    centred = values - middle
    spread_out = jnp.mean(centred * centred, -1, keepdims=True)
    return centred * lax.rsqrt(spread_out + epsilon) * gain_vec + offset


def gelu_exact(values):
    return jax.nn.gelu(values, approximate=False)


def times(left, right):
    return jnp.einsum("sd,de->se", left, right, preferred_element_type=jnp.float32)


def times_back(incoming, weight):
    return jnp.einsum("se,de->sd", incoming, weight, preferred_element_type=jnp.float32)


def outer_sum(left, incoming):
    return jnp.einsum("sd,se->de", left, incoming, preferred_element_type=jnp.float32)


def seq_bits():
    bit, bits = lax.axis_size("seq") >> 1, []
    while bit:
        bits.append(bit)
        bit >>= 1
    return bits


def seq_offsets():
    offsets = [0]
    for bit in seq_bits():
        offsets = offsets + [offset ^ bit for offset in offsets]
    return offsets


def swap(values, bit, axis="seq"):
    return lax.ppermute(values, axis, [(i, i ^ bit) for i in range(lax.axis_size(axis))])


def spread(rows):
    for bit in seq_bits():
        rows = jnp.concatenate([rows, swap(rows, bit)], 0)
    return rows


def collect(partial):
    for bit in reversed(seq_bits()):
        half = partial.shape[0] // 2
        arrived = swap(partial[half:].astype(low), bit)
        partial = partial[:half].astype(jnp.float32) + arrived.astype(jnp.float32)
    return partial


def in_order(spread_blocks):
    me = lax.axis_index("seq")
    offsets = jnp.array([seq_offsets().index(i) for i in range(lax.axis_size("seq"))], jnp.int32)
    return [
        lax.dynamic_index_in_dim(spread_blocks, offsets[me ^ i], 0, keepdims=False)
        for i in range(lax.axis_size("seq"))
    ]


def sum_everywhere(values):
    for axis in ("seq", "batch"):
        bit = 1
        while bit < lax.axis_size(axis):
            values = values + swap(values, bit, axis)
            bit <<= 1
    return values


def mine(values, axis):
    return lax.dynamic_index_in_dim(values, lax.axis_index("seq"), axis, keepdims=False)


def gather_batch(values):
    return lax.all_gather(values, "batch", axis=0, tiled=False)


def scatter_batch(values):
    return lax.psum_scatter(values, "batch", scatter_dimension=0, tiled=False)


def deals_by_line():
    return lax.axis_size("batch") == 2 * lax.axis_size("seq")


def line_pairs(step, count, back):
    pairs = []
    for place in range(count):
        for side in range(2):
            here = (place * 2 + side) * count + place
            there = (((place + step) % count) * 2 + side) * count + place
            pairs.append((there, here) if back else (here, there))
    return pairs


def deal_combiners(combiners):
    count = lax.axis_size("seq")
    me = lax.axis_index("seq")
    place = lax.axis_index("batch") // 2
    rows = combiners.shape[1] // count
    parts = combiners.reshape(combiners.shape[0], count, rows, combiners.shape[2])
    own = lax.dynamic_index_in_dim(parts, me, 1, keepdims=False)
    piece = jnp.where(place == me, own, jnp.zeros_like(own))
    for step in range(1, count):
        sent = lax.dynamic_index_in_dim(parts, (me + step) % count, 1, keepdims=False)
        piece = piece + lax.ppermute(sent, ("batch", "seq"), line_pairs(step, count, False))
    return piece


def return_combiners(pieces):
    count = lax.axis_size("seq")
    me = lax.axis_index("seq")
    place = lax.axis_index("batch") // 2
    arrived = [pieces] + [
        lax.ppermute(pieces, ("batch", "seq"), line_pairs(step, count, True))
        for step in range(1, count)
    ]
    ring = jnp.stack(arrived + arrived[:-1], 1)
    ordered = lax.dynamic_slice_in_dim(ring, (count - me) % count, count, 1)
    ordered = ordered.reshape(pieces.shape[0], count * pieces.shape[1], pieces.shape[2])
    for bit in seq_bits():
        ordered = jnp.where((place & bit) == (me & bit), ordered, swap(ordered, bit))
    return ordered


def pack_lanes(piece, rows):
    lanes = piece.shape[0] * piece.shape[1] // rows
    return piece.reshape(piece.shape[0], -1, lanes).transpose(1, 0, 2).reshape(rows, lanes)


def unpack_lanes(packed, rows):
    lanes = packed.shape[1]
    return packed.reshape(-1, rows, lanes).transpose(1, 0, 2).reshape(rows, -1)


def fetch_attention(projections, combiner, dealt):
    count = lax.axis_size("seq")
    rows, width = projections.shape
    share = mine(projections.reshape(rows, 3, count, width // 3 // count), 2).reshape(rows, -1)
    if dealt is None:
        entry = gather_batch(share).reshape(-1, share.shape[1])
        whole = gather_batch(combiner).reshape(count, -1, combiner.shape[1])
        return entry, mine(whole, 0)
    packed = gather_batch(jnp.concatenate([share, pack_lanes(dealt, rows)], 1))
    entry = packed[..., : share.shape[1]].reshape(-1, share.shape[1])
    pieces = packed[..., share.shape[1] :]
    lanes = pieces.shape[-1]
    pieces = pieces.reshape(count, 2, -1, dealt.shape[0], lanes)
    leave = pieces.transpose(1, 0, 3, 2, 4).reshape(-1, dealt.shape[1])
    return entry, leave


def fetch_feedforward(expander, reducer):
    count = lax.axis_size("seq")
    rows, width = expander.shape
    shards = lax.axis_size("batch")
    share_in = mine(expander.reshape(rows, shards, count, -1), 2).reshape(rows, -1)
    share_out = mine(reducer.reshape(count, -1, reducer.shape[1]), 0)
    if share_in.shape[1] != share_out.shape[1]:
        entry = gather_batch(share_in)
        leave = gather_batch(share_out)
    else:
        packed = gather_batch(jnp.concatenate([share_in, share_out], 0))
        entry, leave = packed[:, :rows], packed[:, rows:]
    return entry.reshape(-1, share_in.shape[1]), leave.reshape(-1, share_out.shape[1])


def send_attention(entry_gradient, exit_gradient):
    shards, count = lax.axis_size("batch"), lax.axis_size("seq")
    entry = entry_gradient.astype(low).reshape(shards, -1, entry_gradient.shape[1])
    if not deals_by_line():
        width = exit_gradient.shape[1]
        me = lax.axis_index("seq")
        whole = jnp.zeros((count,) + exit_gradient.shape, low)
        whole = lax.dynamic_update_slice(whole, exit_gradient.astype(low)[None], (me, 0, 0))
        leave = scatter_batch(whole.reshape(shards, -1, width))
        return scatter_batch(entry), leave
    rows = entry.shape[1]
    piece_rows = exit_gradient.shape[0] // shards
    lanes = piece_rows * exit_gradient.shape[1] // rows
    leave = exit_gradient.astype(low).reshape(2, count, piece_rows, -1, lanes)
    leave = leave.transpose(1, 0, 3, 2, 4).reshape(shards, rows, lanes)
    packed = scatter_batch(jnp.concatenate([entry, leave], 2))
    return packed[:, : entry.shape[2]], unpack_lanes(packed[:, entry.shape[2] :], piece_rows)


def send_feedforward(entry_gradient, exit_gradient):
    shards = lax.axis_size("batch")
    entry = entry_gradient.astype(low).reshape(shards, -1, entry_gradient.shape[1])
    leave = exit_gradient.astype(low).reshape(shards, -1, exit_gradient.shape[1])
    if entry.shape[2] != leave.shape[2]:
        return scatter_batch(entry), scatter_batch(leave)
    packed = scatter_batch(jnp.concatenate([entry, leave], 1))
    return packed[: entry.shape[1]], packed[entry.shape[1] :]


def finish_weights(attention_parts, feedforward_parts):
    shards, count = lax.axis_size("batch"), lax.axis_size("seq")
    entries = jnp.stack([part[0] for part in attention_parts])
    leaves = jnp.stack([part[1] for part in attention_parts])
    expands = jnp.stack([part[0] for part in feedforward_parts])
    reduces = jnp.stack([part[1] for part in feedforward_parts])
    if deals_by_line():
        leaves = return_combiners(leaves)
    else:
        leaves = lax.psum(leaves, "seq")
    entry_all = in_order(spread(entries[None]))
    expand_all = in_order(spread(expands[None]))
    reduce_all = in_order(spread(reduces[None]))
    blocks, rows, width = entries.shape
    projections = jnp.stack([part.reshape(blocks, rows, 3, width // 3) for part in entry_all], 3)
    blocks_out, rows_out, width_out = expands.shape
    expanders = jnp.stack(
        [part.reshape(blocks_out, rows_out, shards, width_out // shards) for part in expand_all], 3
    )
    reducers = jnp.stack(reduce_all, 1)
    return (
        projections.reshape(blocks, rows, -1).astype(jnp.float32),
        leaves.astype(jnp.float32),
        expanders.reshape(blocks_out, rows_out, -1).astype(jnp.float32),
        reducers.reshape(reduces.shape[0], -1, reduces.shape[2]).astype(jnp.float32),
    )


def split_heads(values, width):
    return values.reshape(values.shape[0], values.shape[1] // width, width)


def attend_forward(queries, keys, values, key_mask, width):
    factor = float(width) ** (-0.5)
    raw_scores = (
        jnp.einsum(
            "qhc,khc->hqk",
            split_heads(queries, width),
            split_heads(keys, width),
            preferred_element_type=jnp.float32,
        )
        * factor
    )
    scores = jnp.where(key_mask[None], raw_scores, masked_score)
    row_max = jnp.max(scores, -1, keepdims=True)
    exponent = jnp.exp(scores - row_max)
    row_sum = jnp.sum(exponent, -1, keepdims=True)
    weights = (exponent / row_sum).astype(low)
    mixture = jnp.einsum(
        "hqk,khc->qhc", weights, split_heads(values, width), preferred_element_type=jnp.float32
    )
    return (mixture.reshape(queries.shape).astype(low), row_max + jnp.log(row_sum))


def attend_backward(queries, keys, values, key_mask, log_total, mixture_gradient, width):
    factor = float(width) ** (-0.5)
    query_heads = split_heads(queries, width)
    key_heads = split_heads(keys, width)
    value_heads = split_heads(values, width)
    incoming_heads = split_heads(mixture_gradient, width)
    raw_scores = (
        jnp.einsum("qhc,khc->hqk", query_heads, key_heads, preferred_element_type=jnp.float32)
        * factor
    )
    weights = jnp.where(key_mask[None], jnp.exp(raw_scores - log_total), 0.0)
    value_gradient = jnp.einsum(
        "hqk,qhc->khc", weights.astype(low), incoming_heads, preferred_element_type=jnp.float32
    )
    weight_gradient = jnp.einsum(
        "qhc,khc->hqk", incoming_heads, value_heads, preferred_element_type=jnp.float32
    )
    inner_sum = jnp.sum(weights * weight_gradient, -1, keepdims=True)
    score_gradient = (weights * (weight_gradient - inner_sum)).astype(low)
    query_gradient = (
        jnp.einsum("hqk,khc->qhc", score_gradient, key_heads, preferred_element_type=jnp.float32)
        * factor
    )
    key_gradient = (
        jnp.einsum("hqk,qhc->khc", score_gradient, query_heads, preferred_element_type=jnp.float32)
        * factor
    )
    return (
        query_gradient.reshape(queries.shape),
        key_gradient.reshape(keys.shape),
        value_gradient.reshape(values.shape),
    )


def norm_backward(inputs, gain_vec, offset, incoming, normed_gradient):
    input_gradient, gain_gradient, offset_gradient = jax.vjp(layer_norm, inputs, gain_vec, offset)[
        1
    ](normed_gradient)
    return incoming + input_gradient, gain_gradient, offset_gradient


def per_device(
    source_tokens,
    target_tokens,
    source_lengths,
    target_lengths,
    projections,
    combiners,
    expanders,
    reducers,
    norm_gains,
    norm_shifts,
    attention_biases,
    expander_biases,
    reducer_biases,
    source_cotangent,
    target_cotangent,
):
    source_tokens, target_tokens = source_tokens[0], target_tokens[0]
    source_cotangent, target_cotangent = source_cotangent[0], target_cotangent[0]
    count, shards = lax.axis_size("seq"), lax.axis_size("batch")
    me = lax.axis_index("seq")
    local_count, model_width = source_tokens.shape
    head_width = model_width // HEADS
    share = model_width // count
    padding_segment = source_lengths.shape[1] - 1

    here = jnp.arange(local_count, dtype=jnp.int32)
    places = jnp.concatenate([(me ^ offset) * local_count + here for offset in seq_offsets()])

    def segments(lengths):
        ends = jnp.cumsum(lengths[0], dtype=jnp.int32)
        return jnp.sum((places[:, None] >= ends[None, :]).astype(jnp.int32), -1, dtype=jnp.int32)

    source_segment, target_segment = segments(source_lengths), segments(target_lengths)
    encoder_mask = source_segment[:, None] == source_segment[None, :]
    self_mask = (target_segment[:, None] == target_segment[None, :]) & (
        places[:, None] >= places[None, :]
    )
    cross_mask = target_segment[:, None] == source_segment[None, :]
    source_keep = (source_segment[:local_count] < padding_segment).astype(jnp.float32)[:, None]
    target_keep = (target_segment[:local_count] < padding_segment).astype(jnp.float32)[:, None]

    split_biases = attention_biases.reshape(3, 3, count, share)
    entry_biases = lax.dynamic_index_in_dim(split_biases, me, 2, keepdims=False)
    hidden_biases = mine(expander_biases.reshape(2, shards, count, -1), 2).reshape(2, -1)

    dealt = deal_combiners(combiners) if deals_by_line() else [None] * 3

    source_all = spread(source_tokens)
    target_all = spread(target_tokens)
    target_incoming = target_cotangent.astype(jnp.float32) * target_keep
    target_incoming_all = spread(target_incoming.astype(low))

    source_in = source_tokens.astype(jnp.float32)
    target_in = target_tokens.astype(jnp.float32)

    def attention_weights(block):
        return fetch_attention(projections[block], combiners[block], dealt[block])

    def feedforward_weights(block):
        return fetch_feedforward(expanders[block], reducers[block])

    def attention_exit(inputs, mixture, leave, block):
        return inputs + collect(times(mixture, leave).astype(low)) + attention_biases[block, 2]

    def self_forward(inputs, inputs_all, key_mask, norm, block, weights):
        entry, leave = weights
        normed = layer_norm(
            inputs_all.astype(jnp.float32), norm_gains[norm], norm_shifts[norm]
        ).astype(low)
        projected = times(normed, entry)
        queries = (projected[:, :share] + entry_biases[block, 0]).astype(low)
        keys = projected[:, share : 2 * share].astype(low)
        values = (projected[:, 2 * share :] + entry_biases[block, 1]).astype(low)
        mixture, log_total = attend_forward(queries, keys, values, key_mask, head_width)
        result = attention_exit(inputs, mixture, leave, block)
        return result, (normed, queries, keys, values, log_total, mixture)

    def feedforward_forward(inputs, norm, block, weights):
        entry, leave = weights
        normed = spread(layer_norm(inputs, norm_gains[norm], norm_shifts[norm]).astype(low))
        hidden = times(normed, entry) + hidden_biases[block]
        active = gelu_exact(hidden).astype(low)
        result = inputs + collect(times(active, leave).astype(low)) + reducer_biases[block]
        return result, (normed, hidden, active)

    encoder_weights = attention_weights(0)
    middle, encoder_stored = self_forward(
        source_in, source_all, encoder_mask, 0, 0, encoder_weights
    )
    encoder_feed = feedforward_weights(0)
    decoder_weights = attention_weights(1)
    self_out, decoder_stored = self_forward(target_in, target_all, self_mask, 2, 1, decoder_weights)
    memory, encoder_feed_stored = feedforward_forward(middle, 1, 0, encoder_feed)
    memory_low = memory.astype(low)
    memory_all = spread(memory_low)
    cross_weights = attention_weights(2)
    entry, leave = cross_weights
    cross_normed = spread(layer_norm(self_out, norm_gains[3], norm_shifts[3]).astype(low))
    cross_queries = (times(cross_normed, entry[:, :share]) + entry_biases[2, 0]).astype(low)
    projected = times(memory_all, entry[:, share:])
    cross_keys = projected[:, :share].astype(low)
    cross_values = (projected[:, share:] + entry_biases[2, 1]).astype(low)
    cross_mixture, cross_log_total = attend_forward(
        cross_queries, cross_keys, cross_values, cross_mask, head_width
    )
    cross_out = attention_exit(self_out, cross_mixture, leave, 2)
    decoder_feed = feedforward_weights(1)
    decoded, decoder_feed_stored = feedforward_forward(cross_out, 4, 1, decoder_feed)

    def feedforward_backward(incoming, incoming_all, inputs, norm, weights, stored):
        entry, leave = weights
        normed, hidden, active = stored
        active_gradient = times_back(incoming_all, leave)
        hidden_gradient = jax.vjp(gelu_exact, hidden)[1](active_gradient)[0]
        hidden_low = hidden_gradient.astype(low)
        normed_gradient = collect(times_back(hidden_low, entry).astype(low))
        exit_gradient = outer_sum(active, incoming_all)
        entry_gradient = outer_sum(normed, hidden_low)
        result, gain, shift = norm_backward(
            inputs, norm_gains[norm], norm_shifts[norm], incoming, normed_gradient
        )
        shares = send_feedforward(entry_gradient, exit_gradient)
        return result, shares, (gain, shift), (jnp.sum(hidden_gradient, 0), jnp.sum(incoming, 0))

    def attention_core(incoming, weights, stored, key_mask):
        entry, leave = weights
        queries, keys, values, log_total, mixture = stored
        incoming_all = spread(incoming.astype(low))
        mixture_gradient = times_back(incoming_all, leave).astype(low)
        query_gradient, key_gradient, value_gradient = attend_backward(
            queries, keys, values, key_mask, log_total, mixture_gradient, head_width
        )
        exit_gradient = outer_sum(mixture, incoming_all)
        biases = (jnp.sum(query_gradient, 0), jnp.sum(value_gradient, 0), jnp.sum(incoming, 0))
        gradients = (query_gradient.astype(low), key_gradient.astype(low), value_gradient.astype(low))
        return gradients, exit_gradient, biases

    def self_backward(incoming, inputs, key_mask, norm, weights, stored):
        gradients, exit_gradient, biases = attention_core(incoming, weights, stored[1:], key_mask)
        joined = jnp.concatenate(gradients, -1)
        normed_gradient = collect(times_back(joined, weights[0]).astype(low))
        entry_gradient = outer_sum(stored[0], joined)
        result, gain, shift = norm_backward(
            inputs, norm_gains[norm], norm_shifts[norm], incoming, normed_gradient
        )
        return result, send_attention(entry_gradient, exit_gradient), (gain, shift), biases

    incoming, decoder_feed_shares, norm_four, decoder_feed_bias = feedforward_backward(
        target_incoming, target_incoming_all, cross_out, 4, decoder_feed, decoder_feed_stored
    )
    gradients, exit_gradient, cross_bias = attention_core(
        incoming,
        cross_weights,
        (cross_queries, cross_keys, cross_values, cross_log_total, cross_mixture),
        cross_mask,
    )
    pair = jnp.concatenate(gradients[1:], -1)
    entry = cross_weights[0]
    memory_gradient = collect(times_back(pair, entry[:, share:]).astype(low))
    normed_gradient = collect(times_back(gradients[0], entry[:, :share]).astype(low))
    entry_gradient = jnp.concatenate(
        [outer_sum(cross_normed, gradients[0]), outer_sum(memory_all, pair)], 1
    )
    cross_shares = send_attention(entry_gradient, exit_gradient)
    source_incoming = source_cotangent.astype(jnp.float32) * source_keep + memory_gradient
    incoming, *norm_three = norm_backward(
        self_out, norm_gains[3], norm_shifts[3], incoming, normed_gradient
    )
    middle_incoming, encoder_feed_shares, norm_one, encoder_feed_bias = feedforward_backward(
        source_incoming, spread(source_incoming.astype(low)), middle, 1, encoder_feed, encoder_feed_stored
    )
    target_gradient, decoder_shares, norm_two, decoder_bias = self_backward(
        incoming, target_in, self_mask, 2, decoder_weights, decoder_stored
    )
    source_gradient, encoder_shares, norm_zero, encoder_bias = self_backward(
        middle_incoming, source_in, encoder_mask, 0, encoder_weights, encoder_stored
    )

    weight_gradients = finish_weights(
        (encoder_shares, decoder_shares, cross_shares), (encoder_feed_shares, decoder_feed_shares)
    )

    norms = (norm_zero, norm_one, norm_two, norm_three, norm_four)
    gains = jnp.stack([pair[0] for pair in norms])
    shifts = jnp.stack([pair[1] for pair in norms])
    blocks = (encoder_bias, decoder_bias, cross_bias)
    inner = jnp.stack([jnp.stack(bias[:2]) for bias in blocks])
    inner_whole = lax.dynamic_update_slice(
        jnp.zeros((3, 2, count, share), jnp.float32), inner[:, :, None], (0, 0, me, 0)
    ).reshape(3, 2, model_width)
    outer = jnp.stack([bias[2] for bias in blocks])
    hidden = jnp.stack([encoder_feed_bias[0], decoder_feed_bias[0]]).reshape(2, shards, 1, -1)
    hidden_whole = lax.dynamic_update_slice(
        jnp.zeros((2, shards, count, hidden.shape[3]), jnp.float32), hidden, (0, 0, me, 0)
    )
    exits = jnp.stack([encoder_feed_bias[1], decoder_feed_bias[1]])
    parts = [gains, shifts, inner_whole, outer, hidden_whole, exits]
    summed = sum_everywhere(jnp.concatenate([part.reshape(-1, 128) for part in parts], 0))
    rows = [part.size // 128 for part in parts]
    starts = [sum(rows[:i]) for i in range(len(rows))]
    gains, shifts, inner_whole, outer, hidden_whole, exits = [
        summed[start : start + size].reshape(part.shape)
        for start, size, part in zip(starts, rows, parts)
    ]
    return (
        memory_low[None],
        decoded.astype(low)[None],
        source_gradient[None],
        target_gradient[None],
        *weight_gradients,
        gains,
        shifts,
        jnp.concatenate([inner_whole, outer[:, None]], 1),
        hidden_whole.reshape(2, -1),
        exits,
    )


def solution(mesh):
    in_specs = (
        P("batch", "seq", None),
        P("batch", "seq", None),
        P("batch", None),
        P("batch", None),
        P(None, "batch", None),
        P(None, "batch", None),
        P(None, "batch", None),
        P(None, "batch", None),
        P(),
        P(),
        P(),
        P(),
        P(),
        P("batch", "seq", None),
        P("batch", "seq", None),
    )
    out_specs = (
        P("batch", "seq", None),
        P("batch", "seq", None),
        P("batch", "seq", None),
        P("batch", "seq", None),
        P(None, "batch", None),
        P(None, "batch", None),
        P(None, "batch", None),
        P(None, "batch", None),
        P(),
        P(),
        P(),
        P(),
        P(),
    )
    return jax.shard_map(
        per_device, mesh=mesh, in_specs=in_specs, out_specs=out_specs, check_vma=False
    )
```

```python
import jax
import jax.numpy as jnp
from jax import lax
from jax.experimental import pallas as pl
from jax.experimental.pallas import tpu as pltpu
from jax.sharding import PartitionSpec as P

HEADS = 16


epsilon = 1e-05
masked_score = -1e30
low = jnp.bfloat16
high = jnp.float32
shape = jax.ShapeDtypeStruct
VMEM = pl.BlockSpec(memory_space=pltpu.VMEM)
SMEM = pl.BlockSpec(memory_space=pltpu.SMEM)
across_rows = (((0,), (0,)), ((), ()))
across_lanes = (((1,), (1,)), ((), ()))


def run(kernel, outs, args, name, flops, scratch=(), scalars=0, room=24):
    moved = sum(a.size * a.dtype.itemsize for a in args) + sum(
        o.size * jnp.dtype(o.dtype).itemsize for o in outs
    )
    return pl.pallas_call(
        kernel,
        out_shape=list(outs),
        in_specs=[SMEM] * scalars + [VMEM] * (len(args) - scalars),
        out_specs=[VMEM] * len(outs),
        scratch_shapes=list(scratch),
        compiler_params=pltpu.CompilerParams(vmem_limit_bytes=room << 20),
        cost_estimate=pl.CostEstimate(
            flops=int(flops), bytes_accessed=int(moved), transcendentals=0
        ),
        name=name,
    )(*args)


def normalize(values, gain, shift):
    middle = jnp.mean(values, -1, keepdims=True)
    centred = values - middle
    width = jnp.mean(centred * centred, -1, keepdims=True)
    return centred * lax.rsqrt(width + epsilon) * gain + shift


def matmul(left, right):
    return jnp.dot(left, right, preferred_element_type=high)


def matmul_back(left, right):
    return lax.dot_general(left, right, across_lanes, preferred_element_type=high)


def matmul_outer(left, right):
    return lax.dot_general(left, right, across_rows, preferred_element_type=high)


def piece_rows(pieces):
    start = 0
    for piece in pieces:
        yield pl.ds(start, piece.shape[0]), piece
        start += piece.shape[0]


def assemble(pieces, table, parts):
    def kernel(table_ref, *refs):
        sources, outs = refs[: len(pieces)], refs[len(pieces) :]
        for which, (start, rows, _) in enumerate(parts):
            for i, source in enumerate(sources):
                at = pl.multiple_of(table_ref[which, i], rows)
                outs[which][pl.ds(at, rows), :] = source[start : start + rows, :]

    width = pieces[0].shape[1]
    outs = [shape((whole, width), low) for _, _, whole in parts]
    return run(kernel, outs, [table, *pieces], "assemble", 1, scalars=1)


def project_self(pieces, gain, shift, entry, biases):
    count, width = len(pieces), entry.shape[1] // 3

    def kernel(*refs):
        sources = refs[:count]
        gain_ref, shift_ref, entry_ref, bias_ref, normed_ref, query_ref, key_ref, value_ref = refs[
            count:
        ]
        for rows, source in piece_rows(sources):
            normed = normalize(source[...].astype(high), gain_ref[...], shift_ref[...])
            normed_ref[rows, :] = normed.astype(low)
            joined = matmul(normed_ref[rows, :], entry_ref[...])
            query_ref[rows, :] = (joined[:, :width] + bias_ref[0:1, :]).astype(low)
            key_ref[rows, :] = joined[:, width : 2 * width].astype(low)
            value_ref[rows, :] = (joined[:, 2 * width :] + bias_ref[1:2, :]).astype(low)

    rows = sum(piece.shape[0] for piece in pieces)
    outs = [shape((rows, pieces[0].shape[1]), low)] + [shape((rows, width), low)] * 3
    flops = 2 * rows * entry.shape[0] * entry.shape[1]
    return run(kernel, outs, [*pieces, gain, shift, entry, biases], "project_self", flops)


def project_cross(pieces, memory_pieces, entry, biases):
    count, width = len(pieces), entry.shape[1] // 3

    def kernel(*refs):
        sources, memories = refs[:count], refs[count : 2 * count]
        entry_ref, bias_ref, query_ref, key_ref, value_ref = refs[2 * count :]
        for rows, source in piece_rows(sources):
            joined = matmul(source[...], entry_ref[:, :width])
            query_ref[rows, :] = (joined + bias_ref[0:1, :]).astype(low)
        for rows, source in piece_rows(memories):
            joined = matmul(source[...], entry_ref[:, width:])
            key_ref[rows, :] = joined[:, :width].astype(low)
            value_ref[rows, :] = (joined[:, width:] + bias_ref[1:2, :]).astype(low)

    rows = sum(piece.shape[0] for piece in pieces)
    outs = [shape((rows, width), low)] * 3
    flops = 2 * rows * entry.shape[0] * entry.shape[1]
    return run(kernel, outs, [*pieces, *memory_pieces, entry, biases], "project_cross", flops)


def head_lanes(values, head, width):
    lanes = lax.broadcasted_iota(jnp.int32, values.shape, 1)
    inside = (lanes >= head * width) & (lanes < (head + 1) * width)
    return jnp.where(inside, values, jnp.zeros_like(values))


def block_bias(keys, cols, causal, key_segment, query_segment, key_place, query_place):
    allowed = key_segment[keys, :] == query_segment[:, cols]
    if causal:
        allowed = allowed & (key_place[keys, :] <= query_place[:, cols])
    return jnp.where(allowed, 0.0, masked_score)


def attend_forward(marks, tags, queries, keys, values, leave, heads, causal, count):
    rows, width = queries.shape
    head_width = width // heads
    block = min(256, rows)
    blocks = rows // block
    local = rows // count
    scale = head_width**-0.5
    tall = max(8, heads)

    def kernel(*refs):
        marks_ref, key_segment, query_segment, key_place, query_place = refs[:5]
        query_ref, key_ref, value_ref, leave_ref, mixture_ref, total_ref = refs[5:11]
        partial_refs = refs[11 : 11 + count]
        score_ref, top_ref, sum_ref, mix_ref, value_turned = refs[11 + count :]
        value_turned[...] = value_ref[...].astype(high).T.astype(low)
        total_ref[...] = jnp.zeros(total_ref.shape, high)
        for i in range(blocks):
            mine = pl.ds(i * block, block)
            cols = slice(i * block, (i + 1) * block)
            query = query_ref[mine, :] * low(scale)
            query_heads = [head_lanes(query, head, head_width) for head in range(heads)]
            top_ref[...] = jnp.full(top_ref.shape, masked_score, high)
            sum_ref[...] = jnp.zeros(sum_ref.shape, high)
            mix_ref[...] = jnp.zeros(mix_ref.shape, high)

            def score(j, carry, i=i, cols=cols, query_heads=query_heads):
                @pl.when(marks_ref[i, j] != 0)
                def _():
                    there = pl.ds(pl.multiple_of(j * block, block), block)
                    bias = block_bias(
                        there, cols, causal, key_segment, query_segment, key_place, query_place
                    )
                    for head in range(heads):
                        scores = matmul_back(key_ref[there, :], query_heads[head]) + bias
                        score_ref[head, there, :] = scores
                        row = slice(head, head + 1)
                        top_ref[row, :] = jnp.maximum(
                            top_ref[row, :], jnp.max(scores, 0, keepdims=True)
                        )

                return carry

            lax.fori_loop(0, blocks, score, 0)

            def mix(j, carry, i=i):
                @pl.when(marks_ref[i, j] != 0)
                def _():
                    there = pl.ds(pl.multiple_of(j * block, block), block)
                    for head in range(heads):
                        row = slice(head, head + 1)
                        features = slice(head * head_width, (head + 1) * head_width)
                        weights = jnp.exp(score_ref[head, there, :] - top_ref[row, :])
                        sum_ref[row, :] += jnp.sum(weights, 0, keepdims=True)
                        mix_ref[features, :] += matmul(
                            value_turned[features, there], weights.astype(low)
                        )

                return carry

            lax.fori_loop(0, blocks, mix, 0)
            for head in range(heads):
                row = slice(head, head + 1)
                features = slice(head * head_width, (head + 1) * head_width)
                mix_ref[features, :] = mix_ref[features, :] * (1.0 / sum_ref[row, :])
                total_ref[row, cols] = top_ref[row, :] + jnp.log(sum_ref[row, :])
            mixture_ref[mine, :] = mix_ref[...].T.astype(low)
        for i in range(count):
            mine = pl.ds(i * local, local)
            partial_refs[i][...] = matmul(mixture_ref[mine, :], leave_ref[...]).astype(low)

    outs = [shape((rows, width), low), shape((tall, rows), high)]
    outs += [shape((local, leave.shape[1]), low)] * count
    scratch = [
        pltpu.VMEM((heads, rows, block), high),
        pltpu.VMEM((tall, block), high),
        pltpu.VMEM((tall, block), high),
        pltpu.VMEM((width, block), high),
        pltpu.VMEM((width, rows), low),
    ]
    flops = 8 * rows * rows * width + 2 * rows * width * leave.shape[1]
    args = [marks, *tags, queries, keys, values, leave]
    mixture, total, *partials = run(
        kernel, outs, args, "attend_forward", flops, scratch, scalars=1
    )
    return mixture, total, partials


def attend_backward(marks, tags, pieces, leave, entry, stored, heads, causal, cross):
    queries, keys, values, mixture, total = stored
    count = len(pieces)
    rows, width = queries.shape
    head_width = width // heads
    block = min(256, rows)
    blocks = rows // block
    local = rows // count
    scale = head_width**-0.5

    def kernel(*refs):
        marks_ref, key_segment, query_segment, key_place, query_place = refs[:5]
        incoming_refs = refs[5 : 5 + count]
        leave_ref, entry_ref, query_ref, key_ref, value_ref, mixture_ref, total_ref = refs[
            5 + count : 12 + count
        ]
        joined_ref, sums_ref, exit_ref = refs[12 + count : 15 + count]
        partial_refs = refs[15 + count : 15 + 2 * count]
        memory_refs = refs[15 + 2 * count : -5]
        incoming_mix, key_sum, value_sum, query_turned, key_turned = refs[-5:]
        exit_sum = None
        for where, piece in piece_rows(incoming_refs):
            incoming_mix[where, :] = matmul_back(piece[...], leave_ref[...]).astype(low)
            term = matmul_outer(mixture_ref[where, :], piece[...])
            exit_sum = term if exit_sum is None else exit_sum + term
        exit_ref[...] = exit_sum.astype(low)
        key_turned[...] = key_ref[...].astype(high).T.astype(low)
        key_sum[...] = jnp.zeros(key_sum.shape, high)
        value_sum[...] = jnp.zeros(value_sum.shape, high)
        query_total = jnp.zeros((1, width), high)
        for i in range(blocks):
            mine = pl.ds(i * block, block)
            cols = slice(i * block, (i + 1) * block)
            query = query_ref[mine, :] * low(scale)
            arriving = incoming_mix[mine, :]
            query_heads = [head_lanes(query, head, head_width) for head in range(heads)]
            arriving_heads = [head_lanes(arriving, head, head_width) for head in range(heads)]
            products = (arriving.astype(high) * mixture_ref[mine, :].astype(high)).T
            inner = [
                jnp.sum(products[head * head_width : (head + 1) * head_width, :], 0, keepdims=True)
                for head in range(heads)
            ]
            query_turned[...] = jnp.zeros(query_turned.shape, high)

            def step(j, carry, i=i, cols=cols, qh=query_heads, ah=arriving_heads, inner=inner):
                @pl.when(marks_ref[i, j] != 0)
                def _():
                    there = pl.ds(pl.multiple_of(j * block, block), block)
                    bias = block_bias(
                        there, cols, causal, key_segment, query_segment, key_place, query_place
                    )
                    key_acc, value_acc = key_sum[there, :], value_sum[there, :]
                    for head in range(heads):
                        features = slice(head * head_width, (head + 1) * head_width)
                        scores = matmul_back(key_ref[there, :], qh[head])
                        weights = jnp.exp(scores - total_ref[head : head + 1, cols] + bias)
                        back = matmul_back(value_ref[there, :], ah[head])
                        change = (weights * (back - inner[head])).astype(low)
                        value_acc = value_acc + matmul(weights.astype(low), ah[head])
                        key_acc = key_acc + matmul(change, qh[head])
                        query_turned[features, :] += matmul(key_turned[features, there], change)
                    key_sum[there, :] = key_acc
                    value_sum[there, :] = value_acc

                return carry

            lax.fori_loop(0, blocks, step, 0)
            query_gradient = query_turned[...].T * scale
            query_total = query_total + jnp.sum(query_gradient, 0, keepdims=True)
            joined_ref[mine, :width] = query_gradient.astype(low)
        joined_ref[:, width : 2 * width] = key_sum[...].astype(low)
        joined_ref[:, 2 * width :] = value_sum[...].astype(low)
        sums_ref[0:1, :] = query_total
        sums_ref[1:2, :] = jnp.sum(value_sum[...], 0, keepdims=True)
        for i in range(count):
            mine = pl.ds(i * local, local)
            if cross:
                query_part = matmul_back(joined_ref[mine, :width], entry_ref[:, :width])
                memory_part = matmul_back(joined_ref[mine, width:], entry_ref[:, width:])
                partial_refs[i][...] = query_part.astype(low)
                memory_refs[i][...] = memory_part.astype(low)
            else:
                partial_refs[i][...] = matmul_back(joined_ref[mine, :], entry_ref[...]).astype(low)

    outs = [shape((rows, 3 * width), low), shape((2, width), high), shape(leave.shape, low)]
    outs += [shape((local, entry.shape[0]), low)] * (count * (2 if cross else 1))
    scratch = [
        pltpu.VMEM((rows, width), low),
        pltpu.VMEM((rows, width), high),
        pltpu.VMEM((rows, width), high),
        pltpu.VMEM((width, block), high),
        pltpu.VMEM((width, rows), low),
    ]
    flops = 20 * rows * rows * width + 10 * rows * width * entry.shape[0]
    args = [marks, *tags, *pieces, leave, entry, queries, keys, values, mixture, total]
    joined, sums, exit_gradient, *partials = run(
        kernel, outs, args, "attend_backward", flops, scratch, scalars=1, room=28
    )
    return joined, sums, exit_gradient, partials[:count], partials[count:]


def feed_forward(pieces, entry, leave, bias):
    count, hidden_width = len(pieces), entry.shape[1]
    step = min(512, hidden_width)

    def kernel(*refs):
        sources = refs[:count]
        entry_ref, leave_ref, bias_ref, active_ref, slope_ref = refs[count : count + 5]
        partial_refs = refs[count + 5 :]
        for (rows, source), partial in zip(piece_rows(sources), partial_refs):
            for start in range(0, hidden_width, step):
                cols = slice(start, start + step)
                hidden = matmul(source[...], entry_ref[:, cols]) + bias_ref[:, cols]
                share = 0.5 * (1.0 + lax.erf(hidden * 0.7071067811865476))
                density = jnp.exp(-0.5 * hidden * hidden) * 0.3989422804014327
                active_ref[rows, cols] = (hidden * share).astype(low)
                slope_ref[rows, cols] = (share + hidden * density).astype(low)
            partial[...] = matmul(active_ref[rows, :], leave_ref[...]).astype(low)

    rows = sum(piece.shape[0] for piece in pieces)
    outs = [shape((rows, hidden_width), low)] * 2
    outs += [shape((piece.shape[0], leave.shape[1]), low) for piece in pieces]
    flops = 4 * rows * entry.shape[0] * hidden_width
    args = [*pieces, entry, leave, bias]
    active, slope, *partials = run(kernel, outs, args, "feed_forward", flops)
    return active, slope, partials


def feed_backward(pieces, entry, leave, slope):
    count, hidden_width = len(pieces), entry.shape[1]

    def kernel(*refs):
        sources = refs[:count]
        entry_ref, leave_ref, slope_ref, hidden_ref, sum_ref = refs[count : count + 5]
        partial_refs = refs[count + 5 :]
        total = jnp.zeros(sum_ref.shape, high)
        for (rows, source), partial in zip(piece_rows(sources), partial_refs):
            hidden = matmul_back(source[...], leave_ref[...]) * slope_ref[rows, :].astype(high)
            total = total + jnp.sum(hidden, 0, keepdims=True)
            hidden_ref[rows, :] = hidden.astype(low)
            partial[...] = matmul_back(hidden_ref[rows, :], entry_ref[...]).astype(low)
        sum_ref[...] = total

    rows = sum(piece.shape[0] for piece in pieces)
    outs = [shape((rows, hidden_width), low), shape((1, hidden_width), high)]
    outs += [shape((piece.shape[0], entry.shape[0]), low) for piece in pieces]
    flops = 4 * rows * entry.shape[0] * hidden_width
    args = [*pieces, entry, leave, slope]
    hidden, total, *partials = run(kernel, outs, args, "feed_backward", flops)
    return hidden, total, partials


def blocks_out(shards, height, width):
    quarter = shards // 4
    return [
        shape((2 * quarter, height, width), low),
        shape((quarter, height, width), low),
        shape((quarter, height, width), low),
    ]


def block_targets(refs):
    return [(ref, at) for ref in refs for at in range(ref.shape[0])]


def outer_sums(pairs, order, name, stacked=False):
    flat, counts, flops = [], [], 0
    for lefts, rights, start, lanes in pairs:
        flat += [*lefts, *rights]
        counts.append((len(lefts), len(rights), start, lanes))
        flops += 2 * sum(left.size for left in lefts) * lanes
    sizes = [(pair[0][0].shape[1], pair[3]) for pair in pairs]

    def compute(refs, outs):
        for (left_count, right_count, start, lanes), out in zip(counts, outs):
            lefts, rights = refs[:left_count], refs[left_count : left_count + right_count]
            refs = refs[left_count + right_count :]
            terms = max(left_count, right_count)
            rows = sum(left.shape[0] for left in lefts) // terms
            step = min(256, out.shape[0])
            side = slice(start, start + lanes)
            for first in range(0, out.shape[0], step):
                cols = slice(first, first + step)
                total = None
                for i in range(terms):
                    where = pl.ds(i * rows, rows)
                    left = lefts[i][:, cols] if left_count == terms else lefts[0][where, cols]
                    right = rights[i][:, side] if right_count == terms else rights[0][where, side]
                    term = matmul_outer(left, right)
                    total = term if total is None else total + term
                out[cols, :] = total.astype(low)

    if order is None:

        def plain(*refs):
            compute(refs[: len(flat)], refs[len(flat) :])

        return run(plain, [shape(size, low) for size in sizes], flat, name, flops)

    shards = order.shape[0]
    heights = [size[0] // shards for size in sizes]
    if stacked:
        corners = [(sum(heights[:i]), 0) for i in range(len(sizes))]
        outs = blocks_out(shards, sum(heights), sizes[0][1])
    else:
        corners = [(0, sum(size[1] for size in sizes[:i])) for i in range(len(sizes))]
        outs = blocks_out(shards, heights[0], sum(size[1] for size in sizes))

    def kernel(order_ref, *refs):
        inputs, rest = refs[: len(flat)], refs[len(flat) :]
        compute(inputs, rest[3:])
        for i, (target, at) in enumerate(block_targets(rest[:3])):
            for source, rows, (top, side) in zip(rest[3:], heights, corners):
                where = pl.ds(pl.multiple_of(order_ref[i] * rows, rows), rows)
                target[at, top : top + rows, side : side + source.shape[1]] = source[where, :]

    scratch = [pltpu.VMEM(size, low) for size in sizes]
    return run(kernel, outs, [order, *flat], name, flops, scratch, scalars=1)


def order_combiners(exits, table):
    shards = table.shape[0]
    rows = exits[0].shape[0] // shards

    def kernel(table_ref, *refs):
        sources = refs[: len(exits)]
        for i, (target, at) in enumerate(block_targets(refs[len(exits) :])):
            where = pl.ds(pl.multiple_of(table_ref[i], rows), rows)
            for block, source in enumerate(sources):
                target[at, block * rows : (block + 1) * rows, :] = source[where, :]

    outs = blocks_out(shards, rows * len(exits), exits[0].shape[1])
    return run(kernel, outs, [table, *exits], "order_combiners", 1, scalars=1)


def add_up(refs):
    total = refs[0][...].astype(high)
    for ref in refs[1:]:
        total = total + ref[...].astype(high)
    return total


def residual_norm(base, addends, bias, gain, shift):
    count = 1 + len(addends)

    def kernel(*refs):
        bias_ref, gain_ref, shift_ref, total_ref, normed_ref = refs[count:]
        total = add_up(refs[:count]) + bias_ref[...]
        total_ref[...] = total
        normed_ref[...] = normalize(total, gain_ref[...], shift_ref[...]).astype(low)

    outs = [shape(base.shape, high), shape(base.shape, low)]
    return run(kernel, outs, [base, *addends, bias, gain, shift], "residual_norm", base.size * 12)


def residual_low(base, addends, bias):
    count = 1 + len(addends)

    def kernel(*refs):
        bias_ref, total_ref = refs[count:]
        total_ref[...] = (add_up(refs[:count]) + bias_ref[...]).astype(low)

    outs = [shape(base.shape, low)]
    return run(kernel, outs, [base, *addends, bias], "residual_low", base.size * 4)[0]


def join_gradient(cotangent, keep, addends):
    count = len(addends)

    def kernel(*refs):
        cotangent_ref, keep_ref = refs[:2]
        gradient_ref, low_ref, sum_ref = refs[2 + count :]
        total = cotangent_ref[...].astype(high) * keep_ref[...]
        for ref in refs[2 : 2 + count]:
            total = total + ref[...].astype(high)
        gradient_ref[...] = total
        low_ref[...] = total.astype(low)
        sum_ref[...] = jnp.sum(total, 0, keepdims=True)

    outs = [
        shape(cotangent.shape, high),
        shape(cotangent.shape, low),
        shape((1, cotangent.shape[1]), high),
    ]
    return run(kernel, outs, [cotangent, keep, *addends], "join_gradient", cotangent.size * 4)


def norm_backward(inputs, gain, incoming, addends):
    count = len(addends)

    def kernel(*refs):
        input_ref, gain_ref, incoming_ref = refs[:3]
        result_ref, low_ref, sums_ref = refs[3 + count :]
        gradient = add_up(refs[3 : 3 + count])
        values = input_ref[...].astype(high)
        centred = values - jnp.mean(values, -1, keepdims=True)
        inverse = lax.rsqrt(jnp.mean(centred * centred, -1, keepdims=True) + epsilon)
        unit = centred * inverse
        sums_ref[0:1, :] = jnp.sum(gradient * unit, 0, keepdims=True)
        sums_ref[1:2, :] = jnp.sum(gradient, 0, keepdims=True)
        scaled = gradient * gain_ref[...]
        inner = jnp.mean(scaled * unit, -1, keepdims=True)
        change = (scaled - jnp.mean(scaled, -1, keepdims=True) - unit * inner) * inverse
        result = incoming_ref[...] + change
        result_ref[...] = result
        low_ref[...] = result.astype(low)
        sums_ref[2:3, :] = jnp.sum(result, 0, keepdims=True)

    outs = [
        shape(inputs.shape, high),
        shape(inputs.shape, low),
        shape((3, inputs.shape[1]), high),
    ]
    args = [inputs, gain, incoming, *addends]
    return run(kernel, outs, args, "norm_backward", inputs.size * 20)


def seq_bits():
    bit, bits = lax.axis_size("seq") >> 1, []
    while bit:
        bits.append(bit)
        bit >>= 1
    return bits


def seq_offsets():
    offsets = [0]
    for bit in seq_bits():
        offsets = offsets + [offset ^ bit for offset in offsets]
    return offsets


def swap(values, bit, axis="seq"):
    return lax.ppermute(values, axis, [(i, i ^ bit) for i in range(lax.axis_size(axis))])


def spread(piece):
    pieces = [piece]
    for bit in seq_bits():
        pieces = pieces + [swap(piece, bit) for piece in pieces]
    return pieces


def sum_low(addends):
    total = addends[0].astype(high)
    for addend in addends[1:]:
        total = total + addend.astype(high)
    return total.astype(low)


def collect(partials):
    kept = [[partial] for partial in partials]
    for bit in reversed(seq_bits()):
        half = len(kept) // 2
        sent = kept[half:]
        arrived = [None] * half
        for i in reversed(range(half)):
            value = sent[i][0] if len(sent[i]) == 1 else sum_low(sent[i])
            arrived[i] = swap(value, bit)
        kept = [own + [other] for own, other in zip(kept[:half], arrived)]
    return kept[0]


def sum_everywhere(values):
    for axis in ("seq", "batch"):
        bit = 1
        while bit < lax.axis_size(axis):
            values = values + swap(values, bit, axis)
            bit <<= 1
    return values


def mine(values, axis):
    return lax.dynamic_index_in_dim(values, lax.axis_index("seq"), axis, keepdims=False)


def in_line():
    return lax.axis_size("batch") == 2 * lax.axis_size("seq")


def line_place():
    return lax.axis_index("batch") // 2, lax.axis_index("batch") % 2


def line_shift(values):
    shards = lax.axis_size("batch")
    return lax.ppermute(values, "batch", [(i, (i + 2) % shards) for i in range(shards)])


def line_order(first):
    length = lax.axis_size("batch") // 2
    place, side = line_place()
    at = (place - first - jnp.arange(length, dtype=jnp.int32)) % length
    return jnp.concatenate([2 * at + side, 2 * at + 1 - side])


def after(values, earlier):
    return lax.optimization_barrier((values, earlier))[0]


def gather_line(values):
    line, across = [values], [swap(values, 1, "batch")]
    for _ in range(1, lax.axis_size("batch") // 2):
        line.append(line_shift(line[-1]))
        across.append(swap(line[-1], 1, "batch"))
    return line + across


def scatter_line(keep, near, far):
    across = [swap(near, 1, "batch"), swap(far, 1, "batch")]
    half = near.shape[0]
    total = None
    for step in range(keep.shape[0]):
        addends = [keep[step], across[step // half][step % half]]
        if total is not None:
            addends = [line_shift(total)] + addends
        total = sum_low(addends)
    return total


def line_pairs(step, count, back):
    pairs = []
    for place in range(count):
        for side in range(2):
            here = (place * 2 + side) * count + place
            there = (((place + step) % count) * 2 + side) * count + place
            pairs.append((there, here) if back else (here, there))
    return pairs


def deal_combiners(combiners):
    count = lax.axis_size("seq")
    me = lax.axis_index("seq")
    place, _ = line_place()
    rows = combiners.shape[1] // count
    parts = combiners.reshape(combiners.shape[0], count, rows, combiners.shape[2])
    own = lax.dynamic_index_in_dim(parts, me, 1, keepdims=False)
    piece = jnp.where(place == me, own, jnp.zeros_like(own))
    for step in range(1, count):
        sent = lax.dynamic_index_in_dim(parts, (me + step) % count, 1, keepdims=False)
        piece = piece + lax.ppermute(sent, ("batch", "seq"), line_pairs(step, count, False))
    return piece.reshape(-1, piece.shape[2])


def return_combiners(pieces, blocks):
    count = lax.axis_size("seq")
    me = lax.axis_index("seq")
    place, _ = line_place()
    arrived = [pieces] + [
        lax.ppermute(pieces, ("batch", "seq"), line_pairs(step, count, True))
        for step in range(1, count)
    ]
    arrived = [piece.reshape(blocks, -1, piece.shape[1]) for piece in arrived]
    ring = jnp.stack(arrived + arrived[:-1], 1)
    ordered = lax.dynamic_slice_in_dim(ring, (count - me) % count, count, 1)
    ordered = ordered.reshape(blocks, -1, pieces.shape[1])
    for bit in seq_bits():
        ordered = jnp.where((place & bit) == (me & bit), ordered, swap(ordered, bit))
    return ordered


def gather_weights(projections, combiners, expanders, reducers):
    count, shards = lax.axis_size("seq"), lax.axis_size("batch")
    blocks, rows, _ = projections.shape
    feeds, _, _ = expanders.shape
    model_width = combiners.shape[2]
    entries = mine(projections.reshape(blocks, rows, 3, count, -1), 3).reshape(blocks, rows, -1)
    expand = mine(expanders.reshape(feeds, rows, shards, count, -1), 3).reshape(feeds, rows, -1)
    reduce = mine(reducers.reshape(feeds, count, -1, model_width), 1)
    if not in_line():

        def whole(values):
            return lax.all_gather(values, "batch", axis=0, tiled=True)

        leaves = [whole(combiners[i]).reshape(count, -1, model_width) for i in range(blocks)]
        return (
            [whole(entries[i]) for i in range(blocks)],
            [mine(leave, 0) for leave in leaves],
            [whole(expand[i]) for i in range(feeds)],
            [whole(reduce[i]) for i in range(feeds)],
        )
    order = line_order(0)
    last = shards // 2 - 1
    piece = model_width // count // shards
    straight = order * rows
    lower = reduce.shape[1]
    first = gather_line(entries[0])
    entry_zero = assemble(first, straight[None], [(0, rows, shards * rows)])
    leaf = gather_line(after(deal_combiners(combiners), first[last]))
    leaves = assemble(
        leaf,
        jnp.stack([((order % 2) * (shards // 2) + order // 2) * piece] * blocks),
        [(i * piece, piece, shards * piece) for i in range(blocks)],
    )

    def feed(which, earlier):
        joined = jnp.concatenate([expand[which], reduce[which]], 0)
        pieces = gather_line(after(joined, earlier))
        both = assemble(
            pieces,
            jnp.stack([straight, order * lower]),
            [(0, rows, shards * rows), (rows, lower, shards * lower)],
        )
        return both, pieces[last]

    feed_zero, done = feed(0, leaf[last])
    rest = gather_line(after(entries[1:].reshape(-1, entries.shape[2]), done))
    entry_rest = assemble(
        rest,
        jnp.stack([straight] * (blocks - 1)),
        [(i * rows, rows, shards * rows) for i in range(blocks - 1)],
    )
    feed_one, _ = feed(1, rest[last])
    return (
        [*entry_zero, *entry_rest],
        leaves,
        [feed_zero[0], feed_one[0]],
        [feed_zero[1], feed_one[1]],
    )


def spread_order(pieces, axis):
    me = lax.axis_index("seq")
    stacked = jnp.stack(pieces)
    offsets = jnp.array([seq_offsets().index(i) for i in range(len(pieces))], jnp.int32)
    ordered = [
        lax.dynamic_index_in_dim(stacked, offsets[me ^ i], 0, keepdims=False)
        for i in range(len(pieces))
    ]
    return jnp.stack(ordered, axis)


def per_device(
    source_tokens,
    target_tokens,
    source_lengths,
    target_lengths,
    projections,
    combiners,
    expanders,
    reducers,
    norm_gains,
    norm_shifts,
    attention_biases,
    expander_biases,
    reducer_biases,
    source_cotangent,
    target_cotangent,
):
    source_tokens, target_tokens = source_tokens[0], target_tokens[0]
    source_cotangent, target_cotangent = source_cotangent[0], target_cotangent[0]
    count, shards = lax.axis_size("seq"), lax.axis_size("batch")
    me = lax.axis_index("seq")
    local_count, model_width = source_tokens.shape
    heads = HEADS // count
    share = model_width // count
    padding_segment = source_lengths.shape[1] - 1

    here = jnp.arange(local_count, dtype=jnp.int32)
    places = jnp.concatenate([(me ^ offset) * local_count + here for offset in seq_offsets()])

    def segments(lengths):
        ends = jnp.cumsum(lengths[0], dtype=jnp.int32)
        return jnp.sum((places[:, None] >= ends[None, :]).astype(jnp.int32), -1, dtype=jnp.int32)

    source_segment, target_segment = segments(source_lengths), segments(target_lengths)
    source_keep = (source_segment[:local_count] < padding_segment).astype(high)[:, None]
    target_keep = (target_segment[:local_count] < padding_segment).astype(high)[:, None]

    def view(query_segment, key_segment, causal):
        def ends_of(values):
            blocks = values.reshape(-1, min(256, values.shape[0]))
            return jnp.min(blocks, 1), jnp.max(blocks, 1)

        query_low, query_high = ends_of(query_segment)
        key_low, key_high = ends_of(key_segment)
        marks = (query_low[:, None] <= key_high[None]) & (key_low[None] <= query_high[:, None])
        if causal:
            place_low, place_high = ends_of(places)
            marks = marks & (place_low[None] <= place_high[:, None])
        tags = (key_segment[:, None], query_segment[None], places[:, None], places[None])
        return marks.astype(jnp.int32), tags

    encoder_view = view(source_segment, source_segment, False)
    self_view = view(target_segment, target_segment, True)
    cross_view = view(target_segment, source_segment, False)

    entry_biases = mine(attention_biases[:, :2].reshape(3, 2, count, share), 2)
    exit_biases = attention_biases[:, 2]
    hidden_biases = mine(expander_biases.reshape(2, shards, count, -1), 2).reshape(2, 1, -1)

    def gain(norm):
        return norm_gains[norm : norm + 1]

    def shift(norm):
        return norm_shifts[norm : norm + 1]

    def exit_bias(block):
        return exit_biases[block : block + 1]

    source_pieces = spread(source_tokens)
    entries, leaves, expand, reduce = gather_weights(projections, combiners, expanders, reducers)
    target_pieces = spread(target_tokens)
    target_incoming, target_incoming_low, target_sum = join_gradient(
        target_cotangent, target_keep, []
    )
    target_incoming_pieces = spread(target_incoming_low)

    def self_forward(pieces, seen, causal, norm, block):
        normed, *projected = project_self(
            pieces, gain(norm), shift(norm), entries[block], entry_biases[block]
        )
        mixture, total, partials = attend_forward(
            *seen, *projected, leaves[block], heads, causal, count
        )
        return normed, (*projected, mixture, total), collect(partials)

    encoder_normed, encoder_stored, addends = self_forward(
        source_pieces, encoder_view, False, 0, 0
    )
    middle, middle_normed = residual_norm(source_tokens, addends, exit_bias(0), gain(1), shift(1))
    middle_pieces = spread(middle_normed)
    decoder_normed, decoder_stored, addends = self_forward(target_pieces, self_view, True, 2, 1)
    self_out, self_normed = residual_norm(target_tokens, addends, exit_bias(1), gain(3), shift(3))
    self_pieces = spread(self_normed)
    encoder_active, encoder_slope, partials = feed_forward(
        middle_pieces, expand[0], reduce[0], hidden_biases[0]
    )
    memory_low = residual_low(middle, collect(partials), reducer_biases[0:1])
    memory_pieces = spread(memory_low)
    cross_projected = project_cross(self_pieces, memory_pieces, entries[2], entry_biases[2])
    mixture, total, partials = attend_forward(
        *cross_view, *cross_projected, leaves[2], heads, False, count
    )
    cross_stored = (*cross_projected, mixture, total)
    cross_out, cross_normed = residual_norm(
        self_out, collect(partials), exit_bias(2), gain(4), shift(4)
    )
    cross_pieces = spread(cross_normed)
    decoder_active, decoder_slope, partials = feed_forward(
        cross_pieces, expand[1], reduce[1], hidden_biases[1]
    )
    decoded_low = residual_low(cross_out, collect(partials), reducer_biases[1:2])

    order = line_order(1) if in_line() else None

    def send(blocks):
        if order is not None:
            return scatter_line(*blocks)
        return [
            lax.psum_scatter(part, "batch", scatter_dimension=0, tiled=True) for part in blocks
        ]

    def feed_gradients(pieces, normed_pieces, hidden, active):
        pairs = [
            (normed_pieces, [hidden], 0, hidden.shape[1]),
            ([active], pieces, 0, model_width),
        ]
        return send(outer_sums(pairs, order, "feed_weights", True))

    def attention_gradients(pairs):
        return send(outer_sums(pairs, order, "attention_weights"))

    hidden, decoder_hidden_sum, partials = feed_backward(
        target_incoming_pieces, expand[1], reduce[1], decoder_slope
    )
    incoming, incoming_low, norm_four = norm_backward(
        cross_out, gain(4), target_incoming, collect(partials)
    )
    incoming_pieces = spread(incoming_low)
    decoder_feed_shares = feed_gradients(
        target_incoming_pieces, cross_pieces, hidden, decoder_active
    )
    cross_joined, cross_sums, cross_exit, partials, memory_partials = attend_backward(
        *cross_view, incoming_pieces, leaves[2], entries[2], cross_stored, heads, False, True
    )
    source_incoming, source_incoming_low, source_sum = join_gradient(
        source_cotangent, source_keep, collect(memory_partials)
    )
    source_incoming_pieces = spread(source_incoming_low)
    self_incoming, self_incoming_low, norm_three = norm_backward(
        self_out, gain(3), incoming, collect(partials)
    )
    self_incoming_pieces = spread(self_incoming_low)
    cross_shares = attention_gradients(
        [
            (self_pieces, [cross_joined], 0, share),
            (memory_pieces, [cross_joined], share, 2 * share),
        ]
    )
    hidden, encoder_hidden_sum, partials = feed_backward(
        source_incoming_pieces, expand[0], reduce[0], encoder_slope
    )
    middle_incoming, middle_incoming_low, norm_one = norm_backward(
        middle, gain(1), source_incoming, collect(partials)
    )
    middle_incoming_pieces = spread(middle_incoming_low)
    decoder_joined, decoder_sums, decoder_exit, partials, _ = attend_backward(
        *self_view, self_incoming_pieces, leaves[1], entries[1], decoder_stored, heads, True, False
    )
    target_gradient, _, norm_two = norm_backward(
        target_tokens, gain(2), self_incoming, collect(partials)
    )
    encoder_feed_shares = feed_gradients(
        source_incoming_pieces, middle_pieces, hidden, encoder_active
    )
    decoder_shares = attention_gradients([([decoder_normed], [decoder_joined], 0, 3 * share)])
    encoder_joined, encoder_sums, encoder_exit, partials, _ = attend_backward(
        *encoder_view,
        middle_incoming_pieces,
        leaves[0],
        entries[0],
        encoder_stored,
        heads,
        False,
        False,
    )
    encoder_shares = attention_gradients([([encoder_normed], [encoder_joined], 0, 3 * share)])
    source_gradient, _, norm_zero = norm_backward(
        source_tokens, gain(0), middle_incoming, collect(partials)
    )

    exits = [encoder_exit, decoder_exit, cross_exit]
    rows = projections.shape[1]
    if order is not None:
        table = ((order % 2) * (shards // 2) + order // 2) * (share // shards)
        pieces = scatter_line(*order_combiners(exits, table))
        combiners_gradient = return_combiners(pieces, 3)
        entry_shares = [encoder_shares, decoder_shares, cross_shares]
        expand_shares = [part[:rows] for part in (encoder_feed_shares, decoder_feed_shares)]
        reduce_shares = [part[rows:] for part in (encoder_feed_shares, decoder_feed_shares)]
    else:
        wholes = [
            lax.dynamic_update_slice(
                jnp.zeros((count,) + part.shape, low), part[None], (me, 0, 0)
            ).reshape(-1, model_width)
            for part in exits
        ]
        combiners_gradient = lax.psum(jnp.stack([send([part])[0] for part in wholes]), "seq")
        entry_shares = [encoder_shares[0], decoder_shares[0]]
        entry_shares.append(jnp.concatenate(cross_shares, 1))
        expand_shares = [encoder_feed_shares[0], decoder_feed_shares[0]]
        reduce_shares = [encoder_feed_shares[1], decoder_feed_shares[1]]

    def whole_entry(part):
        joined = spread_order([p.reshape(rows, 3, share) for p in spread(part)], 2)
        return joined.reshape(rows, -1)

    def whole_expand(part):
        joined = spread_order([p.reshape(rows, shards, -1) for p in spread(part)], 2)
        return joined.reshape(rows, -1)

    def whole_reduce(part):
        return spread_order(spread(part), 0).reshape(-1, model_width)

    projections_gradient = jnp.stack([whole_entry(part) for part in entry_shares]).astype(high)
    expanders_gradient = jnp.stack([whole_expand(part) for part in expand_shares]).astype(high)
    reducers_gradient = jnp.stack([whole_reduce(part) for part in reduce_shares]).astype(high)

    norms = (norm_zero, norm_one, norm_two, norm_three, norm_four)
    norm_sums = jnp.stack([sums[:2] for sums in norms])
    inner = jnp.stack([encoder_sums, decoder_sums, cross_sums])
    inner_whole = lax.dynamic_update_slice(
        jnp.zeros((3, 2, count, share), high), inner[:, :, None], (0, 0, me, 0)
    )
    outer = jnp.stack([norm_one[2], norm_three[2], norm_four[2]])
    hidden_sums = jnp.stack([encoder_hidden_sum, decoder_hidden_sum]).reshape(2, shards, 1, -1)
    hidden_whole = lax.dynamic_update_slice(
        jnp.zeros((2, shards, count, hidden_sums.shape[3]), high), hidden_sums, (0, 0, me, 0)
    )
    exit_sums = jnp.concatenate([source_sum, target_sum])
    parts = [norm_sums, inner_whole, outer, hidden_whole, exit_sums]
    summed = sum_everywhere(jnp.concatenate([part.reshape(-1, 128) for part in parts], 0))
    sizes = [part.size // 128 for part in parts]
    starts = [sum(sizes[:i]) for i in range(len(sizes))]
    norm_sums, inner_whole, outer, hidden_whole, exit_sums = [
        summed[start : start + size].reshape(part.shape)
        for start, size, part in zip(starts, sizes, parts)
    ]
    return (
        memory_low[None],
        decoded_low[None],
        source_gradient[None],
        target_gradient[None],
        projections_gradient,
        combiners_gradient.astype(high),
        expanders_gradient,
        reducers_gradient,
        norm_sums[:, 0],
        norm_sums[:, 1],
        jnp.concatenate([inner_whole.reshape(3, 2, -1), outer[:, None]], 1),
        hidden_whole.reshape(2, -1),
        exit_sums,
    )


def solution(mesh):
    in_specs = (
        P("batch", "seq", None),
        P("batch", "seq", None),
        P("batch", None),
        P("batch", None),
        P(None, "batch", None),
        P(None, "batch", None),
        P(None, "batch", None),
        P(None, "batch", None),
        P(),
        P(),
        P(),
        P(),
        P(),
        P("batch", "seq", None),
        P("batch", "seq", None),
    )
    out_specs = (
        P("batch", "seq", None),
        P("batch", "seq", None),
        P("batch", "seq", None),
        P("batch", "seq", None),
        P(None, "batch", None),
        P(None, "batch", None),
        P(None, "batch", None),
        P(None, "batch", None),
        P(),
        P(),
        P(),
        P(),
        P(),
    )
    return jax.shard_map(
        per_device, mesh=mesh, in_specs=in_specs, out_specs=out_specs, check_vma=False
    )
```

```python
import jax
import jax.numpy as jnp
from jax import lax
from jax.experimental import pallas as pl
from jax.experimental.pallas import tpu as pltpu
from jax.sharding import PartitionSpec as P

HEADS = 16
COST = 0.05


epsilon = 1e-05
masked_score = -1e30
low = jnp.bfloat16
high = jnp.float32
shape = jax.ShapeDtypeStruct
VMEM = pl.BlockSpec(memory_space=pltpu.VMEM)
SMEM = pl.BlockSpec(memory_space=pltpu.SMEM)
across_rows = (((0,), (0,)), ((), ()))
across_lanes = (((1,), (1,)), ((), ()))


class Turn:
    last = None


def after(values, earlier):
    return lax.optimization_barrier((values, earlier))[0]


def hold(values):
    return values if Turn.last is None else after(values, Turn.last)


def take_turn(call, args, skip=0):
    args = list(args)
    least = min(range(skip, len(args)), key=lambda i: args[i].size)
    args[least] = hold(args[least])
    results = call(*args)
    Turn.last = min(results, key=lambda value: value.size)
    return results


def run(kernel, outs, args, name, flops, scratch=(), scalars=0, room=24):
    call = pl.pallas_call(
        kernel,
        out_shape=list(outs),
        in_specs=[SMEM] * scalars + [VMEM] * (len(args) - scalars),
        out_specs=[VMEM] * len(outs),
        scratch_shapes=list(scratch),
        compiler_params=pltpu.CompilerParams(vmem_limit_bytes=room << 20),
        cost_estimate=pl.CostEstimate(
            flops=int(flops * COST), bytes_accessed=0, transcendentals=0
        ),
        name=name,
    )
    return take_turn(call, args)


def normalize(values, gain, shift):
    middle = jnp.mean(values, -1, keepdims=True)
    centred = values - middle
    width = jnp.mean(centred * centred, -1, keepdims=True)
    return centred * lax.rsqrt(width + epsilon) * gain + shift


def matmul(left, right):
    return jnp.dot(left, right, preferred_element_type=high)


def matmul_back(left, right):
    return lax.dot_general(left, right, across_lanes, preferred_element_type=high)


def matmul_outer(left, right):
    return lax.dot_general(left, right, across_rows, preferred_element_type=high)


def piece_rows(pieces):
    start = 0
    for piece in pieces:
        yield pl.ds(start, piece.shape[0]), piece
        start += piece.shape[0]


def assemble(sources, table, parts, height):
    counts = [source.shape[0] // height for source in sources]
    spots = [(i, at) for i, count in enumerate(counts) for at in range(count)]

    def kernel(table_ref, *refs):
        outs = refs[len(sources) :]
        for which, (start, rows, _) in enumerate(parts):
            for i, (source, at) in enumerate(spots):
                first = at * height + start
                where = pl.ds(pl.multiple_of(table_ref[which, i], rows), rows)
                outs[which][where, :] = refs[source][first : first + rows, :]

    width = sources[0].shape[1]
    outs = [shape((whole, width), low) for _, _, whole in parts]
    return run(kernel, outs, [table, *sources], "assemble", 1, scalars=1)


def part_rows(pieces, height, first, rows):
    count = pieces.shape[0] // height

    def kernel(source, out):
        for i in range(count):
            start = i * height + first
            out[i * rows : (i + 1) * rows, :] = source[start : start + rows, :]

    outs = [shape((count * rows, pieces.shape[1]), low)]
    return run(kernel, outs, [pieces], "part_rows", 1)[0]


def project_self(pieces, gain, shift, entry, biases):
    count, width = len(pieces), entry.shape[1] // 3

    def kernel(*refs):
        sources = refs[:count]
        gain_ref, shift_ref, entry_ref, bias_ref, normed_ref, query_ref, key_ref, value_ref = refs[
            count:
        ]
        for rows, source in piece_rows(sources):
            normed = normalize(source[...].astype(high), gain_ref[...], shift_ref[...])
            normed_ref[rows, :] = normed.astype(low)
            joined = matmul(normed_ref[rows, :], entry_ref[...])
            query_ref[rows, :] = (joined[:, :width] + bias_ref[0:1, :]).astype(low)
            key_ref[rows, :] = joined[:, width : 2 * width].astype(low)
            value_ref[rows, :] = (joined[:, 2 * width :] + bias_ref[1:2, :]).astype(low)

    rows = sum(piece.shape[0] for piece in pieces)
    outs = [shape((rows, pieces[0].shape[1]), low)] + [shape((rows, width), low)] * 3
    flops = 2 * rows * entry.shape[0] * entry.shape[1]
    return run(kernel, outs, [*pieces, gain, shift, entry, biases], "project_self", flops)


def project_cross(pieces, memory_pieces, entry, biases):
    count, width = len(pieces), entry.shape[1] // 3

    def kernel(*refs):
        sources, memories = refs[:count], refs[count : 2 * count]
        entry_ref, bias_ref, query_ref, key_ref, value_ref = refs[2 * count :]
        for rows, source in piece_rows(sources):
            joined = matmul(source[...], entry_ref[:, :width])
            query_ref[rows, :] = (joined + bias_ref[0:1, :]).astype(low)
        for rows, source in piece_rows(memories):
            joined = matmul(source[...], entry_ref[:, width:])
            key_ref[rows, :] = joined[:, :width].astype(low)
            value_ref[rows, :] = (joined[:, width:] + bias_ref[1:2, :]).astype(low)

    rows = sum(piece.shape[0] for piece in pieces)
    outs = [shape((rows, width), low)] * 3
    flops = 2 * rows * entry.shape[0] * entry.shape[1]
    return run(kernel, outs, [*pieces, *memory_pieces, entry, biases], "project_cross", flops)


def head_lanes(values, head, width):
    lanes = lax.broadcasted_iota(jnp.int32, values.shape, 1)
    inside = (lanes >= head * width) & (lanes < (head + 1) * width)
    return jnp.where(inside, values, jnp.zeros_like(values))


def block_bias(keys, cols, causal, key_segment, query_segment, key_place, query_place):
    allowed = key_segment[keys, :] == query_segment[:, cols]
    if causal:
        allowed = allowed & (key_place[keys, :] <= query_place[:, cols])
    return jnp.where(allowed, 0.0, masked_score)


def attend_forward(marks, tags, queries, keys, values, heads, causal):
    rows, width = queries.shape
    head_width = width // heads
    block = min(256, rows)
    blocks = rows // block
    scale = head_width**-0.5
    tall = max(8, heads)

    def kernel(*refs):
        marks_ref, key_segment, query_segment, key_place, query_place = refs[:5]
        query_ref, key_ref, value_ref, mixture_ref, total_ref = refs[5:10]
        score_ref, top_ref, sum_ref, mix_ref, value_turned = refs[10:]
        value_turned[...] = value_ref[...].astype(high).T.astype(low)
        total_ref[...] = jnp.zeros(total_ref.shape, high)
        for i in range(blocks):
            mine = pl.ds(i * block, block)
            cols = slice(i * block, (i + 1) * block)
            query = query_ref[mine, :] * low(scale)
            query_heads = [head_lanes(query, head, head_width) for head in range(heads)]
            top_ref[...] = jnp.full(top_ref.shape, masked_score, high)
            sum_ref[...] = jnp.zeros(sum_ref.shape, high)
            mix_ref[...] = jnp.zeros(mix_ref.shape, high)

            def score(j, carry, i=i, cols=cols, query_heads=query_heads):
                @pl.when(marks_ref[i, j] != 0)
                def _():
                    there = pl.ds(pl.multiple_of(j * block, block), block)
                    bias = block_bias(
                        there, cols, causal, key_segment, query_segment, key_place, query_place
                    )
                    for head in range(heads):
                        scores = matmul_back(key_ref[there, :], query_heads[head]) + bias
                        score_ref[head, there, :] = scores
                        row = slice(head, head + 1)
                        top_ref[row, :] = jnp.maximum(
                            top_ref[row, :], jnp.max(scores, 0, keepdims=True)
                        )

                return carry

            lax.fori_loop(0, blocks, score, 0)

            def mix(j, carry, i=i):
                @pl.when(marks_ref[i, j] != 0)
                def _():
                    there = pl.ds(pl.multiple_of(j * block, block), block)
                    for head in range(heads):
                        row = slice(head, head + 1)
                        features = slice(head * head_width, (head + 1) * head_width)
                        weights = jnp.exp(score_ref[head, there, :] - top_ref[row, :])
                        sum_ref[row, :] += jnp.sum(weights, 0, keepdims=True)
                        mix_ref[features, :] += matmul(
                            value_turned[features, there], weights.astype(low)
                        )

                return carry

            lax.fori_loop(0, blocks, mix, 0)
            for head in range(heads):
                row = slice(head, head + 1)
                features = slice(head * head_width, (head + 1) * head_width)
                mix_ref[features, :] = mix_ref[features, :] * (1.0 / sum_ref[row, :])
                total_ref[row, cols] = top_ref[row, :] + jnp.log(sum_ref[row, :])
            mixture_ref[mine, :] = mix_ref[...].T.astype(low)

    outs = [shape((rows, width), low), shape((tall, rows), high)]
    scratch = [
        pltpu.VMEM((heads, rows, block), high),
        pltpu.VMEM((tall, block), high),
        pltpu.VMEM((tall, block), high),
        pltpu.VMEM((width, block), high),
        pltpu.VMEM((width, rows), low),
    ]
    flops = 8 * rows * rows * width
    args = [marks, *tags, queries, keys, values]
    return run(kernel, outs, args, "attend_forward", flops, scratch, scalars=1)


def project_out(mixture, leave, count):
    local = mixture.shape[0] // count

    def kernel(mixture_ref, leave_ref, *outs):
        for i, out in enumerate(outs):
            out[...] = matmul(mixture_ref[pl.ds(i * local, local), :], leave_ref[...]).astype(low)

    outs = [shape((local, leave.shape[1]), low)] * count
    return run(kernel, outs, [mixture, leave], "project_out", 2 * mixture.size * leave.shape[1])


def attend_backward(marks, tags, pieces, leave, entry, stored, heads, causal, cross):
    queries, keys, values, mixture, total = stored
    count = len(pieces)
    rows, width = queries.shape
    head_width = width // heads
    block = min(256, rows)
    blocks = rows // block
    local = rows // count
    scale = head_width**-0.5

    def kernel(*refs):
        marks_ref, key_segment, query_segment, key_place, query_place = refs[:5]
        incoming_refs = refs[5 : 5 + count]
        leave_ref, entry_ref, query_ref, key_ref, value_ref, mixture_ref, total_ref = refs[
            5 + count : 12 + count
        ]
        joined_ref, sums_ref = refs[12 + count : 14 + count]
        partial_refs = refs[14 + count : 14 + 2 * count]
        memory_refs = refs[14 + 2 * count : -5]
        incoming_mix, key_sum, value_sum, query_turned, key_turned = refs[-5:]
        for where, piece in piece_rows(incoming_refs):
            incoming_mix[where, :] = matmul_back(piece[...], leave_ref[...]).astype(low)
        key_turned[...] = key_ref[...].astype(high).T.astype(low)
        key_sum[...] = jnp.zeros(key_sum.shape, high)
        value_sum[...] = jnp.zeros(value_sum.shape, high)
        query_total = jnp.zeros((1, width), high)
        for i in range(blocks):
            mine = pl.ds(i * block, block)
            cols = slice(i * block, (i + 1) * block)
            query = query_ref[mine, :] * low(scale)
            arriving = incoming_mix[mine, :]
            query_heads = [head_lanes(query, head, head_width) for head in range(heads)]
            arriving_heads = [head_lanes(arriving, head, head_width) for head in range(heads)]
            products = (arriving.astype(high) * mixture_ref[mine, :].astype(high)).T
            inner = [
                jnp.sum(products[head * head_width : (head + 1) * head_width, :], 0, keepdims=True)
                for head in range(heads)
            ]
            query_turned[...] = jnp.zeros(query_turned.shape, high)

            def step(j, carry, i=i, cols=cols, qh=query_heads, ah=arriving_heads, inner=inner):
                @pl.when(marks_ref[i, j] != 0)
                def _():
                    there = pl.ds(pl.multiple_of(j * block, block), block)
                    bias = block_bias(
                        there, cols, causal, key_segment, query_segment, key_place, query_place
                    )
                    key_acc, value_acc = key_sum[there, :], value_sum[there, :]
                    for head in range(heads):
                        features = slice(head * head_width, (head + 1) * head_width)
                        scores = matmul_back(key_ref[there, :], qh[head])
                        weights = jnp.exp(scores - total_ref[head : head + 1, cols] + bias)
                        back = matmul_back(value_ref[there, :], ah[head])
                        change = (weights * (back - inner[head])).astype(low)
                        value_acc = value_acc + matmul(weights.astype(low), ah[head])
                        key_acc = key_acc + matmul(change, qh[head])
                        query_turned[features, :] += matmul(key_turned[features, there], change)
                    key_sum[there, :] = key_acc
                    value_sum[there, :] = value_acc

                return carry

            lax.fori_loop(0, blocks, step, 0)
            query_gradient = query_turned[...].T * scale
            query_total = query_total + jnp.sum(query_gradient, 0, keepdims=True)
            joined_ref[mine, :width] = query_gradient.astype(low)
        joined_ref[:, width : 2 * width] = key_sum[...].astype(low)
        joined_ref[:, 2 * width :] = value_sum[...].astype(low)
        sums_ref[0:1, :] = query_total
        sums_ref[1:2, :] = jnp.sum(value_sum[...], 0, keepdims=True)
        for i in range(count):
            mine = pl.ds(i * local, local)
            if cross:
                query_part = matmul_back(joined_ref[mine, :width], entry_ref[:, :width])
                memory_part = matmul_back(joined_ref[mine, width:], entry_ref[:, width:])
                partial_refs[i][...] = query_part.astype(low)
                memory_refs[i][...] = memory_part.astype(low)
            else:
                partial_refs[i][...] = matmul_back(joined_ref[mine, :], entry_ref[...]).astype(low)

    outs = [shape((rows, 3 * width), low), shape((2, width), high)]
    outs += [shape((local, entry.shape[0]), low)] * (count * (2 if cross else 1))
    scratch = [
        pltpu.VMEM((rows, width), low),
        pltpu.VMEM((rows, width), high),
        pltpu.VMEM((rows, width), high),
        pltpu.VMEM((width, block), high),
        pltpu.VMEM((width, rows), low),
    ]
    flops = 20 * rows * rows * width + 10 * rows * width * entry.shape[0]
    args = [marks, *tags, *pieces, leave, entry, queries, keys, values, mixture, total]
    joined, sums, *partials = run(
        kernel, outs, args, "attend_backward", flops, scratch, scalars=1, room=28
    )
    return joined, sums, partials[:count], partials[count:]


def feed_forward(pieces, entry, leave, bias):
    count, hidden_width = len(pieces), entry.shape[1]
    step = min(512, hidden_width)

    def kernel(*refs):
        sources = refs[:count]
        entry_ref, leave_ref, bias_ref, active_ref, slope_ref = refs[count : count + 5]
        partial_refs = refs[count + 5 :]
        for (rows, source), partial in zip(piece_rows(sources), partial_refs):
            for start in range(0, hidden_width, step):
                cols = slice(start, start + step)
                hidden = matmul(source[...], entry_ref[:, cols]) + bias_ref[:, cols]
                share = 0.5 * (1.0 + lax.erf(hidden * 0.7071067811865476))
                density = jnp.exp(-0.5 * hidden * hidden) * 0.3989422804014327
                active_ref[rows, cols] = (hidden * share).astype(low)
                slope_ref[rows, cols] = (share + hidden * density).astype(low)
            partial[...] = matmul(active_ref[rows, :], leave_ref[...]).astype(low)

    rows = sum(piece.shape[0] for piece in pieces)
    outs = [shape((rows, hidden_width), low)] * 2
    outs += [shape((piece.shape[0], leave.shape[1]), low) for piece in pieces]
    flops = 4 * rows * entry.shape[0] * hidden_width
    args = [*pieces, entry, leave, bias]
    active, slope, *partials = run(kernel, outs, args, "feed_forward", flops)
    return active, slope, partials


def feed_backward(pieces, entry, leave, slope):
    count, hidden_width = len(pieces), entry.shape[1]

    def kernel(*refs):
        sources = refs[:count]
        entry_ref, leave_ref, slope_ref, hidden_ref, sum_ref = refs[count : count + 5]
        partial_refs = refs[count + 5 :]
        total = jnp.zeros(sum_ref.shape, high)
        for (rows, source), partial in zip(piece_rows(sources), partial_refs):
            hidden = matmul_back(source[...], leave_ref[...]) * slope_ref[rows, :].astype(high)
            total = total + jnp.sum(hidden, 0, keepdims=True)
            hidden_ref[rows, :] = hidden.astype(low)
            partial[...] = matmul_back(hidden_ref[rows, :], entry_ref[...]).astype(low)
        sum_ref[...] = total

    rows = sum(piece.shape[0] for piece in pieces)
    outs = [shape((rows, hidden_width), low), shape((1, hidden_width), high)]
    outs += [shape((piece.shape[0], entry.shape[0]), low) for piece in pieces]
    flops = 4 * rows * entry.shape[0] * hidden_width
    args = [*pieces, entry, leave, slope]
    hidden, total, *partials = run(kernel, outs, args, "feed_backward", flops)
    return hidden, total, partials


def blocks_out(shards, height, width):
    return [shape((shards // 2, height, width), low)] * 2


def block_targets(refs):
    return [(ref, at) for ref in refs for at in range(ref.shape[0])]


def outer_sums(pairs, order, name, stacked=False):
    flat, counts, flops = [], [], 0
    for lefts, rights, start, lanes in pairs:
        flat += [*lefts, *rights]
        counts.append((len(lefts), len(rights), start, lanes))
        flops += 2 * sum(left.size for left in lefts) * lanes
    sizes = [(pair[0][0].shape[1], pair[3]) for pair in pairs]

    def compute(refs, outs):
        for (left_count, right_count, start, lanes), out in zip(counts, outs):
            lefts, rights = refs[:left_count], refs[left_count : left_count + right_count]
            refs = refs[left_count + right_count :]
            terms = max(left_count, right_count)
            rows = sum(left.shape[0] for left in lefts) // terms
            step = min(256, out.shape[0])
            side = slice(start, start + lanes)
            for first in range(0, out.shape[0], step):
                cols = slice(first, first + step)
                total = None
                for i in range(terms):
                    where = pl.ds(i * rows, rows)
                    left = lefts[i][:, cols] if left_count == terms else lefts[0][where, cols]
                    right = rights[i][:, side] if right_count == terms else rights[0][where, side]
                    term = matmul_outer(left, right)
                    total = term if total is None else total + term
                out[cols, :] = total.astype(low)

    if order is None:

        def plain(*refs):
            compute(refs[: len(flat)], refs[len(flat) :])

        return run(plain, [shape(size, low) for size in sizes], flat, name, flops)

    straight = isinstance(order, int)
    shards = order if straight else order.shape[0]
    heights = [size[0] // shards for size in sizes]
    if stacked:
        corners = [(sum(heights[:i]), 0) for i in range(len(sizes))]
        outs = blocks_out(shards, sum(heights), sizes[0][1])
    else:
        corners = [(0, sum(size[1] for size in sizes[:i])) for i in range(len(sizes))]
        outs = blocks_out(shards, heights[0], sum(size[1] for size in sizes))
    scratch = [pltpu.VMEM(size, low) for size in sizes]
    if straight:
        height, width = outs[0].shape[1:]

        def fixed(*refs):
            inputs, (out, *buffers) = refs[: len(flat)], refs[len(flat) :]
            compute(inputs, buffers)
            for i in range(shards):
                for source, rows, (top, side) in zip(buffers, heights, corners):
                    part = source[i * rows : (i + 1) * rows, :]
                    out[i, top : top + rows, side : side + source.shape[1]] = part

        return run(fixed, [shape((shards, height, width), low)], flat, name, flops, scratch)[0]

    def kernel(order_ref, *refs):
        inputs, rest = refs[: len(flat)], refs[len(flat) :]
        compute(inputs, rest[2:])
        for i, (target, at) in enumerate(block_targets(rest[:2])):
            for source, rows, (top, side) in zip(rest[2:], heights, corners):
                where = pl.ds(pl.multiple_of(order_ref[i] * rows, rows), rows)
                target[at, top : top + rows, side : side + source.shape[1]] = source[where, :]

    return run(kernel, outs, [order, *flat], name, flops, scratch, scalars=1)


def order_combiners(exits, table):
    shards = table.shape[0]
    rows = exits[0].shape[0] // shards

    def kernel(table_ref, *refs):
        sources = refs[: len(exits)]
        for i, (target, at) in enumerate(block_targets(refs[len(exits) :])):
            where = pl.ds(pl.multiple_of(table_ref[i], rows), rows)
            for block, source in enumerate(sources):
                target[at, block * rows : (block + 1) * rows, :] = source[where, :]

    outs = blocks_out(shards, rows * len(exits), exits[0].shape[1])
    return run(kernel, outs, [table, *exits], "order_combiners", 1, scalars=1)


def cut(arrays, table, moves, outs, name):
    def kernel(table_ref, *refs):
        sources, targets, semaphore = refs[: len(arrays)], refs[len(arrays) : -1], refs[-1]
        copies = []
        for array, block, rows, (row, down), lanes, (lane, along), entry, out, top, side in moves:
            where = table_ref[entry]
            first = row + pl.multiple_of(where * down, down) if down else row
            left = pl.multiple_of(lane + where * along, lanes) if along else lane
            source = sources[array].at[block, pl.ds(first, rows), pl.ds(left, lanes)]
            target = targets[out].at[pl.ds(top, rows), pl.ds(side, lanes)]
            copies.append(pltpu.make_async_copy(source, target, semaphore.at[len(copies)]))
            copies[-1].start()
        for started in copies:
            started.wait()

    anywhere = pl.BlockSpec(memory_space=pltpu.HBM)
    call = pl.pallas_call(
        kernel,
        out_shape=outs,
        in_specs=[SMEM] + [anywhere] * len(arrays),
        out_specs=[VMEM] * len(outs),
        scratch_shapes=[pltpu.SemaphoreType.DMA((len(moves),))],
        compiler_params=pltpu.CompilerParams(vmem_limit_bytes=16 << 20),
        cost_estimate=pl.CostEstimate(flops=1, bytes_accessed=0, transcendentals=0),
        name=name,
    )
    return take_turn(call, [table, *arrays])


def finish(pieces, table, former, outputs, name):
    count = len(pieces)

    def kernel(table_ref, *refs):
        sources = refs[:count]
        refs = refs[count + len(former) :]
        targets, buffers, semaphore = refs[: len(outputs)], refs[len(outputs) : -1], refs[-1]
        copies = []
        for i, ((_, block, moves), target, buffer) in enumerate(zip(outputs, targets, buffers)):
            for which, source in enumerate(sources):
                owner = table_ref[which]
                for (top, rows), (side, lanes), (row, row_step), (lane, lane_step) in moves:
                    down = row + pl.multiple_of(owner * row_step, row_step) if row_step else row
                    along = lane + owner * lane_step if lane_step else lane
                    if lane_step:
                        along = pl.multiple_of(along, lanes)
                    part = source[top : top + rows, side : side + lanes].astype(high)
                    buffer[pl.ds(down, rows), pl.ds(along, lanes)] = part
            copies.append(pltpu.make_async_copy(buffer, target.at[block], semaphore.at[i]))
            copies[-1].start()
        for started in copies:
            started.wait()

    anywhere = pl.BlockSpec(memory_space=pl.ANY)
    aliases = {1 + count + i: i for i in range(len(former))}
    call = pl.pallas_call(
        kernel,
        out_shape=[shape(size, high) for size, _, _ in outputs],
        in_specs=[SMEM] + [VMEM] * count + [anywhere] * len(former),
        out_specs=[anywhere] * len(outputs),
        scratch_shapes=[pltpu.VMEM(size[1:], high) for size, _, _ in outputs]
        + [pltpu.SemaphoreType.DMA((len(outputs),))],
        input_output_aliases=aliases,
        compiler_params=pltpu.CompilerParams(vmem_limit_bytes=24 << 20),
        cost_estimate=pl.CostEstimate(flops=1, bytes_accessed=0, transcendentals=0),
        name=name,
    )
    table = hold(table)
    return call(table, *pieces, *former)


def lay_sums(rows, shares, hidden, me, shards):
    width, share = rows[0].shape[1], shares[0].shape[1]
    narrow = hidden[0].shape[1] // shards
    group = narrow * (width // share)
    per_row = width // group
    used = sum(part.shape[0] for part in [*rows, *shares]) + len(hidden) * shards // per_row
    total = -(-used // 8) * 8

    def kernel(me_ref, *refs):
        out = refs[-1]
        mine = me_ref[0]
        out[...] = jnp.zeros(out.shape, high)
        at = 0
        for ref in refs[: len(rows)]:
            out[at : at + ref.shape[0], :] = ref[...]
            at += ref.shape[0]
        side = pl.ds(pl.multiple_of(mine * share, share), share)
        for ref in refs[len(rows) : len(rows) + len(shares)]:
            out[at : at + ref.shape[0], side] = ref[...]
            at += ref.shape[0]
        for ref in refs[len(rows) + len(shares) : -1]:
            for shard in range(shards):
                start = (shard % per_row) * group + mine * narrow
                row = at + shard // per_row
                here = slice(shard * narrow, (shard + 1) * narrow)
                out[row : row + 1, pl.ds(pl.multiple_of(start, narrow), narrow)] = ref[:, here]
            at += shards // per_row

    args = [me, *rows, *shares, *hidden]
    return run(kernel, [shape((total, width), high)], args, "lay_sums", total, scalars=1)[0]


def add_up(refs):
    total = refs[0][...].astype(high)
    for ref in refs[1:]:
        total = total + ref[...].astype(high)
    return total


def residual_norm(base, addends, bias, gain, shift):
    count = 1 + len(addends)

    def kernel(*refs):
        bias_ref, gain_ref, shift_ref, total_ref, normed_ref = refs[count:]
        total = add_up(refs[:count]) + bias_ref[...]
        total_ref[...] = total
        normed_ref[...] = normalize(total, gain_ref[...], shift_ref[...]).astype(low)

    outs = [shape(base.shape, high), shape(base.shape, low)]
    return run(kernel, outs, [base, *addends, bias, gain, shift], "residual_norm", base.size * 12)


def residual_low(base, addends, bias):
    count = 1 + len(addends)

    def kernel(*refs):
        bias_ref, total_ref = refs[count:]
        total_ref[...] = (add_up(refs[:count]) + bias_ref[...]).astype(low)

    outs = [shape(base.shape, low)]
    return run(kernel, outs, [base, *addends, bias], "residual_low", base.size * 4)[0]


def join_gradient(cotangent, keep, addends):
    count = len(addends)

    def kernel(*refs):
        cotangent_ref, keep_ref = refs[:2]
        gradient_ref, low_ref, sum_ref = refs[2 + count :]
        total = cotangent_ref[...].astype(high) * keep_ref[...]
        for ref in refs[2 : 2 + count]:
            total = total + ref[...].astype(high)
        gradient_ref[...] = total
        low_ref[...] = total.astype(low)
        sum_ref[...] = jnp.sum(total, 0, keepdims=True)

    outs = [
        shape(cotangent.shape, high),
        shape(cotangent.shape, low),
        shape((1, cotangent.shape[1]), high),
    ]
    return run(kernel, outs, [cotangent, keep, *addends], "join_gradient", cotangent.size * 4)


def norm_backward(inputs, gain, incoming, addends):
    count = len(addends)

    def kernel(*refs):
        input_ref, gain_ref, incoming_ref = refs[:3]
        result_ref, low_ref, sums_ref = refs[3 + count :]
        gradient = add_up(refs[3 : 3 + count])
        values = input_ref[...].astype(high)
        centred = values - jnp.mean(values, -1, keepdims=True)
        inverse = lax.rsqrt(jnp.mean(centred * centred, -1, keepdims=True) + epsilon)
        unit = centred * inverse
        sums_ref[0:1, :] = jnp.sum(gradient * unit, 0, keepdims=True)
        sums_ref[1:2, :] = jnp.sum(gradient, 0, keepdims=True)
        scaled = gradient * gain_ref[...]
        inner = jnp.mean(scaled * unit, -1, keepdims=True)
        change = (scaled - jnp.mean(scaled, -1, keepdims=True) - unit * inner) * inverse
        result = incoming_ref[...] + change
        result_ref[...] = result
        low_ref[...] = result.astype(low)
        sums_ref[2:3, :] = jnp.sum(result, 0, keepdims=True)

    outs = [
        shape(inputs.shape, high),
        shape(inputs.shape, low),
        shape((3, inputs.shape[1]), high),
    ]
    args = [inputs, gain, incoming, *addends]
    return run(kernel, outs, args, "norm_backward", inputs.size * 20)


def seq_bits():
    bit, bits = lax.axis_size("seq") >> 1, []
    while bit:
        bits.append(bit)
        bit >>= 1
    return bits


def seq_offsets():
    offsets = [0]
    for bit in seq_bits():
        offsets = offsets + [offset ^ bit for offset in offsets]
    return offsets


def swap(values, bit, axis="seq"):
    return lax.ppermute(values, axis, [(i, i ^ bit) for i in range(lax.axis_size(axis))])


def spread(piece):
    pieces = [piece]
    for bit in seq_bits():
        pieces = pieces + [swap(piece, bit) for piece in pieces]
    return pieces


def quick():
    return lax.axis_size("seq") == 4 and lax.axis_size("batch") == 8


class Spread:
    def __init__(self, piece):
        self.pieces = [piece]
        if quick():
            self.far = swap(piece, 2)
            self.near = swap(piece, 1)

    def finish(self):
        if not quick():
            return spread(self.pieces[0])
        far = hold(self.far)
        return [self.pieces[0], far, self.near, swap(far, 1)]


class Collect:
    def __init__(self, partials):
        self.partials = partials
        if quick():
            self.second = swap(partials[3], 1)
            self.first = swap(partials[2], 1)

    def turn(self):
        if quick():
            total = add_low([self.partials[1], self.second])
            self.far = swap(total, 2)

    def finish(self):
        if quick():
            return [self.partials[0], self.first, self.far]
        kept = [[partial] for partial in self.partials]
        for bit in reversed(seq_bits()):
            half = len(kept) // 2
            sent = [part[0] if len(part) == 1 else add_low(part) for part in kept[half:]]
            kept = [own + [swap(other, bit)] for own, other in zip(kept[:half], sent)]
        return kept[0]


def add_low(addends):
    def kernel(*refs):
        refs[-1][...] = add_up(refs[:-1]).astype(low)

    return run(kernel, [shape(addends[0].shape, low)], addends, "add_low", addends[0].size)[0]


def add_high(addends):
    def kernel(*refs):
        refs[-1][...] = add_up(refs[:-1])

    return run(kernel, [shape(addends[0].shape, high)], addends, "add_high", addends[0].size)[0]


def mine(values, axis):
    return lax.dynamic_index_in_dim(values, lax.axis_index("seq"), axis, keepdims=False)


def line_place():
    return lax.axis_index("batch") // 2, lax.axis_index("batch") % 2


def line_groups():
    shards = lax.axis_size("batch")
    return [list(range(side, shards, 2)) for side in range(2)]


def line_order():
    _, side = line_place()
    at = 2 * jnp.arange(lax.axis_size("batch") // 2, dtype=jnp.int32)
    return jnp.concatenate([at + side, at + 1 - side])


def relay_order():
    place, side = line_place()
    at = (place - jnp.arange(4, dtype=jnp.int32)) % 4
    return jnp.concatenate([2 * at + side, 2 * at + 1 - side])


class Relay:
    def __init__(self, values):
        self.line, self.across = [values], []
        self.touch()

    def touch(self):
        newest = self.line[-1] = hold(self.line[-1])
        if len(self.line) < 4:
            shards = lax.axis_size("batch")
            pairs = [(i, (i + 2) % shards) for i in range(shards)]
            self.line.append(lax.ppermute(newest, "batch", pairs))
        self.across.append(to_side(newest))

    def pieces(self):
        return self.line + self.across


def gather_line(values):
    return lax.all_gather(values, "batch", axis=0, tiled=True, axis_index_groups=line_groups())


def to_side(values):
    return swap(values, 1, "batch")


class Scatter:
    def __init__(self, blocks):
        self.keep, sent = blocks
        self.arrived = to_side(sent)

    def turn(self):
        total = add_low([self.keep, self.arrived])
        self.sums = lax.psum_scatter(
            total, "batch", scatter_dimension=0, tiled=False, axis_index_groups=line_groups()
        )

    def finish(self):
        return add_low([self.sums])


class Sum:
    def __init__(self, values):
        bits = [(axis, 1 << i) for axis in ("seq", "batch") for i in range(5)]
        self.left = [(axis, bit) for axis, bit in bits if bit < lax.axis_size(axis)]
        self.values = values
        self.send()

    def send(self):
        axis, bit = self.left.pop(0)
        self.arrived = swap(self.values, bit, axis)

    def turn(self):
        self.values = add_high([self.values, self.arrived])
        if self.left:
            self.send()


def line_pairs(step, count, back):
    pairs = []
    for place in range(count):
        for side in range(2):
            here = (place * 2 + side) * count + place
            there = (((place + step) % count) * 2 + side) * count + place
            pairs.append((there, here) if back else (here, there))
    return pairs


def add_dealt(own, sent, owned):
    def kernel(owned_ref, own_ref, *refs):
        total = add_up(refs[:-1])
        kept = own_ref[...].astype(high)
        refs[-1][...] = jnp.where(owned_ref[0] != 0, kept, total).astype(low)

    outs = [shape(own.shape, low)]
    return run(kernel, outs, [owned, own, *sent], "add_dealt", own.size, scalars=1)[0]


class Return:
    def __init__(self, pieces, blocks):
        self.blocks, self.left = blocks, seq_bits()
        self.arrived = [pieces] + [
            lax.ppermute(pieces, ("batch", "seq"), line_pairs(step, 4, True)) for step in range(1, 4)
        ]

    def turn(self):
        me = lax.axis_index("seq")
        place, _ = line_place()
        if isinstance(self.arrived, list):
            table = (me + jnp.arange(4, dtype=jnp.int32)) % 4
            self.ordered = stack_places(self.arrived, table, self.blocks)
        else:
            self.ordered = self.pick()
        bit = self.left.pop(0)
        self.mine = ((place & bit) == (me & bit)).astype(jnp.int32)[None]
        self.arrived = swap(self.ordered, bit)

    def pick(self):
        return choose(self.ordered, self.arrived, self.mine, low)

    def finish(self):
        return choose(self.ordered, self.arrived, self.mine, high)


def stack_places(pieces, table, blocks):
    rows = pieces[0].shape[0] // blocks

    def kernel(table_ref, *refs):
        out = refs[-1]
        for i, source in enumerate(refs[:-1]):
            where = pl.ds(pl.multiple_of(table_ref[i] * rows, rows), rows)
            for block in range(blocks):
                out[block, where, :] = source[block * rows : (block + 1) * rows, :]

    outs = [shape((blocks, rows * len(pieces), pieces[0].shape[1]), low)]
    return run(kernel, outs, [table, *pieces], "stack_places", 1, scalars=1)[0]


def choose(one, other, first, kind):
    def kernel(first_ref, one_ref, other_ref, out):
        out[...] = jnp.where(first_ref[0] != 0, one_ref[...], other_ref[...]).astype(kind)

    return run(kernel, [shape(one.shape, kind)], [first, one, other], "choose", 1, scalars=1)[0]


def gather_whole(projections, combiners, expanders, reducers):
    count, shards = lax.axis_size("seq"), lax.axis_size("batch")
    blocks, rows, _ = projections.shape
    feeds, _, _ = expanders.shape
    model_width = combiners.shape[2]
    entries = mine(projections.reshape(blocks, rows, 3, count, -1), 3).reshape(blocks, rows, -1)
    expand = mine(expanders.reshape(feeds, rows, shards, count, -1), 3).reshape(feeds, rows, -1)
    reduce = mine(reducers.reshape(feeds, count, -1, model_width), 1)

    def whole(values):
        return lax.all_gather(values, "batch", axis=0, tiled=True)

    leaves = [whole(combiners[i]).reshape(count, -1, model_width) for i in range(blocks)]
    return (
        [whole(entries[i]) for i in range(blocks)],
        [mine(leave, 0) for leave in leaves],
        [whole(expand[i]) for i in range(feeds)],
        [whole(reduce[i]) for i in range(feeds)],
    )


def spread_order(pieces, axis):
    me = lax.axis_index("seq")
    stacked = jnp.stack(pieces)
    offsets = jnp.array([seq_offsets().index(i) for i in range(len(pieces))], jnp.int32)
    ordered = [
        lax.dynamic_index_in_dim(stacked, offsets[me ^ i], 0, keepdims=False)
        for i in range(len(pieces))
    ]
    return jnp.stack(ordered, axis)


def per_device(
    source_tokens,
    target_tokens,
    source_lengths,
    target_lengths,
    projections,
    combiners,
    expanders,
    reducers,
    norm_gains,
    norm_shifts,
    attention_biases,
    expander_biases,
    reducer_biases,
    source_cotangent,
    target_cotangent,
):
    Turn.last = None
    source_tokens, target_tokens = source_tokens[0], target_tokens[0]
    source_cotangent, target_cotangent = source_cotangent[0], target_cotangent[0]
    count, shards = lax.axis_size("seq"), lax.axis_size("batch")
    me = lax.axis_index("seq")
    local_count, model_width = source_tokens.shape
    heads = HEADS // count
    share = model_width // count
    padding_segment = source_lengths.shape[1] - 1

    here = jnp.arange(local_count, dtype=jnp.int32)
    places = jnp.concatenate([(me ^ offset) * local_count + here for offset in seq_offsets()])

    def segments(lengths):
        ends = jnp.cumsum(lengths[0], dtype=jnp.int32)
        return jnp.sum((places[:, None] >= ends[None, :]).astype(jnp.int32), -1, dtype=jnp.int32)

    source_segment, target_segment = segments(source_lengths), segments(target_lengths)
    source_keep = (source_segment[:local_count] < padding_segment).astype(high)[:, None]
    target_keep = (target_segment[:local_count] < padding_segment).astype(high)[:, None]

    def view(query_segment, key_segment, causal):
        def ends_of(values):
            blocks = values.reshape(-1, min(256, values.shape[0]))
            return jnp.min(blocks, 1), jnp.max(blocks, 1)

        query_low, query_high = ends_of(query_segment)
        key_low, key_high = ends_of(key_segment)
        marks = (query_low[:, None] <= key_high[None]) & (key_low[None] <= query_high[:, None])
        if causal:
            place_low, place_high = ends_of(places)
            marks = marks & (place_low[None] <= place_high[:, None])
        tags = (key_segment[:, None], query_segment[None], places[:, None], places[None])
        return marks.astype(jnp.int32), tags

    encoder_view = view(source_segment, source_segment, False)
    self_view = view(target_segment, target_segment, True)
    cross_view = view(target_segment, source_segment, False)

    entry_biases = mine(attention_biases[:, :2].reshape(3, 2, count, share), 2)
    exit_biases = attention_biases[:, 2]
    hidden_biases = mine(expander_biases.reshape(2, shards, count, -1), 2).reshape(2, 1, -1)

    def gain(norm):
        return norm_gains[norm : norm + 1]

    def shift(norm):
        return norm_shifts[norm : norm + 1]

    def exit_bias(block):
        return exit_biases[block : block + 1]

    rows = projections.shape[1]
    feed_rows = reducers.shape[1] // count
    if quick():
        piece = share // shards
        line = (me + jnp.arange(count, dtype=jnp.int32)) % count
        table = jnp.concatenate([me[None], line])

        def entry_cut(block, out, top):
            return [
                (0, block, rows, (0, 0), share, (part * model_width, share), 0, out, top, part * share)
                for part in range(3)
            ]

        moves = entry_cut(0, 0, 0) + [
            (1, block, piece, (0, piece), model_width, (0, 0), 1 + i, 1 + i, block * piece, 0)
            for i in range(count)
            for block in range(3)
        ]
        outs = [shape((rows, 3 * share), low)] + [shape((3 * piece, model_width), low)] * count
        first, *deals = cut([projections, combiners], table, moves, outs, "cut_first")
        entry_relay = Relay(first)
        sent = [
            lax.ppermute(deals[step], ("batch", "seq"), line_pairs(step, count, False))
            for step in range(1, count)
        ]
        lanes = expanders.shape[2] // shards
        moves = entry_cut(1, 2, 0) + entry_cut(2, 2, rows)
        for feed in range(2):
            moves += [
                (1, feed, rows, (0, 0), feed_rows, (part * lanes, feed_rows), 0, feed, 0, part * feed_rows)
                for part in range(shards)
            ]
            moves.append(
                (2, feed, feed_rows, (0, feed_rows), model_width, (0, 0), 0, feed, rows, 0)
            )
        outs = [shape((rows + feed_rows, model_width), low)] * 2
        outs += [shape((2 * rows, 3 * share), low)]
        feed_zero, feed_one, entry_rest = cut(
            [projections, expanders, reducers], table, moves, outs, "cut_rest"
        )
        entry_relay.touch()
        source_spread = Spread(hold(source_tokens))
        entry_relay.touch()
        entry_relay.touch()
        place, _ = line_place()
        order, relayed = line_order(), relay_order()
        entry_table = (order * rows)[None]
        whole_rows = shards * rows
        dealt = add_dealt(deals[0], sent, (place == me).astype(jnp.int32)[None])
        leave_relay = Relay(dealt)
        feed_line = gather_line(hold(feed_zero))
        source_pieces = source_spread.finish()
        encoder_entry = assemble(
            entry_relay.pieces(), (relayed * rows)[None], [(0, rows, whole_rows)], rows
        )[0]
        leave_relay.touch()
        target_spread = Spread(hold(target_tokens))
    else:
        entries, leaves, expand, reduce = gather_whole(
            projections, combiners, expanders, reducers
        )
        encoder_entry, decoder_entry, cross_entry = entries
        source_pieces = spread(source_tokens)
        target_spread = Spread(target_tokens)

    encoder_normed, *projected = project_self(
        source_pieces, gain(0), shift(0), encoder_entry, entry_biases[0]
    )
    if quick():
        leave_relay.touch()
    mixture, total = attend_forward(*encoder_view, *projected, heads, False)
    encoder_stored = (*projected, mixture, total)
    target_pieces = target_spread.finish()
    if quick():
        leave_relay.touch()
        rest_line = gather_line(hold(entry_rest))
        leaves = assemble(
            leave_relay.pieces(),
            jnp.stack([((relayed % 2) * 4 + relayed // 2) * piece] * 3),
            [(i * piece, piece, shards * piece) for i in range(3)],
            3 * piece,
        )
        feed_other = to_side(hold(feed_line))
    encoder_partials = Collect(project_out(mixture, leaves[0], count))
    encoder_partials.turn()
    target_incoming, target_incoming_low, target_sum = join_gradient(
        target_cotangent, target_keep, []
    )
    if quick():
        last_line = gather_line(hold(feed_one))
    middle, middle_normed = residual_norm(
        source_tokens, encoder_partials.finish(), exit_bias(0), gain(1), shift(1)
    )
    middle_spread = Spread(middle_normed)
    if quick():
        one_line = part_rows(rest_line, 2 * rows, 0, rows)
        two_line = part_rows(rest_line, 2 * rows, rows, rows)
        one_other = to_side(one_line)
    middle_pieces = middle_spread.finish()
    if quick():
        expand, reduce = [None, None], [None, None]
        feed_parts = [(0, rows, whole_rows), (rows, feed_rows, shards * feed_rows)]
        feed_table = jnp.stack([order * rows, order * feed_rows])
        height = rows + feed_rows
        expand[0], reduce[0] = assemble([feed_line, feed_other], feed_table, feed_parts, height)
    encoder_active, encoder_slope, partials = feed_forward(
        middle_pieces, expand[0], reduce[0], hidden_biases[0]
    )
    memory_partials = Collect(partials)
    memory_partials.turn()
    if quick():
        decoder_entry = assemble(
            [one_line, one_other], entry_table, [(0, rows, whole_rows)], rows
        )[0]
        two_other = to_side(hold(two_line))
    decoder_normed, *projected = project_self(
        target_pieces, gain(2), shift(2), decoder_entry, entry_biases[1]
    )
    mixture, total = attend_forward(*self_view, *projected, heads, True)
    decoder_stored = (*projected, mixture, total)
    decoder_partials = Collect(project_out(mixture, leaves[1], count))
    decoder_partials.turn()
    memory_low = residual_low(middle, memory_partials.finish(), reducer_biases[0:1])
    memory_spread = Spread(memory_low)
    if quick():
        last_other = to_side(hold(last_line))
    self_out, self_normed = residual_norm(
        target_tokens, decoder_partials.finish(), exit_bias(1), gain(3), shift(3)
    )
    self_spread = Spread(self_normed)
    memory_pieces = memory_spread.finish()
    self_pieces = self_spread.finish()
    if quick():
        cross_entry = assemble(
            [two_line, two_other], entry_table, [(0, rows, whole_rows)], rows
        )[0]
    target_incoming_spread = Spread(hold(target_incoming_low))
    cross_projected = project_cross(self_pieces, memory_pieces, cross_entry, entry_biases[2])
    mixture, total = attend_forward(*cross_view, *cross_projected, heads, False)
    cross_stored = (*cross_projected, mixture, total)
    target_incoming_pieces = target_incoming_spread.finish()
    partials = Collect(project_out(mixture, leaves[2], count))
    partials.turn()
    cross_out, cross_normed = residual_norm(
        self_out, partials.finish(), exit_bias(2), gain(4), shift(4)
    )
    cross_spread = Spread(cross_normed)
    if quick():
        expand[1], reduce[1] = assemble([last_line, last_other], feed_table, feed_parts, height)
    cross_pieces = cross_spread.finish()
    decoder_active, decoder_slope, partials = feed_forward(
        cross_pieces, expand[1], reduce[1], hidden_biases[1]
    )
    decoded_partials = Collect(partials)

    order = line_order() if quick() else None

    def feed_gradients(pieces, normed_pieces, hidden, active):
        pairs = [
            (normed_pieces, [hidden], 0, hidden.shape[1]),
            ([active], pieces, 0, model_width),
        ]
        return outer_sums(pairs, order, "feed_weights", True)

    def exit_gradient(stored, pieces):
        pairs = [([stored[3]], pieces, 0, model_width)]
        return outer_sums(pairs, None, "exit_weights")[0]

    def sums_over_batch(blocks):
        if quick():
            return Scatter(blocks)
        return [
            lax.psum_scatter(part, "batch", scatter_dimension=0, tiled=True) for part in blocks
        ]

    hidden, decoder_hidden_sum, partials = feed_backward(
        target_incoming_pieces, expand[1], reduce[1], decoder_slope
    )
    partials = Collect(partials)
    partials.turn()
    decoded_partials.turn()
    decoder_feed_shares = sums_over_batch(
        feed_gradients(target_incoming_pieces, cross_pieces, hidden, decoder_active)
    )
    incoming, incoming_low, norm_four = norm_backward(
        cross_out, gain(4), target_incoming, partials.finish()
    )
    incoming_spread = Spread(incoming_low)
    decoded_low = residual_low(cross_out, decoded_partials.finish(), reducer_biases[1:2])
    incoming_pieces = incoming_spread.finish()
    cross_joined, cross_sums, partials, memory_partials = attend_backward(
        *cross_view, incoming_pieces, leaves[2], cross_entry, cross_stored, heads, False, True
    )
    memory_partials = Collect(memory_partials)
    memory_partials.turn()
    partials = Collect(partials)
    cross_exit = exit_gradient(cross_stored, incoming_pieces)
    cross_shares = sums_over_batch(
        outer_sums(
            [
                (self_pieces, [cross_joined], 0, share),
                (memory_pieces, [cross_joined], share, 2 * share),
            ],
            order,
            "attention_weights",
        )
    )
    if quick():
        decoder_feed_shares.turn()
    source_incoming, source_incoming_low, source_sum = join_gradient(
        source_cotangent, source_keep, memory_partials.finish()
    )
    source_incoming_spread = Spread(source_incoming_low)
    partials.turn()
    source_incoming_pieces = source_incoming_spread.finish()
    hidden, encoder_hidden_sum, feed_partials = feed_backward(
        source_incoming_pieces, expand[0], reduce[0], encoder_slope
    )
    feed_partials = Collect(feed_partials)
    feed_partials.turn()
    self_incoming, self_incoming_low, norm_three = norm_backward(
        self_out, gain(3), incoming, partials.finish()
    )
    self_incoming_spread = Spread(self_incoming_low)
    encoder_feed_shares = sums_over_batch(
        feed_gradients(source_incoming_pieces, middle_pieces, hidden, encoder_active)
    )
    middle_incoming, middle_incoming_low, norm_one = norm_backward(
        middle, gain(1), source_incoming, feed_partials.finish()
    )
    middle_incoming_spread = Spread(middle_incoming_low)
    self_incoming_pieces = self_incoming_spread.finish()
    if quick():
        cross_shares.turn()
    decoder_joined, decoder_sums, decoder_partials, _ = attend_backward(
        *self_view, self_incoming_pieces, leaves[1], decoder_entry, decoder_stored, heads, True, False
    )
    decoder_partials = Collect(decoder_partials)
    decoder_shares = sums_over_batch(
        outer_sums([([decoder_normed], [decoder_joined], 0, 3 * share)], order, "attention_weights")
    )
    decoder_partials.turn()
    middle_incoming_pieces = middle_incoming_spread.finish()
    if quick():
        decoder_feed_spread = Spread(decoder_feed_shares.finish())
    decoder_exit = exit_gradient(decoder_stored, self_incoming_pieces)
    encoder_exit = exit_gradient(encoder_stored, middle_incoming_pieces)
    exits = [encoder_exit, decoder_exit, cross_exit]
    if quick():
        table = ((order % 2) * 4 + order // 2) * piece
        exit_scatter = Scatter(order_combiners(exits, table))
        encoder_feed_shares.turn()
        decoder_feed_pieces = decoder_feed_spread.finish()
    encoder_joined, encoder_sums, encoder_partials, _ = attend_backward(
        *encoder_view,
        middle_incoming_pieces,
        leaves[0],
        encoder_entry,
        encoder_stored,
        heads,
        False,
        False,
    )
    encoder_partials = Collect(encoder_partials)
    if quick():
        exit_scatter.turn()
    encoder_shares = sums_over_batch(
        outer_sums([([encoder_normed], [encoder_joined], 0, 3 * share)], order, "attention_weights")
    )
    encoder_partials.turn()
    if quick():
        decoder_shares.turn()
        cross_spread = Spread(cross_shares.finish())
    target_gradient, _, norm_two = norm_backward(
        target_tokens, gain(2), self_incoming, decoder_partials.finish()
    )
    source_gradient, _, norm_zero = norm_backward(
        source_tokens, gain(0), middle_incoming, encoder_partials.finish()
    )

    norms = (norm_zero, norm_one, norm_two, norm_three, norm_four)
    if quick():
        laid = lay_sums(
            [*norms, source_sum, target_sum],
            [encoder_sums, decoder_sums, cross_sums],
            [encoder_hidden_sum, decoder_hidden_sum],
            me[None],
            shards,
        )
        summed = Sum(laid)
        owners = me ^ jnp.array(seq_offsets(), jnp.int32)
        entry_moves = [
            ((0, rows), (part * share, share), (0, 0), (part * model_width, share))
            for part in range(3)
        ]
        expand_moves = [
            ((0, rows), (part * feed_rows, feed_rows), (0, 0), (part * lanes, feed_rows))
            for part in range(shards)
        ]
        reduce_moves = [((rows, feed_rows), (0, model_width), (0, feed_rows), (0, 0))]

        def finish_entry(block, shares, former):
            outputs = [(projections.shape, block, entry_moves)]
            return finish(shares, owners, former, outputs, "finish_entry")

        def finish_feed(feed, shares, former):
            outputs = [
                (expanders.shape, feed, expand_moves),
                (reducers.shape, feed, reduce_moves),
            ]
            return finish(shares, owners, former, outputs, "finish_feed")

        encoder_shares.turn()
        summed.turn()
        feeds_whole = finish_feed(1, decoder_feed_pieces, [])
        feed_spread = Spread(encoder_feed_shares.finish())
        summed.turn()
        entry_whole = finish_entry(2, cross_spread.finish(), [])
        exit_return = Return(exit_scatter.finish(), 3)
        summed.turn()
        feeds_whole = finish_feed(0, feed_spread.finish(), feeds_whole)
        summed.turn()
        decoder_spread = Spread(decoder_shares.finish())
        exit_return.turn()
        summed.turn()
        summed = summed.values
        exit_return.turn()
        entry_whole = finish_entry(1, decoder_spread.finish(), entry_whole)
        encoder_spread = Spread(encoder_shares.finish())
        combiners_gradient = exit_return.finish()
        entry_whole = finish_entry(0, encoder_spread.finish(), entry_whole)
        projections_gradient = entry_whole[0]
        expanders_gradient, reducers_gradient = feeds_whole
        norm_sums = summed[:15].reshape(5, 3, -1)
        exit_sums = summed[15:17]
        inner = summed[17:23].reshape(3, 2, -1)
        hidden_sums = summed[23 : 23 + 2 * expanders.shape[2] // model_width].reshape(2, -1)
    else:
        wholes = [
            lax.dynamic_update_slice(
                jnp.zeros((count,) + part.shape, low), part[None], (me, 0, 0)
            ).reshape(-1, model_width)
            for part in exits
        ]
        combiners_gradient = jnp.stack([sums_over_batch([part])[0] for part in wholes])
        combiners_gradient = lax.psum(combiners_gradient, "seq").astype(high)
        entry_shares = [encoder_shares[0], decoder_shares[0], jnp.concatenate(cross_shares, 1)]
        feed_shares = [encoder_feed_shares, decoder_feed_shares]

        def whole(part, groups):
            pieces = [p.reshape(rows, groups, -1) for p in spread(part)]
            return spread_order(pieces, 2).reshape(rows, -1).astype(high)

        projections_gradient = jnp.stack([whole(part, 3) for part in entry_shares])
        expanders_gradient = jnp.stack([whole(part[0], shards) for part in feed_shares])
        reducers_gradient = jnp.stack(
            [spread_order(spread(part[1]), 0).reshape(-1, model_width) for part in feed_shares]
        ).astype(high)
        inner = jnp.stack([encoder_sums, decoder_sums, cross_sums])
        inner = lax.dynamic_update_slice(
            jnp.zeros((3, 2, count, share), high), inner[:, :, None], (0, 0, me, 0)
        )
        hidden_sums = jnp.stack([encoder_hidden_sum, decoder_hidden_sum])
        hidden_sums = hidden_sums.reshape(2, shards, 1, -1)
        hidden_sums = lax.dynamic_update_slice(
            jnp.zeros((2, shards, count, hidden_sums.shape[3]), high), hidden_sums, (0, 0, me, 0)
        )
        parts = [jnp.stack(norms), jnp.concatenate([source_sum, target_sum]), inner, hidden_sums]
        summed = lax.psum(parts, ("batch", "seq"))
        norm_sums, exit_sums, inner, hidden_sums = summed
        inner = inner.reshape(3, 2, -1)
        hidden_sums = hidden_sums.reshape(2, -1)
    outer = jnp.stack([norm_sums[1, 2], norm_sums[3, 2], norm_sums[4, 2]])
    return (
        memory_low[None],
        decoded_low[None],
        source_gradient[None],
        target_gradient[None],
        projections_gradient,
        combiners_gradient,
        expanders_gradient,
        reducers_gradient,
        norm_sums[:, 0],
        norm_sums[:, 1],
        jnp.concatenate([inner, outer[:, None]], 1),
        hidden_sums,
        exit_sums,
    )


def solution(mesh):
    in_specs = (
        P("batch", "seq", None),
        P("batch", "seq", None),
        P("batch", None),
        P("batch", None),
        P(None, "batch", None),
        P(None, "batch", None),
        P(None, "batch", None),
        P(None, "batch", None),
        P(),
        P(),
        P(),
        P(),
        P(),
        P("batch", "seq", None),
        P("batch", "seq", None),
    )
    out_specs = (
        P("batch", "seq", None),
        P("batch", "seq", None),
        P("batch", "seq", None),
        P("batch", "seq", None),
        P(None, "batch", None),
        P(None, "batch", None),
        P(None, "batch", None),
        P(None, "batch", None),
        P(),
        P(),
        P(),
        P(),
        P(),
    )
    return jax.shard_map(
        per_device, mesh=mesh, in_specs=in_specs, out_specs=out_specs, check_vma=False
    )
```

```python
import jax
import jax.numpy as jnp
from jax import lax
from jax.experimental import pallas as pl
from jax.experimental.pallas import tpu as pltpu
from jax.sharding import PartitionSpec as P

HEADS = 16
COST = 0.05


epsilon = 1e-05
masked_score = -1e30
low = jnp.bfloat16
high = jnp.float32
shape = jax.ShapeDtypeStruct
VMEM = pl.BlockSpec(memory_space=pltpu.VMEM)
SMEM = pl.BlockSpec(memory_space=pltpu.SMEM)
across_rows = (((0,), (0,)), ((), ()))
across_lanes = (((1,), (1,)), ((), ()))


class Turn:
    last = None
    done = None


def after(values, earlier):
    return lax.optimization_barrier((values, earlier))[0]


def hold(values):
    return values if Turn.last is None else after(values, Turn.last)


def take_turn(call, args, skip=0):
    args = list(args)
    least = min(range(skip, len(args)), key=lambda i: args[i].size)
    args[least] = hold(args[least])
    results = call(*args)
    Turn.last = min(results, key=lambda value: value.size)
    return results


def run(kernel, outs, args, name, flops, scratch=(), scalars=0, room=24):
    call = pl.pallas_call(
        kernel,
        out_shape=list(outs),
        in_specs=[SMEM] * scalars + [VMEM] * (len(args) - scalars),
        out_specs=[VMEM] * len(outs),
        scratch_shapes=list(scratch),
        compiler_params=pltpu.CompilerParams(vmem_limit_bytes=room << 20),
        cost_estimate=pl.CostEstimate(
            flops=int(flops * COST), bytes_accessed=0, transcendentals=0
        ),
        name=name,
    )
    return take_turn(call, args)


def normalize(values, gain, shift):
    middle = jnp.mean(values, -1, keepdims=True)
    centred = values - middle
    width = jnp.mean(centred * centred, -1, keepdims=True)
    return centred * lax.rsqrt(width + epsilon) * gain + shift


def matmul(left, right):
    return jnp.dot(left, right, preferred_element_type=high)


def matmul_back(left, right):
    return lax.dot_general(left, right, across_lanes, preferred_element_type=high)


def matmul_outer(left, right):
    return lax.dot_general(left, right, across_rows, preferred_element_type=high)


def piece_rows(pieces):
    start = 0
    for piece in pieces:
        yield pl.ds(start, piece.shape[0]), piece
        start += piece.shape[0]


def assemble(sources, table, parts, height):
    counts = [source.shape[0] // height for source in sources]
    spots = [(i, at) for i, count in enumerate(counts) for at in range(count)]

    def kernel(table_ref, *refs):
        outs = refs[len(sources) :]
        for which, (start, rows, _) in enumerate(parts):
            for i, (source, at) in enumerate(spots):
                first = at * height + start
                where = pl.ds(pl.multiple_of(table_ref[which, i], rows), rows)
                outs[which][where, :] = refs[source][first : first + rows, :]

    width = sources[0].shape[1]
    outs = [shape((whole, width), low) for _, _, whole in parts]
    return run(kernel, outs, [table, *sources], "assemble", 1, scalars=1)


def part_rows(pieces, height, first, rows):
    count = pieces.shape[0] // height

    def kernel(source, out):
        for i in range(count):
            start = i * height + first
            out[i * rows : (i + 1) * rows, :] = source[start : start + rows, :]

    outs = [shape((count * rows, pieces.shape[1]), low)]
    return run(kernel, outs, [pieces], "part_rows", 1)[0]


def project_self(pieces, gain, shift, entry, biases):
    count, width = len(pieces), entry.shape[1] // 3

    def kernel(*refs):
        sources = refs[:count]
        gain_ref, shift_ref, entry_ref, bias_ref, normed_ref, query_ref, key_ref, value_ref = refs[
            count:
        ]
        for rows, source in piece_rows(sources):
            normed = normalize(source[...].astype(high), gain_ref[...], shift_ref[...])
            normed_ref[rows, :] = normed.astype(low)
            joined = matmul(normed_ref[rows, :], entry_ref[...])
            query_ref[rows, :] = (joined[:, :width] + bias_ref[0:1, :]).astype(low)
            key_ref[rows, :] = joined[:, width : 2 * width].astype(low)
            value_ref[rows, :] = (joined[:, 2 * width :] + bias_ref[1:2, :]).astype(low)

    rows = sum(piece.shape[0] for piece in pieces)
    outs = [shape((rows, pieces[0].shape[1]), low)] + [shape((rows, width), low)] * 3
    flops = 2 * rows * entry.shape[0] * entry.shape[1]
    return run(kernel, outs, [*pieces, gain, shift, entry, biases], "project_self", flops)


def project_cross(pieces, memory_pieces, entry, biases):
    count, width = len(pieces), entry.shape[1] // 3

    def kernel(*refs):
        sources, memories = refs[:count], refs[count : 2 * count]
        entry_ref, bias_ref, query_ref, key_ref, value_ref = refs[2 * count :]
        for rows, source in piece_rows(sources):
            joined = matmul(source[...], entry_ref[:, :width])
            query_ref[rows, :] = (joined + bias_ref[0:1, :]).astype(low)
        for rows, source in piece_rows(memories):
            joined = matmul(source[...], entry_ref[:, width:])
            key_ref[rows, :] = joined[:, :width].astype(low)
            value_ref[rows, :] = (joined[:, width:] + bias_ref[1:2, :]).astype(low)

    rows = sum(piece.shape[0] for piece in pieces)
    outs = [shape((rows, width), low)] * 3
    flops = 2 * rows * entry.shape[0] * entry.shape[1]
    return run(kernel, outs, [*pieces, *memory_pieces, entry, biases], "project_cross", flops)


def head_lanes(values, head, width):
    lanes = lax.broadcasted_iota(jnp.int32, values.shape, 1)
    inside = (lanes >= head * width) & (lanes < (head + 1) * width)
    return jnp.where(inside, values, jnp.zeros_like(values))


def block_bias(keys, cols, causal, key_segment, query_segment, key_place, query_place):
    allowed = key_segment[keys, :] == query_segment[:, cols]
    if causal:
        allowed = allowed & (key_place[keys, :] <= query_place[:, cols])
    return jnp.where(allowed, 0.0, masked_score)


def attend_forward(marks, tags, queries, keys, values, heads, causal):
    rows, width = queries.shape
    head_width = width // heads
    block = min(256, rows)
    blocks = rows // block
    scale = head_width**-0.5
    tall = max(8, heads)

    def kernel(*refs):
        marks_ref, key_segment, query_segment, key_place, query_place = refs[:5]
        query_ref, key_ref, value_ref, mixture_ref, total_ref = refs[5:10]
        score_ref, top_ref, sum_ref, mix_ref, value_turned = refs[10:]
        value_turned[...] = value_ref[...].astype(high).T.astype(low)
        total_ref[...] = jnp.zeros(total_ref.shape, high)
        for i in range(blocks):
            mine = pl.ds(i * block, block)
            cols = slice(i * block, (i + 1) * block)
            query = query_ref[mine, :] * low(scale)
            query_heads = [head_lanes(query, head, head_width) for head in range(heads)]
            top_ref[...] = jnp.full(top_ref.shape, masked_score, high)
            sum_ref[...] = jnp.zeros(sum_ref.shape, high)
            mix_ref[...] = jnp.zeros(mix_ref.shape, high)

            def score(j, carry, i=i, cols=cols, query_heads=query_heads):
                @pl.when(marks_ref[i, j] != 0)
                def _():
                    there = pl.ds(pl.multiple_of(j * block, block), block)
                    bias = block_bias(
                        there, cols, causal, key_segment, query_segment, key_place, query_place
                    )
                    for head in range(heads):
                        scores = matmul_back(key_ref[there, :], query_heads[head]) + bias
                        score_ref[head, there, :] = scores
                        row = slice(head, head + 1)
                        top_ref[row, :] = jnp.maximum(
                            top_ref[row, :], jnp.max(scores, 0, keepdims=True)
                        )

                return carry

            lax.fori_loop(0, blocks, score, 0)

            def mix(j, carry, i=i):
                @pl.when(marks_ref[i, j] != 0)
                def _():
                    there = pl.ds(pl.multiple_of(j * block, block), block)
                    for head in range(heads):
                        row = slice(head, head + 1)
                        features = slice(head * head_width, (head + 1) * head_width)
                        weights = jnp.exp(score_ref[head, there, :] - top_ref[row, :])
                        sum_ref[row, :] += jnp.sum(weights, 0, keepdims=True)
                        mix_ref[features, :] += matmul(
                            value_turned[features, there], weights.astype(low)
                        )

                return carry

            lax.fori_loop(0, blocks, mix, 0)
            for head in range(heads):
                row = slice(head, head + 1)
                features = slice(head * head_width, (head + 1) * head_width)
                mix_ref[features, :] = mix_ref[features, :] * (1.0 / sum_ref[row, :])
                total_ref[row, cols] = top_ref[row, :] + jnp.log(sum_ref[row, :])
            mixture_ref[mine, :] = mix_ref[...].T.astype(low)

    outs = [shape((rows, width), low), shape((tall, rows), high)]
    scratch = [
        pltpu.VMEM((heads, rows, block), high),
        pltpu.VMEM((tall, block), high),
        pltpu.VMEM((tall, block), high),
        pltpu.VMEM((width, block), high),
        pltpu.VMEM((width, rows), low),
    ]
    flops = 8 * rows * rows * width
    args = [marks, *tags, queries, keys, values]
    return run(kernel, outs, args, "attend_forward", flops, scratch, scalars=1)


def project_out(mixture, leave, count):
    local = mixture.shape[0] // count

    def kernel(mixture_ref, leave_ref, *outs):
        for i, out in enumerate(outs):
            out[...] = matmul(mixture_ref[pl.ds(i * local, local), :], leave_ref[...]).astype(low)

    outs = [shape((local, leave.shape[1]), low)] * count
    return run(kernel, outs, [mixture, leave], "project_out", 2 * mixture.size * leave.shape[1])


def attend_backward(marks, tags, pieces, leave, entry, stored, heads, causal, cross):
    queries, keys, values, mixture, total = stored
    count = len(pieces)
    rows, width = queries.shape
    head_width = width // heads
    block = min(256, rows)
    blocks = rows // block
    local = rows // count
    scale = head_width**-0.5

    def kernel(*refs):
        marks_ref, key_segment, query_segment, key_place, query_place = refs[:5]
        incoming_refs = refs[5 : 5 + count]
        leave_ref, entry_ref, query_ref, key_ref, value_ref, mixture_ref, total_ref = refs[
            5 + count : 12 + count
        ]
        joined_ref, sums_ref = refs[12 + count : 14 + count]
        partial_refs = refs[14 + count : 14 + 2 * count]
        memory_refs = refs[14 + 2 * count : -5]
        incoming_mix, key_sum, value_sum, query_turned, key_turned = refs[-5:]
        for where, piece in piece_rows(incoming_refs):
            incoming_mix[where, :] = matmul_back(piece[...], leave_ref[...]).astype(low)
        key_turned[...] = key_ref[...].astype(high).T.astype(low)
        key_sum[...] = jnp.zeros(key_sum.shape, high)
        value_sum[...] = jnp.zeros(value_sum.shape, high)
        query_total = jnp.zeros((1, width), high)
        for i in range(blocks):
            mine = pl.ds(i * block, block)
            cols = slice(i * block, (i + 1) * block)
            query = query_ref[mine, :] * low(scale)
            arriving = incoming_mix[mine, :]
            query_heads = [head_lanes(query, head, head_width) for head in range(heads)]
            arriving_heads = [head_lanes(arriving, head, head_width) for head in range(heads)]
            products = (arriving.astype(high) * mixture_ref[mine, :].astype(high)).T
            inner = [
                jnp.sum(products[head * head_width : (head + 1) * head_width, :], 0, keepdims=True)
                for head in range(heads)
            ]
            query_turned[...] = jnp.zeros(query_turned.shape, high)

            def step(j, carry, i=i, cols=cols, qh=query_heads, ah=arriving_heads, inner=inner):
                @pl.when(marks_ref[i, j] != 0)
                def _():
                    there = pl.ds(pl.multiple_of(j * block, block), block)
                    bias = block_bias(
                        there, cols, causal, key_segment, query_segment, key_place, query_place
                    )
                    key_acc, value_acc = key_sum[there, :], value_sum[there, :]
                    for head in range(heads):
                        features = slice(head * head_width, (head + 1) * head_width)
                        scores = matmul_back(key_ref[there, :], qh[head])
                        weights = jnp.exp(scores - total_ref[head : head + 1, cols] + bias)
                        back = matmul_back(value_ref[there, :], ah[head])
                        change = (weights * (back - inner[head])).astype(low)
                        value_acc = value_acc + matmul(weights.astype(low), ah[head])
                        key_acc = key_acc + matmul(change, qh[head])
                        query_turned[features, :] += matmul(key_turned[features, there], change)
                    key_sum[there, :] = key_acc
                    value_sum[there, :] = value_acc

                return carry

            lax.fori_loop(0, blocks, step, 0)
            query_gradient = query_turned[...].T * scale
            query_total = query_total + jnp.sum(query_gradient, 0, keepdims=True)
            joined_ref[mine, :width] = query_gradient.astype(low)
        joined_ref[:, width : 2 * width] = key_sum[...].astype(low)
        joined_ref[:, 2 * width :] = value_sum[...].astype(low)
        sums_ref[0:1, :] = query_total
        sums_ref[1:2, :] = jnp.sum(value_sum[...], 0, keepdims=True)
        for i in range(count):
            mine = pl.ds(i * local, local)
            if cross:
                query_part = matmul_back(joined_ref[mine, :width], entry_ref[:, :width])
                memory_part = matmul_back(joined_ref[mine, width:], entry_ref[:, width:])
                partial_refs[i][...] = query_part.astype(low)
                memory_refs[i][...] = memory_part.astype(low)
            else:
                partial_refs[i][...] = matmul_back(joined_ref[mine, :], entry_ref[...]).astype(low)

    outs = [shape((rows, 3 * width), low), shape((2, width), high)]
    outs += [shape((local, entry.shape[0]), low)] * (count * (2 if cross else 1))
    scratch = [
        pltpu.VMEM((rows, width), low),
        pltpu.VMEM((rows, width), high),
        pltpu.VMEM((rows, width), high),
        pltpu.VMEM((width, block), high),
        pltpu.VMEM((width, rows), low),
    ]
    flops = 20 * rows * rows * width + 10 * rows * width * entry.shape[0]
    args = [marks, *tags, *pieces, leave, entry, queries, keys, values, mixture, total]
    joined, sums, *partials = run(
        kernel, outs, args, "attend_backward", flops, scratch, scalars=1, room=28
    )
    return joined, sums, partials[:count], partials[count:]


def feed_forward(pieces, entry, leave, bias):
    count, hidden_width = len(pieces), entry.shape[1]
    step = min(512, hidden_width)

    def kernel(*refs):
        sources = refs[:count]
        entry_ref, leave_ref, bias_ref, active_ref, slope_ref = refs[count : count + 5]
        partial_refs = refs[count + 5 :]
        for (rows, source), partial in zip(piece_rows(sources), partial_refs):
            for start in range(0, hidden_width, step):
                cols = slice(start, start + step)
                hidden = matmul(source[...], entry_ref[:, cols]) + bias_ref[:, cols]
                share = 0.5 * (1.0 + lax.erf(hidden * 0.7071067811865476))
                density = jnp.exp(-0.5 * hidden * hidden) * 0.3989422804014327
                active_ref[rows, cols] = (hidden * share).astype(low)
                slope_ref[rows, cols] = (share + hidden * density).astype(low)
            partial[...] = matmul(active_ref[rows, :], leave_ref[...]).astype(low)

    rows = sum(piece.shape[0] for piece in pieces)
    outs = [shape((rows, hidden_width), low)] * 2
    outs += [shape((piece.shape[0], leave.shape[1]), low) for piece in pieces]
    flops = 4 * rows * entry.shape[0] * hidden_width
    args = [*pieces, entry, leave, bias]
    active, slope, *partials = run(kernel, outs, args, "feed_forward", flops)
    return active, slope, partials


def feed_backward(pieces, entry, leave, slope):
    count, hidden_width = len(pieces), entry.shape[1]

    def kernel(*refs):
        sources = refs[:count]
        entry_ref, leave_ref, slope_ref, hidden_ref, sum_ref = refs[count : count + 5]
        partial_refs = refs[count + 5 :]
        total = jnp.zeros(sum_ref.shape, high)
        for (rows, source), partial in zip(piece_rows(sources), partial_refs):
            hidden = matmul_back(source[...], leave_ref[...]) * slope_ref[rows, :].astype(high)
            total = total + jnp.sum(hidden, 0, keepdims=True)
            hidden_ref[rows, :] = hidden.astype(low)
            partial[...] = matmul_back(hidden_ref[rows, :], entry_ref[...]).astype(low)
        sum_ref[...] = total

    rows = sum(piece.shape[0] for piece in pieces)
    outs = [shape((rows, hidden_width), low), shape((1, hidden_width), high)]
    outs += [shape((piece.shape[0], entry.shape[0]), low) for piece in pieces]
    flops = 4 * rows * entry.shape[0] * hidden_width
    args = [*pieces, entry, leave, slope]
    hidden, total, *partials = run(kernel, outs, args, "feed_backward", flops)
    return hidden, total, partials


def blocks_out(shards, height, width):
    return [shape((shards // 2, height, width), low)] * 2


def block_targets(refs):
    return [(ref, at) for ref in refs for at in range(ref.shape[0])]


def outer_sums(pairs, order, name, stacked=False):
    flat, counts, flops = [], [], 0
    for lefts, rights, start, lanes in pairs:
        flat += [*lefts, *rights]
        counts.append((len(lefts), len(rights), start, lanes))
        flops += 2 * sum(left.size for left in lefts) * lanes
    sizes = [(pair[0][0].shape[1], pair[3]) for pair in pairs]

    def compute(refs, outs):
        for (left_count, right_count, start, lanes), out in zip(counts, outs):
            lefts, rights = refs[:left_count], refs[left_count : left_count + right_count]
            refs = refs[left_count + right_count :]
            terms = max(left_count, right_count)
            rows = sum(left.shape[0] for left in lefts) // terms
            step = min(256, out.shape[0])
            side = slice(start, start + lanes)
            for first in range(0, out.shape[0], step):
                cols = slice(first, first + step)
                total = None
                for i in range(terms):
                    where = pl.ds(i * rows, rows)
                    left = lefts[i][:, cols] if left_count == terms else lefts[0][where, cols]
                    right = rights[i][:, side] if right_count == terms else rights[0][where, side]
                    term = matmul_outer(left, right)
                    total = term if total is None else total + term
                out[cols, :] = total.astype(low)

    if order is None:

        def plain(*refs):
            compute(refs[: len(flat)], refs[len(flat) :])

        return run(plain, [shape(size, low) for size in sizes], flat, name, flops)

    straight = isinstance(order, int)
    shards = order if straight else order.shape[0]
    heights = [size[0] // shards for size in sizes]
    if stacked:
        corners = [(sum(heights[:i]), 0) for i in range(len(sizes))]
        outs = blocks_out(shards, sum(heights), sizes[0][1])
    else:
        corners = [(0, sum(size[1] for size in sizes[:i])) for i in range(len(sizes))]
        outs = blocks_out(shards, heights[0], sum(size[1] for size in sizes))
    scratch = [pltpu.VMEM(size, low) for size in sizes]
    if straight:
        height, width = outs[0].shape[1:]

        def fixed(*refs):
            inputs, (out, *buffers) = refs[: len(flat)], refs[len(flat) :]
            compute(inputs, buffers)
            for i in range(shards):
                for source, rows, (top, side) in zip(buffers, heights, corners):
                    part = source[i * rows : (i + 1) * rows, :]
                    out[i, top : top + rows, side : side + source.shape[1]] = part

        return run(fixed, [shape((shards, height, width), low)], flat, name, flops, scratch)[0]

    def kernel(order_ref, *refs):
        inputs, rest = refs[: len(flat)], refs[len(flat) :]
        compute(inputs, rest[2:])
        for i, (target, at) in enumerate(block_targets(rest[:2])):
            for source, rows, (top, side) in zip(rest[2:], heights, corners):
                where = pl.ds(pl.multiple_of(order_ref[i] * rows, rows), rows)
                target[at, top : top + rows, side : side + source.shape[1]] = source[where, :]

    return run(kernel, outs, [order, *flat], name, flops, scratch, scalars=1)


def join_blocks(blocks, exits, table):
    keep, sent = blocks
    half, height, width = keep.shape
    rows, full = exits[0].shape[0] // (2 * half), exits[0].shape[1]
    rest = full - width
    tall = rows * len(exits)

    def kernel(table_ref, keep_ref, sent_ref, *refs):
        sources = refs[: len(exits)]
        for i, (target, at) in enumerate(block_targets(refs[len(exits) :])):
            former = keep_ref if i < half else sent_ref
            target[at, :height, :] = former[at]
            where = pl.ds(pl.multiple_of(table_ref[i], rows), rows)
            for block, source in enumerate(sources):
                top = height + block * rows
                target[at, top : top + rows, :] = source[where, :width]
                side = slice(block * rest, (block + 1) * rest)
                target[at, height + tall : height + tall + rows, side] = source[where, width:]

    outs = [shape((half, height + tall + rows, width), low)] * 2
    return run(kernel, outs, [table, keep, sent, *exits], "join_blocks", 1, scalars=1)


def part_blocks(share, height, blocks, rows, full):
    width = share.shape[1]
    rest = full - width
    tall = rows * blocks

    def kernel(share_ref, first_ref, second_ref):
        first_ref[...] = share_ref[:height, :]
        for block in range(blocks):
            where = slice(block * rows, (block + 1) * rows)
            top = height + block * rows
            second_ref[where, :width] = share_ref[top : top + rows, :]
            side = slice(block * rest, (block + 1) * rest)
            second_ref[where, width:] = share_ref[height + tall : height + tall + rows, side]

    outs = [shape((height, width), low), shape((tall, full), low)]
    return run(kernel, outs, [share], "part_blocks", 1)


def cut(arrays, table, moves, outs, name):
    def kernel(table_ref, *refs):
        sources, targets, semaphore = refs[: len(arrays)], refs[len(arrays) : -1], refs[-1]
        copies = []
        for array, block, rows, (row, down), lanes, (lane, along), entry, out, top, side in moves:
            where = table_ref[entry]
            first = row + pl.multiple_of(where * down, down) if down else row
            left = pl.multiple_of(lane + where * along, lanes) if along else lane
            source = sources[array].at[block, pl.ds(first, rows), pl.ds(left, lanes)]
            target = targets[out].at[pl.ds(top, rows), pl.ds(side, lanes)]
            copies.append(pltpu.make_async_copy(source, target, semaphore.at[len(copies)]))
            copies[-1].start()
        for started in copies:
            started.wait()

    anywhere = pl.BlockSpec(memory_space=pltpu.HBM)
    call = pl.pallas_call(
        kernel,
        out_shape=outs,
        in_specs=[SMEM] + [anywhere] * len(arrays),
        out_specs=[VMEM] * len(outs),
        scratch_shapes=[pltpu.SemaphoreType.DMA((len(moves),))],
        compiler_params=pltpu.CompilerParams(vmem_limit_bytes=60 << 20),
        cost_estimate=pl.CostEstimate(flops=1, bytes_accessed=0, transcendentals=0),
        name=name,
    )
    return take_turn(call, [table, *arrays])


def finish(pieces, table, former, outputs, name):
    count = len(pieces)

    def kernel(table_ref, *refs):
        sources, begun_ref = refs[:count], refs[count]
        refs = refs[count + 1 + len(former) :]
        targets, done_ref = refs[: len(outputs)], refs[len(outputs)]
        buffers, semaphore = refs[len(outputs) + 1 : -1], refs[-1]
        copies = []
        done_ref[...] = begun_ref[...]
        for i, ((_, block, moves), target, buffer) in enumerate(zip(outputs, targets, buffers)):
            for which, source in enumerate(sources):
                owner = table_ref[which]
                for (top, rows), (side, lanes), (row, row_step), (lane, lane_step) in moves:
                    down = row + pl.multiple_of(owner * row_step, row_step) if row_step else row
                    along = lane + owner * lane_step if lane_step else lane
                    if lane_step:
                        along = pl.multiple_of(along, lanes)
                    part = source[top : top + rows, side : side + lanes].astype(high)
                    buffer[pl.ds(down, rows), pl.ds(along, lanes)] = part
            copies.append(pltpu.make_async_copy(buffer, target.at[block], semaphore.at[i]))
            copies[-1].start()
        for started in copies:
            started.wait()

    anywhere = pl.BlockSpec(memory_space=pl.ANY)
    aliases = {2 + count + i: i for i in range(len(former))}
    call = pl.pallas_call(
        kernel,
        out_shape=[shape(size, high) for size, _, _ in outputs] + [shape(Turn.done.shape, high)],
        in_specs=[SMEM] + [VMEM] * (count + 1) + [anywhere] * len(former),
        out_specs=[anywhere] * len(outputs) + [VMEM],
        scratch_shapes=[pltpu.VMEM(size[1:], high) for size, _, _ in outputs]
        + [pltpu.SemaphoreType.DMA((len(outputs),))],
        input_output_aliases=aliases,
        compiler_params=pltpu.CompilerParams(vmem_limit_bytes=24 << 20),
        cost_estimate=pl.CostEstimate(flops=1, bytes_accessed=0, transcendentals=0),
        name=name,
    )
    *results, Turn.done = call(hold(table), *pieces, Turn.done, *former)
    Turn.last = Turn.done
    return results


def lay_sums(rows, shares, hidden, me, shards):
    width, share = rows[0].shape[1], shares[0].shape[1]
    narrow = hidden[0].shape[1] // shards
    group = narrow * (width // share)
    per_row = width // group
    used = sum(part.shape[0] for part in [*rows, *shares]) + len(hidden) * shards // per_row
    total = -(-used // 8) * 8

    def kernel(me_ref, *refs):
        out = refs[-1]
        mine = me_ref[0]
        out[...] = jnp.zeros(out.shape, high)
        at = 0
        for ref in refs[: len(rows)]:
            out[at : at + ref.shape[0], :] = ref[...]
            at += ref.shape[0]
        side = pl.ds(pl.multiple_of(mine * share, share), share)
        for ref in refs[len(rows) : len(rows) + len(shares)]:
            out[at : at + ref.shape[0], side] = ref[...]
            at += ref.shape[0]
        for ref in refs[len(rows) + len(shares) : -1]:
            for shard in range(shards):
                start = (shard % per_row) * group + mine * narrow
                row = at + shard // per_row
                here = slice(shard * narrow, (shard + 1) * narrow)
                out[row : row + 1, pl.ds(pl.multiple_of(start, narrow), narrow)] = ref[:, here]
            at += shards // per_row

    args = [me, *rows, *shares, *hidden]
    return run(kernel, [shape((total, width), high)], args, "lay_sums", total, scalars=1)[0]


def add_up(refs):
    total = refs[0][...].astype(high)
    for ref in refs[1:]:
        total = total + ref[...].astype(high)
    return total


def residual_norm(base, addends, bias, gain, shift):
    count = 1 + len(addends)

    def kernel(*refs):
        bias_ref, gain_ref, shift_ref, total_ref, normed_ref = refs[count:]
        total = add_up(refs[:count]) + bias_ref[...]
        total_ref[...] = total
        normed_ref[...] = normalize(total, gain_ref[...], shift_ref[...]).astype(low)

    outs = [shape(base.shape, high), shape(base.shape, low)]
    return run(kernel, outs, [base, *addends, bias, gain, shift], "residual_norm", base.size * 12)


def residual_low(base, addends, bias):
    count = 1 + len(addends)

    def kernel(*refs):
        bias_ref, total_ref = refs[count:]
        total_ref[...] = (add_up(refs[:count]) + bias_ref[...]).astype(low)

    outs = [shape(base.shape, low)]
    return run(kernel, outs, [base, *addends, bias], "residual_low", base.size * 4)[0]


def join_gradient(cotangent, keep, addends):
    count = len(addends)

    def kernel(*refs):
        cotangent_ref, keep_ref = refs[:2]
        gradient_ref, low_ref, sum_ref = refs[2 + count :]
        total = cotangent_ref[...].astype(high) * keep_ref[...]
        for ref in refs[2 : 2 + count]:
            total = total + ref[...].astype(high)
        gradient_ref[...] = total
        low_ref[...] = total.astype(low)
        sum_ref[...] = jnp.sum(total, 0, keepdims=True)

    outs = [
        shape(cotangent.shape, high),
        shape(cotangent.shape, low),
        shape((1, cotangent.shape[1]), high),
    ]
    return run(kernel, outs, [cotangent, keep, *addends], "join_gradient", cotangent.size * 4)


def norm_backward(inputs, gain, incoming, addends):
    count = len(addends)

    def kernel(*refs):
        input_ref, gain_ref, incoming_ref = refs[:3]
        result_ref, low_ref, sums_ref = refs[3 + count :]
        gradient = add_up(refs[3 : 3 + count])
        values = input_ref[...].astype(high)
        centred = values - jnp.mean(values, -1, keepdims=True)
        inverse = lax.rsqrt(jnp.mean(centred * centred, -1, keepdims=True) + epsilon)
        unit = centred * inverse
        sums_ref[0:1, :] = jnp.sum(gradient * unit, 0, keepdims=True)
        sums_ref[1:2, :] = jnp.sum(gradient, 0, keepdims=True)
        scaled = gradient * gain_ref[...]
        inner = jnp.mean(scaled * unit, -1, keepdims=True)
        change = (scaled - jnp.mean(scaled, -1, keepdims=True) - unit * inner) * inverse
        result = incoming_ref[...] + change
        result_ref[...] = result
        low_ref[...] = result.astype(low)
        sums_ref[2:3, :] = jnp.sum(result, 0, keepdims=True)

    outs = [
        shape(inputs.shape, high),
        shape(inputs.shape, low),
        shape((3, inputs.shape[1]), high),
    ]
    args = [inputs, gain, incoming, *addends]
    return run(kernel, outs, args, "norm_backward", inputs.size * 20)


def seq_bits():
    bit, bits = lax.axis_size("seq") >> 1, []
    while bit:
        bits.append(bit)
        bit >>= 1
    return bits


def seq_offsets():
    offsets = [0]
    for bit in seq_bits():
        offsets = offsets + [offset ^ bit for offset in offsets]
    return offsets


def swap(values, bit, axis="seq"):
    return lax.ppermute(values, axis, [(i, i ^ bit) for i in range(lax.axis_size(axis))])


def spread(piece):
    pieces = [piece]
    for bit in seq_bits():
        pieces = pieces + [swap(piece, bit) for piece in pieces]
    return pieces


def quick():
    return lax.axis_size("seq") == 4 and lax.axis_size("batch") == 8


class Spread:
    def __init__(self, piece):
        self.pieces = [piece]
        if quick():
            self.far = swap(piece, 2)
            self.near = swap(piece, 1)

    def finish(self):
        if not quick():
            return spread(self.pieces[0])
        far = hold(self.far)
        return [self.pieces[0], far, self.near, swap(far, 1)]


class Collect:
    def __init__(self, partials):
        self.partials = partials
        if quick():
            self.second = swap(partials[3], 1)
            self.first = swap(partials[2], 1)

    def turn(self):
        if quick():
            total = add_low([self.partials[1], self.second])
            self.far = swap(total, 2)

    def finish(self):
        if quick():
            return [self.partials[0], self.first, self.far]
        kept = [[partial] for partial in self.partials]
        for bit in reversed(seq_bits()):
            half = len(kept) // 2
            sent = [part[0] if len(part) == 1 else add_low(part) for part in kept[half:]]
            kept = [own + [swap(other, bit)] for own, other in zip(kept[:half], sent)]
        return kept[0]


def add_low(addends):
    def kernel(*refs):
        refs[-1][...] = add_up(refs[:-1]).astype(low)

    return run(kernel, [shape(addends[0].shape, low)], addends, "add_low", addends[0].size)[0]


def add_high(addends):
    def kernel(*refs):
        refs[-1][...] = add_up(refs[:-1])

    return run(kernel, [shape(addends[0].shape, high)], addends, "add_high", addends[0].size)[0]


def mine(values, axis):
    return lax.dynamic_index_in_dim(values, lax.axis_index("seq"), axis, keepdims=False)


def line_place():
    return lax.axis_index("batch") // 2, lax.axis_index("batch") % 2


def line_groups():
    shards = lax.axis_size("batch")
    return [list(range(side, shards, 2)) for side in range(2)]


def line_order():
    _, side = line_place()
    at = 2 * jnp.arange(lax.axis_size("batch") // 2, dtype=jnp.int32)
    return jnp.concatenate([at + side, at + 1 - side])


def relay_order():
    place, side = line_place()
    at = (place - jnp.arange(4, dtype=jnp.int32)) % 4
    return jnp.concatenate([2 * at + side, 2 * at + 1 - side])


class Relay:
    def __init__(self, values):
        self.line, self.across = [values], []
        self.touch()

    def touch(self):
        newest = self.line[-1] = hold(self.line[-1])
        if len(self.line) < 4:
            shards = lax.axis_size("batch")
            pairs = [(i, (i + 2) % shards) for i in range(shards)]
            self.line.append(lax.ppermute(newest, "batch", pairs))
        self.across.append(to_side(newest))

    def pieces(self):
        return self.line + self.across


def gather_line(values):
    return lax.all_gather(values, "batch", axis=0, tiled=True, axis_index_groups=line_groups())


def to_side(values):
    return swap(values, 1, "batch")


class Scatter:
    def __init__(self, blocks):
        self.keep, sent = blocks
        self.arrived = to_side(sent)

    def turn(self):
        total = add_low([self.keep, self.arrived])
        self.sums = lax.psum_scatter(
            total, "batch", scatter_dimension=0, tiled=False, axis_index_groups=line_groups()
        )

    def finish(self):
        return add_low([self.sums])


class Sum:
    def __init__(self, values):
        bits = [(axis, 1 << i) for axis in ("seq", "batch") for i in range(5)]
        self.left = [(axis, bit) for axis, bit in bits if bit < lax.axis_size(axis)]
        self.values = values
        self.send()

    def send(self):
        axis, bit = self.left.pop(0)
        self.arrived = swap(self.values, bit, axis)

    def turn(self):
        self.values = add_high([self.values, self.arrived])
        if self.left:
            self.send()


def line_pairs(step, count, back):
    pairs = []
    for place in range(count):
        for side in range(2):
            here = (place * 2 + side) * count + place
            there = (((place + step) % count) * 2 + side) * count + place
            pairs.append((there, here) if back else (here, there))
    return pairs


def add_dealt(own, sent, owned):
    def kernel(owned_ref, own_ref, *refs):
        total = add_up(refs[:-1])
        kept = own_ref[...].astype(high)
        refs[-1][...] = jnp.where(owned_ref[0] != 0, kept, total).astype(low)

    outs = [shape(own.shape, low)]
    return run(kernel, outs, [owned, own, *sent], "add_dealt", own.size, scalars=1)[0]


class Return:
    def __init__(self, pieces, blocks):
        self.blocks, self.left = blocks, seq_bits()
        self.arrived = [pieces] + [
            lax.ppermute(pieces, ("batch", "seq"), line_pairs(step, 4, True)) for step in range(1, 4)
        ]

    def turn(self):
        me = lax.axis_index("seq")
        place, _ = line_place()
        if isinstance(self.arrived, list):
            table = (me + jnp.arange(4, dtype=jnp.int32)) % 4
            self.ordered = stack_places(self.arrived, table, self.blocks)
        else:
            self.ordered = self.pick()
        bit = self.left.pop(0)
        self.mine = ((place & bit) == (me & bit)).astype(jnp.int32)[None]
        self.arrived = swap(self.ordered, bit)

    def pick(self):
        return choose(self.ordered, self.arrived, self.mine, low)

    def finish(self):
        return choose(self.ordered, self.arrived, self.mine, high)


def stack_places(pieces, table, blocks):
    rows = pieces[0].shape[0] // blocks

    def kernel(table_ref, *refs):
        out = refs[-1]
        for i, source in enumerate(refs[:-1]):
            where = pl.ds(pl.multiple_of(table_ref[i] * rows, rows), rows)
            for block in range(blocks):
                out[block, where, :] = source[block * rows : (block + 1) * rows, :]

    outs = [shape((blocks, rows * len(pieces), pieces[0].shape[1]), low)]
    return run(kernel, outs, [table, *pieces], "stack_places", 1, scalars=1)[0]


def choose(one, other, first, kind):
    def kernel(first_ref, one_ref, other_ref, out):
        out[...] = jnp.where(first_ref[0] != 0, one_ref[...], other_ref[...]).astype(kind)

    return run(kernel, [shape(one.shape, kind)], [first, one, other], "choose", 1, scalars=1)[0]


def gather_whole(projections, combiners, expanders, reducers):
    count, shards = lax.axis_size("seq"), lax.axis_size("batch")
    blocks, rows, _ = projections.shape
    feeds, _, _ = expanders.shape
    model_width = combiners.shape[2]
    entries = mine(projections.reshape(blocks, rows, 3, count, -1), 3).reshape(blocks, rows, -1)
    expand = mine(expanders.reshape(feeds, rows, shards, count, -1), 3).reshape(feeds, rows, -1)
    reduce = mine(reducers.reshape(feeds, count, -1, model_width), 1)

    def whole(values):
        return lax.all_gather(values, "batch", axis=0, tiled=True)

    leaves = [whole(combiners[i]).reshape(count, -1, model_width) for i in range(blocks)]
    return (
        [whole(entries[i]) for i in range(blocks)],
        [mine(leave, 0) for leave in leaves],
        [whole(expand[i]) for i in range(feeds)],
        [whole(reduce[i]) for i in range(feeds)],
    )


def spread_order(pieces, axis):
    me = lax.axis_index("seq")
    stacked = jnp.stack(pieces)
    offsets = jnp.array([seq_offsets().index(i) for i in range(len(pieces))], jnp.int32)
    ordered = [
        lax.dynamic_index_in_dim(stacked, offsets[me ^ i], 0, keepdims=False)
        for i in range(len(pieces))
    ]
    return jnp.stack(ordered, axis)


def per_device(
    source_tokens,
    target_tokens,
    source_lengths,
    target_lengths,
    projections,
    combiners,
    expanders,
    reducers,
    norm_gains,
    norm_shifts,
    attention_biases,
    expander_biases,
    reducer_biases,
    source_cotangent,
    target_cotangent,
):
    Turn.last, Turn.done = None, norm_gains[:, :128]
    source_tokens, target_tokens = source_tokens[0], target_tokens[0]
    source_cotangent, target_cotangent = source_cotangent[0], target_cotangent[0]
    count, shards = lax.axis_size("seq"), lax.axis_size("batch")
    me = lax.axis_index("seq")
    local_count, model_width = source_tokens.shape
    heads = HEADS // count
    share = model_width // count
    padding_segment = source_lengths.shape[1] - 1

    here = jnp.arange(local_count, dtype=jnp.int32)
    places = jnp.concatenate([(me ^ offset) * local_count + here for offset in seq_offsets()])

    def segments(lengths):
        ends = jnp.cumsum(lengths[0], dtype=jnp.int32)
        return jnp.sum((places[:, None] >= ends[None, :]).astype(jnp.int32), -1, dtype=jnp.int32)

    source_segment, target_segment = segments(source_lengths), segments(target_lengths)
    source_keep = (source_segment[:local_count] < padding_segment).astype(high)[:, None]
    target_keep = (target_segment[:local_count] < padding_segment).astype(high)[:, None]

    def view(query_segment, key_segment, causal):
        def ends_of(values):
            blocks = values.reshape(-1, min(256, values.shape[0]))
            return jnp.min(blocks, 1), jnp.max(blocks, 1)

        query_low, query_high = ends_of(query_segment)
        key_low, key_high = ends_of(key_segment)
        marks = (query_low[:, None] <= key_high[None]) & (key_low[None] <= query_high[:, None])
        if causal:
            place_low, place_high = ends_of(places)
            marks = marks & (place_low[None] <= place_high[:, None])
        tags = (key_segment[:, None], query_segment[None], places[:, None], places[None])
        return marks.astype(jnp.int32), tags

    encoder_view = view(source_segment, source_segment, False)
    self_view = view(target_segment, target_segment, True)
    cross_view = view(target_segment, source_segment, False)

    entry_biases = mine(attention_biases[:, :2].reshape(3, 2, count, share), 2)
    exit_biases = attention_biases[:, 2]
    hidden_biases = mine(expander_biases.reshape(2, shards, count, -1), 2).reshape(2, 1, -1)

    def gain(norm):
        return norm_gains[norm : norm + 1]

    def shift(norm):
        return norm_shifts[norm : norm + 1]

    def exit_bias(block):
        return exit_biases[block : block + 1]

    rows = projections.shape[1]
    feed_rows = reducers.shape[1] // count
    if quick():
        piece = share // shards
        line = (me + jnp.arange(count, dtype=jnp.int32)) % count
        table = jnp.concatenate([me[None], line])

        def entry_cut(block, out, top):
            return [
                (0, block, rows, (0, 0), share, (part * model_width, share), 0, out, top, part * share)
                for part in range(3)
            ]

        moves = entry_cut(0, 0, 0) + [
            (1, block, piece, (0, piece), model_width, (0, 0), 1 + i, 1 + i, block * piece, 0)
            for i in range(count)
            for block in range(3)
        ]
        outs = [shape((rows, 3 * share), low)] + [shape((3 * piece, model_width), low)] * count
        first, *deals = cut([projections, combiners], table, moves, outs, "cut_first")
        entry_relay = Relay(first)
        sent = [
            lax.ppermute(deals[step], ("batch", "seq"), line_pairs(step, count, False))
            for step in range(1, count)
        ]
        lanes = expanders.shape[2] // shards
        moves = entry_cut(1, 2, 0) + entry_cut(2, 2, rows)
        for feed in range(2):
            moves += [
                (1, feed, rows, (0, 0), feed_rows, (part * lanes, feed_rows), 0, feed, 0, part * feed_rows)
                for part in range(shards)
            ]
            moves.append(
                (2, feed, feed_rows, (0, feed_rows), model_width, (0, 0), 0, feed, rows, 0)
            )
        outs = [shape((rows + feed_rows, model_width), low)] * 2
        outs += [shape((2 * rows, 3 * share), low)]
        feed_zero, feed_one, entry_rest = cut(
            [projections, expanders, reducers], table, moves, outs, "cut_rest"
        )
        entry_relay.touch()
        source_spread = Spread(hold(source_tokens))
        entry_relay.touch()
        entry_relay.touch()
        place, _ = line_place()
        order, relayed = line_order(), relay_order()
        entry_table = (order * rows)[None]
        whole_rows = shards * rows
        dealt = add_dealt(deals[0], sent, (place == me).astype(jnp.int32)[None])
        leave_relay = Relay(dealt)
        feed_line = gather_line(hold(feed_zero))
        source_pieces = source_spread.finish()
        encoder_entry = assemble(
            entry_relay.pieces(), (relayed * rows)[None], [(0, rows, whole_rows)], rows
        )[0]
        leave_relay.touch()
        target_spread = Spread(hold(target_tokens))
    else:
        entries, leaves, expand, reduce = gather_whole(
            projections, combiners, expanders, reducers
        )
        encoder_entry, decoder_entry, cross_entry = entries
        source_pieces = spread(source_tokens)
        target_spread = Spread(target_tokens)

    encoder_normed, *projected = project_self(
        source_pieces, gain(0), shift(0), encoder_entry, entry_biases[0]
    )
    if quick():
        leave_relay.touch()
    mixture, total = attend_forward(*encoder_view, *projected, heads, False)
    encoder_stored = (*projected, mixture, total)
    target_pieces = target_spread.finish()
    if quick():
        leave_relay.touch()
        rest_line = gather_line(hold(entry_rest))
        leaves = assemble(
            leave_relay.pieces(),
            jnp.stack([((relayed % 2) * 4 + relayed // 2) * piece] * 3),
            [(i * piece, piece, shards * piece) for i in range(3)],
            3 * piece,
        )
        feed_other = to_side(hold(feed_line))
    encoder_partials = Collect(project_out(mixture, leaves[0], count))
    encoder_partials.turn()
    target_incoming, target_incoming_low, target_sum = join_gradient(
        target_cotangent, target_keep, []
    )
    if quick():
        last_line = gather_line(hold(feed_one))
    middle, middle_normed = residual_norm(
        source_tokens, encoder_partials.finish(), exit_bias(0), gain(1), shift(1)
    )
    middle_spread = Spread(middle_normed)
    if quick():
        one_line = part_rows(rest_line, 2 * rows, 0, rows)
        two_line = part_rows(rest_line, 2 * rows, rows, rows)
        one_other = to_side(one_line)
    middle_pieces = middle_spread.finish()
    if quick():
        expand, reduce = [None, None], [None, None]
        feed_parts = [(0, rows, whole_rows), (rows, feed_rows, shards * feed_rows)]
        feed_table = jnp.stack([order * rows, order * feed_rows])
        height = rows + feed_rows
        expand[0], reduce[0] = assemble([feed_line, feed_other], feed_table, feed_parts, height)
    encoder_active, encoder_slope, partials = feed_forward(
        middle_pieces, expand[0], reduce[0], hidden_biases[0]
    )
    memory_partials = Collect(partials)
    memory_partials.turn()
    if quick():
        decoder_entry = assemble(
            [one_line, one_other], entry_table, [(0, rows, whole_rows)], rows
        )[0]
        two_other = to_side(hold(two_line))
    decoder_normed, *projected = project_self(
        target_pieces, gain(2), shift(2), decoder_entry, entry_biases[1]
    )
    mixture, total = attend_forward(*self_view, *projected, heads, True)
    decoder_stored = (*projected, mixture, total)
    memory_low = residual_low(middle, memory_partials.finish(), reducer_biases[0:1])
    memory_spread = Spread(memory_low)
    decoder_partials = Collect(project_out(mixture, leaves[1], count))
    decoder_partials.turn()
    if quick():
        last_other = to_side(hold(last_line))
    self_out, self_normed = residual_norm(
        target_tokens, decoder_partials.finish(), exit_bias(1), gain(3), shift(3)
    )
    self_spread = Spread(self_normed)
    memory_pieces = memory_spread.finish()
    self_pieces = self_spread.finish()
    if quick():
        cross_entry = assemble(
            [two_line, two_other], entry_table, [(0, rows, whole_rows)], rows
        )[0]
    target_incoming_spread = Spread(hold(target_incoming_low))
    cross_projected = project_cross(self_pieces, memory_pieces, cross_entry, entry_biases[2])
    mixture, total = attend_forward(*cross_view, *cross_projected, heads, False)
    cross_stored = (*cross_projected, mixture, total)
    target_incoming_pieces = target_incoming_spread.finish()
    partials = Collect(project_out(mixture, leaves[2], count))
    partials.turn()
    cross_out, cross_normed = residual_norm(
        self_out, partials.finish(), exit_bias(2), gain(4), shift(4)
    )
    cross_spread = Spread(cross_normed)
    if quick():
        expand[1], reduce[1] = assemble([last_line, last_other], feed_table, feed_parts, height)
    cross_pieces = cross_spread.finish()
    decoder_active, decoder_slope, partials = feed_forward(
        cross_pieces, expand[1], reduce[1], hidden_biases[1]
    )
    decoded_partials = Collect(partials)

    order = line_order() if quick() else None

    def feed_gradients(pieces, normed_pieces, hidden, active):
        pairs = [
            (normed_pieces, [hidden], 0, hidden.shape[1]),
            ([active], pieces, 0, model_width),
        ]
        return outer_sums(pairs, order, "feed_weights", True)

    def exit_gradient(stored, pieces):
        pairs = [([stored[3]], pieces, 0, model_width)]
        return outer_sums(pairs, None, "exit_weights")[0]

    def sums_over_batch(blocks):
        if quick():
            return Scatter(blocks)
        return [
            lax.psum_scatter(part, "batch", scatter_dimension=0, tiled=True) for part in blocks
        ]

    hidden, decoder_hidden_sum, partials = feed_backward(
        target_incoming_pieces, expand[1], reduce[1], decoder_slope
    )
    partials = Collect(partials)
    partials.turn()
    decoded_partials.turn()
    decoder_feed_shares = sums_over_batch(
        feed_gradients(target_incoming_pieces, cross_pieces, hidden, decoder_active)
    )
    incoming, incoming_low, norm_four = norm_backward(
        cross_out, gain(4), target_incoming, partials.finish()
    )
    incoming_spread = Spread(incoming_low)
    decoded_low = residual_low(cross_out, decoded_partials.finish(), reducer_biases[1:2])
    incoming_pieces = incoming_spread.finish()
    cross_joined, cross_sums, partials, memory_partials = attend_backward(
        *cross_view, incoming_pieces, leaves[2], cross_entry, cross_stored, heads, False, True
    )
    memory_partials = Collect(memory_partials)
    memory_partials.turn()
    partials = Collect(partials)
    cross_exit = exit_gradient(cross_stored, incoming_pieces)
    cross_shares = sums_over_batch(
        outer_sums(
            [
                (self_pieces, [cross_joined], 0, share),
                (memory_pieces, [cross_joined], share, 2 * share),
            ],
            order,
            "attention_weights",
        )
    )
    if quick():
        decoder_feed_shares.turn()
    source_incoming, source_incoming_low, source_sum = join_gradient(
        source_cotangent, source_keep, memory_partials.finish()
    )
    source_incoming_spread = Spread(source_incoming_low)
    partials.turn()
    source_incoming_pieces = source_incoming_spread.finish()
    hidden, encoder_hidden_sum, feed_partials = feed_backward(
        source_incoming_pieces, expand[0], reduce[0], encoder_slope
    )
    feed_partials = Collect(feed_partials)
    feed_partials.turn()
    self_incoming, self_incoming_low, norm_three = norm_backward(
        self_out, gain(3), incoming, partials.finish()
    )
    self_incoming_spread = Spread(self_incoming_low)
    encoder_feed_shares = sums_over_batch(
        feed_gradients(source_incoming_pieces, middle_pieces, hidden, encoder_active)
    )
    middle_incoming, middle_incoming_low, norm_one = norm_backward(
        middle, gain(1), source_incoming, feed_partials.finish()
    )
    middle_incoming_spread = Spread(middle_incoming_low)
    self_incoming_pieces = self_incoming_spread.finish()
    if quick():
        cross_shares.turn()
    decoder_exit = exit_gradient(decoder_stored, self_incoming_pieces)
    decoder_joined, decoder_sums, decoder_partials, _ = attend_backward(
        *self_view, self_incoming_pieces, leaves[1], decoder_entry, decoder_stored, heads, True, False
    )
    decoder_partials = Collect(decoder_partials)
    decoder_blocks = outer_sums(
        [([decoder_normed], [decoder_joined], 0, 3 * share)], order, "attention_weights"
    )
    middle_incoming_pieces = middle_incoming_spread.finish()
    encoder_exit = exit_gradient(encoder_stored, middle_incoming_pieces)
    exits = [encoder_exit, decoder_exit, cross_exit]
    if quick():
        table = ((order % 2) * 4 + order // 2) * piece
        decoder_shares = Scatter(join_blocks(decoder_blocks, exits, table))
        encoder_feed_shares.turn()
        decoder_feed_share, cross_share = decoder_feed_shares.finish(), cross_shares.finish()
    else:
        decoder_shares = sums_over_batch(decoder_blocks)
    decoder_partials.turn()
    encoder_joined, encoder_sums, encoder_partials, _ = attend_backward(
        *encoder_view,
        middle_incoming_pieces,
        leaves[0],
        encoder_entry,
        encoder_stored,
        heads,
        False,
        False,
    )
    encoder_partials = Collect(encoder_partials)
    encoder_shares = sums_over_batch(
        outer_sums([([encoder_normed], [encoder_joined], 0, 3 * share)], order, "attention_weights")
    )
    encoder_partials.turn()
    if quick():
        decoder_shares.turn()
        encoder_feed_share = encoder_feed_shares.finish()
        decoder_feed_spread = Spread(decoder_feed_share)
    target_gradient, _, norm_two = norm_backward(
        target_tokens, gain(2), self_incoming, decoder_partials.finish()
    )
    source_gradient, _, norm_zero = norm_backward(
        source_tokens, gain(0), middle_incoming, encoder_partials.finish()
    )

    norms = (norm_zero, norm_one, norm_two, norm_three, norm_four)
    if quick():
        owners = me ^ jnp.array(seq_offsets(), jnp.int32)
        entry_moves = [
            ((0, rows), (part * share, share), (0, 0), (part * model_width, share))
            for part in range(3)
        ]
        expand_moves = [
            ((0, rows), (part * feed_rows, feed_rows), (0, 0), (part * lanes, feed_rows))
            for part in range(shards)
        ]
        reduce_moves = [((rows, feed_rows), (0, model_width), (0, feed_rows), (0, 0))]

        def finish_entry(block, shares, former):
            outputs = [(projections.shape, block, entry_moves)]
            return finish(shares, owners, former, outputs, "finish_entry")

        def finish_feed(feed, shares, former):
            outputs = [
                (expanders.shape, feed, expand_moves),
                (reducers.shape, feed, reduce_moves),
            ]
            return finish(shares, owners, former, outputs, "finish_feed")

        laid = lay_sums(
            [*norms, source_sum, target_sum],
            [encoder_sums, decoder_sums, cross_sums],
            [encoder_hidden_sum, decoder_hidden_sum],
            me[None],
            shards,
        )
        summed = Sum(laid)
        encoder_shares.turn()
        cross_spread = Spread(cross_share)
        feeds_whole = finish_feed(1, decoder_feed_spread.finish(), [])
        summed.turn()
        feed_spread = Spread(encoder_feed_share)
        entry_whole = finish_entry(2, cross_spread.finish(), [])
        summed.turn()
        decoder_share, exit_share = part_blocks(
            decoder_shares.finish(), rows, 3, piece, model_width
        )
        feeds_whole = finish_feed(0, feed_spread.finish(), feeds_whole)
        exit_return = Return(exit_share, 3)
        summed.turn()
        decoder_spread = Spread(decoder_share)
        summed.turn()
        exit_return.turn()
        entry_whole = finish_entry(1, decoder_spread.finish(), entry_whole)
        summed.turn()
        summed = summed.values
        exit_return.turn()
        combiners_gradient = exit_return.finish()
        encoder_spread = Spread(encoder_shares.finish())
        entry_whole = finish_entry(0, encoder_spread.finish(), entry_whole)
        projections_gradient = entry_whole[0]
        expanders_gradient, reducers_gradient = feeds_whole
        norm_sums = summed[:15].reshape(5, 3, -1)
        exit_sums = summed[15:17]
        inner = summed[17:23].reshape(3, 2, -1)
        hidden_sums = summed[23 : 23 + 2 * expanders.shape[2] // model_width].reshape(2, -1)
    else:
        wholes = [
            lax.dynamic_update_slice(
                jnp.zeros((count,) + part.shape, low), part[None], (me, 0, 0)
            ).reshape(-1, model_width)
            for part in exits
        ]
        combiners_gradient = jnp.stack([sums_over_batch([part])[0] for part in wholes])
        combiners_gradient = lax.psum(combiners_gradient, "seq").astype(high)
        entry_shares = [encoder_shares[0], decoder_shares[0], jnp.concatenate(cross_shares, 1)]
        feed_shares = [encoder_feed_shares, decoder_feed_shares]

        def whole(part, groups):
            pieces = [p.reshape(rows, groups, -1) for p in spread(part)]
            return spread_order(pieces, 2).reshape(rows, -1).astype(high)

        projections_gradient = jnp.stack([whole(part, 3) for part in entry_shares])
        expanders_gradient = jnp.stack([whole(part[0], shards) for part in feed_shares])
        reducers_gradient = jnp.stack(
            [spread_order(spread(part[1]), 0).reshape(-1, model_width) for part in feed_shares]
        ).astype(high)
        inner = jnp.stack([encoder_sums, decoder_sums, cross_sums])
        inner = lax.dynamic_update_slice(
            jnp.zeros((3, 2, count, share), high), inner[:, :, None], (0, 0, me, 0)
        )
        hidden_sums = jnp.stack([encoder_hidden_sum, decoder_hidden_sum])
        hidden_sums = hidden_sums.reshape(2, shards, 1, -1)
        hidden_sums = lax.dynamic_update_slice(
            jnp.zeros((2, shards, count, hidden_sums.shape[3]), high), hidden_sums, (0, 0, me, 0)
        )
        parts = [jnp.stack(norms), jnp.concatenate([source_sum, target_sum]), inner, hidden_sums]
        summed = lax.psum(parts, ("batch", "seq"))
        norm_sums, exit_sums, inner, hidden_sums = summed
        inner = inner.reshape(3, 2, -1)
        hidden_sums = hidden_sums.reshape(2, -1)
    outer = jnp.stack([norm_sums[1, 2], norm_sums[3, 2], norm_sums[4, 2]])
    return (
        memory_low[None],
        decoded_low[None],
        source_gradient[None],
        target_gradient[None],
        projections_gradient,
        combiners_gradient,
        expanders_gradient,
        reducers_gradient,
        norm_sums[:, 0],
        norm_sums[:, 1],
        jnp.concatenate([inner, outer[:, None]], 1),
        hidden_sums,
        exit_sums,
    )


def solution(mesh):
    in_specs = (
        P("batch", "seq", None),
        P("batch", "seq", None),
        P("batch", None),
        P("batch", None),
        P(None, "batch", None),
        P(None, "batch", None),
        P(None, "batch", None),
        P(None, "batch", None),
        P(),
        P(),
        P(),
        P(),
        P(),
        P("batch", "seq", None),
        P("batch", "seq", None),
    )
    out_specs = (
        P("batch", "seq", None),
        P("batch", "seq", None),
        P("batch", "seq", None),
        P("batch", "seq", None),
        P(None, "batch", None),
        P(None, "batch", None),
        P(None, "batch", None),
        P(None, "batch", None),
        P(),
        P(),
        P(),
        P(),
        P(),
    )
    return jax.shard_map(
        per_device, mesh=mesh, in_specs=in_specs, out_specs=out_specs, check_vma=False
    )
```

```python
import jax
import jax.numpy as jnp
from jax import lax
from jax.experimental import pallas as pl
from jax.experimental.pallas import tpu as pltpu
from jax.sharding import PartitionSpec as P

HEADS = 16
COST = 0.05


epsilon = 1e-05
masked_score = -1e30
low = jnp.bfloat16
high = jnp.float32
shape = jax.ShapeDtypeStruct
VMEM = pl.BlockSpec(memory_space=pltpu.VMEM)
SMEM = pl.BlockSpec(memory_space=pltpu.SMEM)
across_rows = (((0,), (0,)), ((), ()))
across_lanes = (((1,), (1,)), ((), ()))


class Turn:
    last = None
    done = None


def after(values, earlier):
    return lax.optimization_barrier((values, earlier))[0]


def hold(values):
    return values if Turn.last is None else after(values, Turn.last)


def take_turn(call, args, skip=0):
    args = list(args)
    least = min(range(skip, len(args)), key=lambda i: args[i].size)
    args[least] = hold(args[least])
    results = call(*args)
    Turn.last = min(results, key=lambda value: value.size)
    return results


def run(kernel, outs, args, name, flops, scratch=(), scalars=0, room=24):
    call = pl.pallas_call(
        kernel,
        out_shape=list(outs),
        in_specs=[SMEM] * scalars + [VMEM] * (len(args) - scalars),
        out_specs=[VMEM] * len(outs),
        scratch_shapes=list(scratch),
        compiler_params=pltpu.CompilerParams(vmem_limit_bytes=room << 20),
        cost_estimate=pl.CostEstimate(
            flops=int(flops * COST), bytes_accessed=0, transcendentals=0
        ),
        name=name,
    )
    return take_turn(call, args)


def normalize(values, gain, shift):
    middle = jnp.mean(values, -1, keepdims=True)
    centred = values - middle
    width = jnp.mean(centred * centred, -1, keepdims=True)
    return centred * lax.rsqrt(width + epsilon) * gain + shift


def matmul(left, right):
    return jnp.dot(left, right, preferred_element_type=high)


def matmul_back(left, right):
    return lax.dot_general(left, right, across_lanes, preferred_element_type=high)


def matmul_outer(left, right):
    return lax.dot_general(left, right, across_rows, preferred_element_type=high)


def piece_rows(pieces):
    start = 0
    for piece in pieces:
        yield pl.ds(start, piece.shape[0]), piece
        start += piece.shape[0]


def assemble(sources, table, parts, height):
    counts = [source.shape[0] // height for source in sources]
    spots = [(i, at) for i, count in enumerate(counts) for at in range(count)]

    def kernel(table_ref, *refs):
        outs = refs[len(sources) :]
        for which, (start, rows, _) in enumerate(parts):
            for i, (source, at) in enumerate(spots):
                first = at * height + start
                where = pl.ds(pl.multiple_of(table_ref[which, i], rows), rows)
                outs[which][where, :] = refs[source][first : first + rows, :]

    width = sources[0].shape[1]
    outs = [shape((whole, width), low) for _, _, whole in parts]
    return run(kernel, outs, [table, *sources], "assemble", 1, scalars=1)


def part_rows(pieces, height, first, rows):
    count = pieces.shape[0] // height

    def kernel(source, out):
        for i in range(count):
            start = i * height + first
            out[i * rows : (i + 1) * rows, :] = source[start : start + rows, :]

    outs = [shape((count * rows, pieces.shape[1]), low)]
    return run(kernel, outs, [pieces], "part_rows", 1)[0]


def project_self(pieces, gain, shift, entry, biases):
    count, width = len(pieces), entry.shape[1] // 3

    def kernel(*refs):
        sources = refs[:count]
        gain_ref, shift_ref, entry_ref, bias_ref, normed_ref, query_ref, key_ref, value_ref = refs[
            count:
        ]
        for rows, source in piece_rows(sources):
            normed = normalize(source[...].astype(high), gain_ref[...], shift_ref[...])
            normed_ref[rows, :] = normed.astype(low)
            joined = matmul(normed_ref[rows, :], entry_ref[...])
            query_ref[rows, :] = (joined[:, :width] + bias_ref[0:1, :]).astype(low)
            key_ref[rows, :] = joined[:, width : 2 * width].astype(low)
            value_ref[rows, :] = (joined[:, 2 * width :] + bias_ref[1:2, :]).astype(low)

    rows = sum(piece.shape[0] for piece in pieces)
    outs = [shape((rows, pieces[0].shape[1]), low)] + [shape((rows, width), low)] * 3
    flops = 2 * rows * entry.shape[0] * entry.shape[1]
    return run(kernel, outs, [*pieces, gain, shift, entry, biases], "project_self", flops)


def project_cross(pieces, memory_pieces, entry, biases):
    count, width = len(pieces), entry.shape[1] // 3

    def kernel(*refs):
        sources, memories = refs[:count], refs[count : 2 * count]
        entry_ref, bias_ref, query_ref, key_ref, value_ref = refs[2 * count :]
        for rows, source in piece_rows(sources):
            joined = matmul(source[...], entry_ref[:, :width])
            query_ref[rows, :] = (joined + bias_ref[0:1, :]).astype(low)
        for rows, source in piece_rows(memories):
            joined = matmul(source[...], entry_ref[:, width:])
            key_ref[rows, :] = joined[:, :width].astype(low)
            value_ref[rows, :] = (joined[:, width:] + bias_ref[1:2, :]).astype(low)

    rows = sum(piece.shape[0] for piece in pieces)
    outs = [shape((rows, width), low)] * 3
    flops = 2 * rows * entry.shape[0] * entry.shape[1]
    return run(kernel, outs, [*pieces, *memory_pieces, entry, biases], "project_cross", flops)


def head_lanes(values, head, width):
    lanes = lax.broadcasted_iota(jnp.int32, values.shape, 1)
    inside = (lanes >= head * width) & (lanes < (head + 1) * width)
    return jnp.where(inside, values, jnp.zeros_like(values))


def block_bias(keys, cols, causal, key_segment, query_segment, key_place, query_place):
    allowed = key_segment[keys, :] == query_segment[:, cols]
    if causal:
        allowed = allowed & (key_place[keys, :] <= query_place[:, cols])
    return jnp.where(allowed, 0.0, masked_score)


def attend_forward(marks, tags, queries, keys, values, heads, causal):
    rows, width = queries.shape
    head_width = width // heads
    block = min(256, rows)
    blocks = rows // block
    scale = head_width**-0.5
    tall = max(8, heads)

    def kernel(*refs):
        marks_ref, key_segment, query_segment, key_place, query_place = refs[:5]
        query_ref, key_ref, value_ref, mixture_ref, total_ref = refs[5:10]
        score_ref, top_ref, sum_ref, mix_ref, value_turned = refs[10:]
        value_turned[...] = value_ref[...].astype(high).T.astype(low)
        total_ref[...] = jnp.zeros(total_ref.shape, high)
        for i in range(blocks):
            mine = pl.ds(i * block, block)
            cols = slice(i * block, (i + 1) * block)
            query = query_ref[mine, :] * low(scale)
            query_heads = [head_lanes(query, head, head_width) for head in range(heads)]
            top_ref[...] = jnp.full(top_ref.shape, masked_score, high)
            sum_ref[...] = jnp.zeros(sum_ref.shape, high)
            mix_ref[...] = jnp.zeros(mix_ref.shape, high)

            def score(j, carry, i=i, cols=cols, query_heads=query_heads):
                @pl.when(marks_ref[i, j] != 0)
                def _():
                    there = pl.ds(pl.multiple_of(j * block, block), block)
                    bias = block_bias(
                        there, cols, causal, key_segment, query_segment, key_place, query_place
                    )
                    for head in range(heads):
                        scores = matmul_back(key_ref[there, :], query_heads[head]) + bias
                        score_ref[head, there, :] = scores
                        row = slice(head, head + 1)
                        top_ref[row, :] = jnp.maximum(
                            top_ref[row, :], jnp.max(scores, 0, keepdims=True)
                        )

                return carry

            lax.fori_loop(0, blocks, score, 0)

            def mix(j, carry, i=i):
                @pl.when(marks_ref[i, j] != 0)
                def _():
                    there = pl.ds(pl.multiple_of(j * block, block), block)
                    for head in range(heads):
                        row = slice(head, head + 1)
                        features = slice(head * head_width, (head + 1) * head_width)
                        weights = jnp.exp(score_ref[head, there, :] - top_ref[row, :])
                        sum_ref[row, :] += jnp.sum(weights, 0, keepdims=True)
                        mix_ref[features, :] += matmul(
                            value_turned[features, there], weights.astype(low)
                        )

                return carry

            lax.fori_loop(0, blocks, mix, 0)
            for head in range(heads):
                row = slice(head, head + 1)
                features = slice(head * head_width, (head + 1) * head_width)
                mix_ref[features, :] = mix_ref[features, :] * (1.0 / sum_ref[row, :])
                total_ref[row, cols] = top_ref[row, :] + jnp.log(sum_ref[row, :])
            mixture_ref[mine, :] = mix_ref[...].T.astype(low)

    outs = [shape((rows, width), low), shape((tall, rows), high)]
    scratch = [
        pltpu.VMEM((heads, rows, block), high),
        pltpu.VMEM((tall, block), high),
        pltpu.VMEM((tall, block), high),
        pltpu.VMEM((width, block), high),
        pltpu.VMEM((width, rows), low),
    ]
    flops = 8 * rows * rows * width
    args = [marks, *tags, queries, keys, values]
    return run(kernel, outs, args, "attend_forward", flops, scratch, scalars=1)


def project_out(mixture, leave, count):
    local = mixture.shape[0] // count

    def kernel(mixture_ref, leave_ref, *outs):
        for i, out in enumerate(outs):
            out[...] = matmul(mixture_ref[pl.ds(i * local, local), :], leave_ref[...]).astype(low)

    outs = [shape((local, leave.shape[1]), low)] * count
    return run(kernel, outs, [mixture, leave], "project_out", 2 * mixture.size * leave.shape[1])


def attend_backward(marks, tags, pieces, leave, entry, stored, heads, causal, cross):
    queries, keys, values, mixture, total = stored
    count = len(pieces)
    rows, width = queries.shape
    head_width = width // heads
    block = min(256, rows)
    blocks = rows // block
    local = rows // count
    scale = head_width**-0.5

    def kernel(*refs):
        marks_ref, key_segment, query_segment, key_place, query_place = refs[:5]
        incoming_refs = refs[5 : 5 + count]
        leave_ref, entry_ref, query_ref, key_ref, value_ref, mixture_ref, total_ref = refs[
            5 + count : 12 + count
        ]
        joined_ref, sums_ref = refs[12 + count : 14 + count]
        partial_refs = refs[14 + count : 14 + 2 * count]
        memory_refs = refs[14 + 2 * count : -5]
        incoming_mix, key_sum, value_sum, query_turned, key_turned = refs[-5:]
        for where, piece in piece_rows(incoming_refs):
            incoming_mix[where, :] = matmul_back(piece[...], leave_ref[...]).astype(low)
        key_turned[...] = key_ref[...].astype(high).T.astype(low)
        key_sum[...] = jnp.zeros(key_sum.shape, high)
        value_sum[...] = jnp.zeros(value_sum.shape, high)
        query_total = jnp.zeros((1, width), high)
        for i in range(blocks):
            mine = pl.ds(i * block, block)
            cols = slice(i * block, (i + 1) * block)
            query = query_ref[mine, :] * low(scale)
            arriving = incoming_mix[mine, :]
            query_heads = [head_lanes(query, head, head_width) for head in range(heads)]
            arriving_heads = [head_lanes(arriving, head, head_width) for head in range(heads)]
            products = (arriving.astype(high) * mixture_ref[mine, :].astype(high)).T
            inner = [
                jnp.sum(products[head * head_width : (head + 1) * head_width, :], 0, keepdims=True)
                for head in range(heads)
            ]
            query_turned[...] = jnp.zeros(query_turned.shape, high)

            def step(j, carry, i=i, cols=cols, qh=query_heads, ah=arriving_heads, inner=inner):
                @pl.when(marks_ref[i, j] != 0)
                def _():
                    there = pl.ds(pl.multiple_of(j * block, block), block)
                    bias = block_bias(
                        there, cols, causal, key_segment, query_segment, key_place, query_place
                    )
                    key_acc, value_acc = key_sum[there, :], value_sum[there, :]
                    for head in range(heads):
                        features = slice(head * head_width, (head + 1) * head_width)
                        scores = matmul_back(key_ref[there, :], qh[head])
                        weights = jnp.exp(scores - total_ref[head : head + 1, cols] + bias)
                        back = matmul_back(value_ref[there, :], ah[head])
                        change = (weights * (back - inner[head])).astype(low)
                        value_acc = value_acc + matmul(weights.astype(low), ah[head])
                        key_acc = key_acc + matmul(change, qh[head])
                        query_turned[features, :] += matmul(key_turned[features, there], change)
                    key_sum[there, :] = key_acc
                    value_sum[there, :] = value_acc

                return carry

            lax.fori_loop(0, blocks, step, 0)
            query_gradient = query_turned[...].T * scale
            query_total = query_total + jnp.sum(query_gradient, 0, keepdims=True)
            joined_ref[mine, :width] = query_gradient.astype(low)
        joined_ref[:, width : 2 * width] = key_sum[...].astype(low)
        joined_ref[:, 2 * width :] = value_sum[...].astype(low)
        sums_ref[0:1, :] = query_total
        sums_ref[1:2, :] = jnp.sum(value_sum[...], 0, keepdims=True)
        for i in range(count):
            mine = pl.ds(i * local, local)
            if cross:
                query_part = matmul_back(joined_ref[mine, :width], entry_ref[:, :width])
                memory_part = matmul_back(joined_ref[mine, width:], entry_ref[:, width:])
                partial_refs[i][...] = query_part.astype(low)
                memory_refs[i][...] = memory_part.astype(low)
            else:
                partial_refs[i][...] = matmul_back(joined_ref[mine, :], entry_ref[...]).astype(low)

    outs = [shape((rows, 3 * width), low), shape((2, width), high)]
    outs += [shape((local, entry.shape[0]), low)] * (count * (2 if cross else 1))
    scratch = [
        pltpu.VMEM((rows, width), low),
        pltpu.VMEM((rows, width), high),
        pltpu.VMEM((rows, width), high),
        pltpu.VMEM((width, block), high),
        pltpu.VMEM((width, rows), low),
    ]
    flops = 20 * rows * rows * width + 10 * rows * width * entry.shape[0]
    args = [marks, *tags, *pieces, leave, entry, queries, keys, values, mixture, total]
    joined, sums, *partials = run(
        kernel, outs, args, "attend_backward", flops, scratch, scalars=1, room=28
    )
    return joined, sums, partials[:count], partials[count:]


def feed_forward(pieces, entry, leave, bias):
    count, hidden_width = len(pieces), entry.shape[1]
    step = min(512, hidden_width)

    def kernel(*refs):
        sources = refs[:count]
        entry_ref, leave_ref, bias_ref, active_ref, slope_ref = refs[count : count + 5]
        partial_refs = refs[count + 5 :]
        for (rows, source), partial in zip(piece_rows(sources), partial_refs):
            for start in range(0, hidden_width, step):
                cols = slice(start, start + step)
                hidden = matmul(source[...], entry_ref[:, cols]) + bias_ref[:, cols]
                share = 0.5 * (1.0 + lax.erf(hidden * 0.7071067811865476))
                density = jnp.exp(-0.5 * hidden * hidden) * 0.3989422804014327
                active_ref[rows, cols] = (hidden * share).astype(low)
                slope_ref[rows, cols] = (share + hidden * density).astype(low)
            partial[...] = matmul(active_ref[rows, :], leave_ref[...]).astype(low)

    rows = sum(piece.shape[0] for piece in pieces)
    outs = [shape((rows, hidden_width), low)] * 2
    outs += [shape((piece.shape[0], leave.shape[1]), low) for piece in pieces]
    flops = 4 * rows * entry.shape[0] * hidden_width
    args = [*pieces, entry, leave, bias]
    active, slope, *partials = run(kernel, outs, args, "feed_forward", flops)
    return active, slope, partials


def feed_backward(pieces, entry, leave, slope):
    count, hidden_width = len(pieces), entry.shape[1]

    def kernel(*refs):
        sources = refs[:count]
        entry_ref, leave_ref, slope_ref, hidden_ref, sum_ref = refs[count : count + 5]
        partial_refs = refs[count + 5 :]
        total = jnp.zeros(sum_ref.shape, high)
        for (rows, source), partial in zip(piece_rows(sources), partial_refs):
            hidden = matmul_back(source[...], leave_ref[...]) * slope_ref[rows, :].astype(high)
            total = total + jnp.sum(hidden, 0, keepdims=True)
            hidden_ref[rows, :] = hidden.astype(low)
            partial[...] = matmul_back(hidden_ref[rows, :], entry_ref[...]).astype(low)
        sum_ref[...] = total

    rows = sum(piece.shape[0] for piece in pieces)
    outs = [shape((rows, hidden_width), low), shape((1, hidden_width), high)]
    outs += [shape((piece.shape[0], entry.shape[0]), low) for piece in pieces]
    flops = 4 * rows * entry.shape[0] * hidden_width
    args = [*pieces, entry, leave, slope]
    hidden, total, *partials = run(kernel, outs, args, "feed_backward", flops)
    return hidden, total, partials


def blocks_out(shards, height, width):
    return [shape((shards // 2, height, width), low)] * 2


def block_targets(refs):
    return [(ref, at) for ref in refs for at in range(ref.shape[0])]


def outer_sums(pairs, order, name, stacked=False):
    flat, counts, flops = [], [], 0
    for lefts, rights, start, lanes in pairs:
        flat += [*lefts, *rights]
        counts.append((len(lefts), len(rights), start, lanes))
        flops += 2 * sum(left.size for left in lefts) * lanes
    sizes = [(pair[0][0].shape[1], pair[3]) for pair in pairs]

    def compute(refs, outs):
        for (left_count, right_count, start, lanes), out in zip(counts, outs):
            lefts, rights = refs[:left_count], refs[left_count : left_count + right_count]
            refs = refs[left_count + right_count :]
            terms = max(left_count, right_count)
            rows = sum(left.shape[0] for left in lefts) // terms
            step = min(256, out.shape[0])
            side = slice(start, start + lanes)
            for first in range(0, out.shape[0], step):
                cols = slice(first, first + step)
                total = None
                for i in range(terms):
                    where = pl.ds(i * rows, rows)
                    left = lefts[i][:, cols] if left_count == terms else lefts[0][where, cols]
                    right = rights[i][:, side] if right_count == terms else rights[0][where, side]
                    term = matmul_outer(left, right)
                    total = term if total is None else total + term
                out[cols, :] = total.astype(low)

    if order is None:

        def plain(*refs):
            compute(refs[: len(flat)], refs[len(flat) :])

        return run(plain, [shape(size, low) for size in sizes], flat, name, flops)

    straight = isinstance(order, int)
    shards = order if straight else order.shape[0]
    heights = [size[0] // shards for size in sizes]
    if stacked:
        corners = [(sum(heights[:i]), 0) for i in range(len(sizes))]
        outs = blocks_out(shards, sum(heights), sizes[0][1])
    else:
        corners = [(0, sum(size[1] for size in sizes[:i])) for i in range(len(sizes))]
        outs = blocks_out(shards, heights[0], sum(size[1] for size in sizes))
    scratch = [pltpu.VMEM(size, low) for size in sizes]
    if straight:
        height, width = outs[0].shape[1:]

        def fixed(*refs):
            inputs, (out, *buffers) = refs[: len(flat)], refs[len(flat) :]
            compute(inputs, buffers)
            for i in range(shards):
                for source, rows, (top, side) in zip(buffers, heights, corners):
                    part = source[i * rows : (i + 1) * rows, :]
                    out[i, top : top + rows, side : side + source.shape[1]] = part

        return run(fixed, [shape((shards, height, width), low)], flat, name, flops, scratch)[0]

    def kernel(order_ref, *refs):
        inputs, rest = refs[: len(flat)], refs[len(flat) :]
        compute(inputs, rest[2:])
        for i, (target, at) in enumerate(block_targets(rest[:2])):
            for source, rows, (top, side) in zip(rest[2:], heights, corners):
                where = pl.ds(pl.multiple_of(order_ref[i] * rows, rows), rows)
                target[at, top : top + rows, side : side + source.shape[1]] = source[where, :]

    return run(kernel, outs, [order, *flat], name, flops, scratch, scalars=1)


def join_blocks(blocks, exits, table):
    keep, sent = blocks
    half, height, width = keep.shape
    rows, full = exits[0].shape[0] // (2 * half), exits[0].shape[1]
    rest = full - width
    tall = rows * len(exits)

    def kernel(table_ref, keep_ref, sent_ref, *refs):
        sources = refs[: len(exits)]
        for i, (target, at) in enumerate(block_targets(refs[len(exits) :])):
            former = keep_ref if i < half else sent_ref
            target[at, :height, :] = former[at]
            where = pl.ds(pl.multiple_of(table_ref[i], rows), rows)
            for block, source in enumerate(sources):
                top = height + block * rows
                target[at, top : top + rows, :] = source[where, :width]
                side = slice(block * rest, (block + 1) * rest)
                target[at, height + tall : height + tall + rows, side] = source[where, width:]

    outs = [shape((half, height + tall + rows, width), low)] * 2
    return run(kernel, outs, [table, keep, sent, *exits], "join_blocks", 1, scalars=1)


def part_blocks(share, height, blocks, rows, full):
    width = share.shape[1]
    rest = full - width
    tall = rows * blocks

    def kernel(share_ref, first_ref, second_ref):
        first_ref[...] = share_ref[:height, :]
        for block in range(blocks):
            where = slice(block * rows, (block + 1) * rows)
            top = height + block * rows
            second_ref[where, :width] = share_ref[top : top + rows, :]
            side = slice(block * rest, (block + 1) * rest)
            second_ref[where, width:] = share_ref[height + tall : height + tall + rows, side]

    outs = [shape((height, width), low), shape((tall, full), low)]
    return run(kernel, outs, [share], "part_blocks", 1)


def cut(arrays, table, moves, outs, name):
    def kernel(table_ref, *refs):
        sources, targets, semaphore = refs[: len(arrays)], refs[len(arrays) : -1], refs[-1]
        copies = []
        for array, block, rows, (row, down), lanes, (lane, along), entry, out, top, side in moves:
            where = table_ref[entry]
            first = row + pl.multiple_of(where * down, down) if down else row
            left = pl.multiple_of(lane + where * along, lanes) if along else lane
            source = sources[array].at[block, pl.ds(first, rows), pl.ds(left, lanes)]
            target = targets[out].at[pl.ds(top, rows), pl.ds(side, lanes)]
            copies.append(pltpu.make_async_copy(source, target, semaphore.at[len(copies)]))
            copies[-1].start()
        for started in copies:
            started.wait()

    anywhere = pl.BlockSpec(memory_space=pltpu.HBM)
    call = pl.pallas_call(
        kernel,
        out_shape=outs,
        in_specs=[SMEM] + [anywhere] * len(arrays),
        out_specs=[VMEM] * len(outs),
        scratch_shapes=[pltpu.SemaphoreType.DMA((len(moves),))],
        compiler_params=pltpu.CompilerParams(vmem_limit_bytes=60 << 20),
        cost_estimate=pl.CostEstimate(flops=1, bytes_accessed=0, transcendentals=0),
        name=name,
    )
    return take_turn(call, [table, *arrays])


def finish(pieces, table, former, outputs, name):
    count = len(pieces)

    def kernel(table_ref, *refs):
        sources, begun_ref = refs[:count], refs[count]
        refs = refs[count + 1 + len(former) :]
        targets, done_ref = refs[: len(outputs)], refs[len(outputs)]
        buffers, semaphore = refs[len(outputs) + 1 : -1], refs[-1]
        copies = []
        done_ref[...] = begun_ref[...]
        for i, ((_, block, moves), target, buffer) in enumerate(zip(outputs, targets, buffers)):
            for which, source in enumerate(sources):
                owner = table_ref[which]
                for (top, rows), (side, lanes), (row, row_step), (lane, lane_step) in moves:
                    down = row + pl.multiple_of(owner * row_step, row_step) if row_step else row
                    along = lane + owner * lane_step if lane_step else lane
                    if lane_step:
                        along = pl.multiple_of(along, lanes)
                    part = source[top : top + rows, side : side + lanes].astype(high)
                    buffer[pl.ds(down, rows), pl.ds(along, lanes)] = part
            copies.append(pltpu.make_async_copy(buffer, target.at[block], semaphore.at[i]))
            copies[-1].start()
        for started in copies:
            started.wait()

    anywhere = pl.BlockSpec(memory_space=pl.ANY)
    aliases = {2 + count + i: i for i in range(len(former))}
    call = pl.pallas_call(
        kernel,
        out_shape=[shape(size, high) for size, _, _ in outputs] + [shape(Turn.done.shape, high)],
        in_specs=[SMEM] + [VMEM] * (count + 1) + [anywhere] * len(former),
        out_specs=[anywhere] * len(outputs) + [VMEM],
        scratch_shapes=[pltpu.VMEM(size[1:], high) for size, _, _ in outputs]
        + [pltpu.SemaphoreType.DMA((len(outputs),))],
        input_output_aliases=aliases,
        compiler_params=pltpu.CompilerParams(vmem_limit_bytes=24 << 20),
        cost_estimate=pl.CostEstimate(flops=1, bytes_accessed=0, transcendentals=0),
        name=name,
    )
    *results, Turn.done = call(hold(table), *pieces, Turn.done, *former)
    Turn.last = Turn.done
    return results


def lay_sums(rows, shares, hidden, me, shards):
    width, share = rows[0].shape[1], shares[0].shape[1]
    narrow = hidden[0].shape[1] // shards
    group = narrow * (width // share)
    per_row = width // group
    used = sum(part.shape[0] for part in [*rows, *shares]) + len(hidden) * shards // per_row
    total = -(-used // 8) * 8

    def kernel(me_ref, *refs):
        out = refs[-1]
        mine = me_ref[0]
        out[...] = jnp.zeros(out.shape, high)
        at = 0
        for ref in refs[: len(rows)]:
            out[at : at + ref.shape[0], :] = ref[...]
            at += ref.shape[0]
        side = pl.ds(pl.multiple_of(mine * share, share), share)
        for ref in refs[len(rows) : len(rows) + len(shares)]:
            out[at : at + ref.shape[0], side] = ref[...]
            at += ref.shape[0]
        for ref in refs[len(rows) + len(shares) : -1]:
            for shard in range(shards):
                start = (shard % per_row) * group + mine * narrow
                row = at + shard // per_row
                here = slice(shard * narrow, (shard + 1) * narrow)
                out[row : row + 1, pl.ds(pl.multiple_of(start, narrow), narrow)] = ref[:, here]
            at += shards // per_row

    args = [me, *rows, *shares, *hidden]
    return run(kernel, [shape((total, width), high)], args, "lay_sums", total, scalars=1)[0]


def add_up(refs):
    total = refs[0][...].astype(high)
    for ref in refs[1:]:
        total = total + ref[...].astype(high)
    return total


def residual_norm(base, addends, bias, gain, shift):
    count = 1 + len(addends)

    def kernel(*refs):
        bias_ref, gain_ref, shift_ref, total_ref, normed_ref = refs[count:]
        total = add_up(refs[:count]) + bias_ref[...]
        total_ref[...] = total
        normed_ref[...] = normalize(total, gain_ref[...], shift_ref[...]).astype(low)

    outs = [shape(base.shape, high), shape(base.shape, low)]
    return run(kernel, outs, [base, *addends, bias, gain, shift], "residual_norm", base.size * 12)


def residual_low(base, addends, bias):
    count = 1 + len(addends)

    def kernel(*refs):
        bias_ref, total_ref = refs[count:]
        total_ref[...] = (add_up(refs[:count]) + bias_ref[...]).astype(low)

    outs = [shape(base.shape, low)]
    return run(kernel, outs, [base, *addends, bias], "residual_low", base.size * 4)[0]


def join_gradient(cotangent, keep, addends):
    count = len(addends)

    def kernel(*refs):
        cotangent_ref, keep_ref = refs[:2]
        gradient_ref, low_ref, sum_ref = refs[2 + count :]
        total = cotangent_ref[...].astype(high) * keep_ref[...]
        for ref in refs[2 : 2 + count]:
            total = total + ref[...].astype(high)
        gradient_ref[...] = total
        low_ref[...] = total.astype(low)
        sum_ref[...] = jnp.sum(total, 0, keepdims=True)

    outs = [
        shape(cotangent.shape, high),
        shape(cotangent.shape, low),
        shape((1, cotangent.shape[1]), high),
    ]
    return run(kernel, outs, [cotangent, keep, *addends], "join_gradient", cotangent.size * 4)


def norm_backward(inputs, gain, incoming, addends):
    count = len(addends)

    def kernel(*refs):
        input_ref, gain_ref, incoming_ref = refs[:3]
        result_ref, low_ref, sums_ref = refs[3 + count :]
        gradient = add_up(refs[3 : 3 + count])
        values = input_ref[...].astype(high)
        centred = values - jnp.mean(values, -1, keepdims=True)
        inverse = lax.rsqrt(jnp.mean(centred * centred, -1, keepdims=True) + epsilon)
        unit = centred * inverse
        sums_ref[0:1, :] = jnp.sum(gradient * unit, 0, keepdims=True)
        sums_ref[1:2, :] = jnp.sum(gradient, 0, keepdims=True)
        scaled = gradient * gain_ref[...]
        inner = jnp.mean(scaled * unit, -1, keepdims=True)
        change = (scaled - jnp.mean(scaled, -1, keepdims=True) - unit * inner) * inverse
        result = incoming_ref[...] + change
        result_ref[...] = result
        low_ref[...] = result.astype(low)
        sums_ref[2:3, :] = jnp.sum(result, 0, keepdims=True)

    outs = [
        shape(inputs.shape, high),
        shape(inputs.shape, low),
        shape((3, inputs.shape[1]), high),
    ]
    args = [inputs, gain, incoming, *addends]
    return run(kernel, outs, args, "norm_backward", inputs.size * 20)


def seq_bits():
    bit, bits = lax.axis_size("seq") >> 1, []
    while bit:
        bits.append(bit)
        bit >>= 1
    return bits


def seq_offsets():
    offsets = [0]
    for bit in seq_bits():
        offsets = offsets + [offset ^ bit for offset in offsets]
    return offsets


def swap(values, bit, axis="seq"):
    return lax.ppermute(values, axis, [(i, i ^ bit) for i in range(lax.axis_size(axis))])


def spread(piece):
    pieces = [piece]
    for bit in seq_bits():
        pieces = pieces + [swap(piece, bit) for piece in pieces]
    return pieces


def quick():
    return lax.axis_size("seq") == 4 and lax.axis_size("batch") == 8


class Spread:
    def __init__(self, piece):
        self.pieces = [piece]
        if quick():
            self.far = swap(piece, 2)
            self.near = swap(piece, 1)

    def finish(self):
        if not quick():
            return spread(self.pieces[0])
        far = hold(self.far)
        return [self.pieces[0], far, self.near, swap(far, 1)]


class Collect:
    def __init__(self, partials):
        self.partials = partials
        if quick():
            self.second = swap(partials[3], 1)
            self.first = swap(partials[2], 1)

    def turn(self):
        if quick():
            total = add_low([self.partials[1], self.second])
            self.far = swap(total, 2)

    def finish(self):
        if quick():
            return [self.partials[0], self.first, self.far]
        kept = [[partial] for partial in self.partials]
        for bit in reversed(seq_bits()):
            half = len(kept) // 2
            sent = [part[0] if len(part) == 1 else add_low(part) for part in kept[half:]]
            kept = [own + [swap(other, bit)] for own, other in zip(kept[:half], sent)]
        return kept[0]


def add_low(addends):
    def kernel(*refs):
        refs[-1][...] = add_up(refs[:-1]).astype(low)

    return run(kernel, [shape(addends[0].shape, low)], addends, "add_low", addends[0].size)[0]


def add_high(addends):
    def kernel(*refs):
        refs[-1][...] = add_up(refs[:-1])

    return run(kernel, [shape(addends[0].shape, high)], addends, "add_high", addends[0].size)[0]


def mine(values, axis):
    return lax.dynamic_index_in_dim(values, lax.axis_index("seq"), axis, keepdims=False)


def line_place():
    return lax.axis_index("batch") // 2, lax.axis_index("batch") % 2


def line_groups():
    shards = lax.axis_size("batch")
    return [list(range(side, shards, 2)) for side in range(2)]


def line_order():
    _, side = line_place()
    at = 2 * jnp.arange(lax.axis_size("batch") // 2, dtype=jnp.int32)
    return jnp.concatenate([at + side, at + 1 - side])


def relay_order():
    place, side = line_place()
    at = (place - jnp.arange(4, dtype=jnp.int32)) % 4
    return jnp.concatenate([2 * at + side, 2 * at + 1 - side])


class Relay:
    def __init__(self, values):
        self.line, self.across = [values], []
        self.touch()

    def touch(self):
        newest = self.line[-1] = hold(self.line[-1])
        if len(self.line) < 4:
            shards = lax.axis_size("batch")
            pairs = [(i, (i + 2) % shards) for i in range(shards)]
            self.line.append(lax.ppermute(newest, "batch", pairs))
        self.across.append(to_side(newest))

    def pieces(self):
        return self.line + self.across


def gather_line(values):
    return lax.all_gather(values, "batch", axis=0, tiled=True, axis_index_groups=line_groups())


def to_side(values):
    return swap(values, 1, "batch")


class Scatter:
    def __init__(self, blocks):
        self.keep, sent = blocks
        self.arrived = to_side(sent)

    def turn(self):
        total = add_low([self.keep, self.arrived])
        self.sums = lax.psum_scatter(
            total, "batch", scatter_dimension=0, tiled=False, axis_index_groups=line_groups()
        )

    def finish(self):
        return add_low([self.sums])


class Sum:
    def __init__(self, values):
        bits = [(axis, 1 << i) for axis in ("seq", "batch") for i in range(5)]
        self.left = [(axis, bit) for axis, bit in bits if bit < lax.axis_size(axis)]
        self.values = values
        self.send()

    def send(self):
        axis, bit = self.left.pop(0)
        self.arrived = swap(self.values, bit, axis)

    def turn(self):
        self.values = add_high([self.values, self.arrived])
        if self.left:
            self.send()


def line_pairs(step, count, back):
    pairs = []
    for place in range(count):
        for side in range(2):
            here = (place * 2 + side) * count + place
            there = (((place + step) % count) * 2 + side) * count + place
            pairs.append((there, here) if back else (here, there))
    return pairs


def add_dealt(own, sent, owned):
    def kernel(owned_ref, own_ref, *refs):
        total = add_up(refs[:-1])
        kept = own_ref[...].astype(high)
        refs[-1][...] = jnp.where(owned_ref[0] != 0, kept, total).astype(low)

    outs = [shape(own.shape, low)]
    return run(kernel, outs, [owned, own, *sent], "add_dealt", own.size, scalars=1)[0]


class Return:
    def __init__(self, pieces, blocks):
        self.blocks, self.left = blocks, seq_bits()
        self.arrived = [pieces] + [
            lax.ppermute(pieces, ("batch", "seq"), line_pairs(step, 4, True)) for step in range(1, 4)
        ]

    def turn(self):
        me = lax.axis_index("seq")
        place, _ = line_place()
        if isinstance(self.arrived, list):
            table = (me + jnp.arange(4, dtype=jnp.int32)) % 4
            self.ordered = stack_places(self.arrived, table, self.blocks)
        else:
            self.ordered = self.pick()
        bit = self.left.pop(0)
        self.mine = ((place & bit) == (me & bit)).astype(jnp.int32)[None]
        self.arrived = swap(self.ordered, bit)

    def pick(self):
        return choose(self.ordered, self.arrived, self.mine, low)

    def finish(self):
        return choose(self.ordered, self.arrived, self.mine, high)


def stack_places(pieces, table, blocks):
    rows = pieces[0].shape[0] // blocks

    def kernel(table_ref, *refs):
        out = refs[-1]
        for i, source in enumerate(refs[:-1]):
            where = pl.ds(pl.multiple_of(table_ref[i] * rows, rows), rows)
            for block in range(blocks):
                out[block, where, :] = source[block * rows : (block + 1) * rows, :]

    outs = [shape((blocks, rows * len(pieces), pieces[0].shape[1]), low)]
    return run(kernel, outs, [table, *pieces], "stack_places", 1, scalars=1)[0]


def choose(one, other, first, kind):
    def kernel(first_ref, one_ref, other_ref, out):
        out[...] = jnp.where(first_ref[0] != 0, one_ref[...], other_ref[...]).astype(kind)

    return run(kernel, [shape(one.shape, kind)], [first, one, other], "choose", 1, scalars=1)[0]


def gather_whole(projections, combiners, expanders, reducers):
    count, shards = lax.axis_size("seq"), lax.axis_size("batch")
    blocks, rows, _ = projections.shape
    feeds, _, _ = expanders.shape
    model_width = combiners.shape[2]
    entries = mine(projections.reshape(blocks, rows, 3, count, -1), 3).reshape(blocks, rows, -1)
    expand = mine(expanders.reshape(feeds, rows, shards, count, -1), 3).reshape(feeds, rows, -1)
    reduce = mine(reducers.reshape(feeds, count, -1, model_width), 1)

    def whole(values):
        return lax.all_gather(values, "batch", axis=0, tiled=True)

    leaves = [whole(combiners[i]).reshape(count, -1, model_width) for i in range(blocks)]
    return (
        [whole(entries[i]) for i in range(blocks)],
        [mine(leave, 0) for leave in leaves],
        [whole(expand[i]) for i in range(feeds)],
        [whole(reduce[i]) for i in range(feeds)],
    )


def spread_order(pieces, axis):
    me = lax.axis_index("seq")
    stacked = jnp.stack(pieces)
    offsets = jnp.array([seq_offsets().index(i) for i in range(len(pieces))], jnp.int32)
    ordered = [
        lax.dynamic_index_in_dim(stacked, offsets[me ^ i], 0, keepdims=False)
        for i in range(len(pieces))
    ]
    return jnp.stack(ordered, axis)


def per_device(
    source_tokens,
    target_tokens,
    source_lengths,
    target_lengths,
    projections,
    combiners,
    expanders,
    reducers,
    norm_gains,
    norm_shifts,
    attention_biases,
    expander_biases,
    reducer_biases,
    source_cotangent,
    target_cotangent,
):
    Turn.last, Turn.done = None, norm_gains[:, :128]
    source_tokens, target_tokens = source_tokens[0], target_tokens[0]
    source_cotangent, target_cotangent = source_cotangent[0], target_cotangent[0]
    count, shards = lax.axis_size("seq"), lax.axis_size("batch")
    me = lax.axis_index("seq")
    local_count, model_width = source_tokens.shape
    heads = HEADS // count
    share = model_width // count
    padding_segment = source_lengths.shape[1] - 1

    here = jnp.arange(local_count, dtype=jnp.int32)
    places = jnp.concatenate([(me ^ offset) * local_count + here for offset in seq_offsets()])

    def segments(lengths):
        ends = jnp.cumsum(lengths[0], dtype=jnp.int32)
        return jnp.sum((places[:, None] >= ends[None, :]).astype(jnp.int32), -1, dtype=jnp.int32)

    source_segment, target_segment = segments(source_lengths), segments(target_lengths)
    source_keep = (source_segment[:local_count] < padding_segment).astype(high)[:, None]
    target_keep = (target_segment[:local_count] < padding_segment).astype(high)[:, None]

    def view(query_segment, key_segment, causal):
        def ends_of(values):
            blocks = values.reshape(-1, min(256, values.shape[0]))
            return jnp.min(blocks, 1), jnp.max(blocks, 1)

        query_low, query_high = ends_of(query_segment)
        key_low, key_high = ends_of(key_segment)
        marks = (query_low[:, None] <= key_high[None]) & (key_low[None] <= query_high[:, None])
        if causal:
            place_low, place_high = ends_of(places)
            marks = marks & (place_low[None] <= place_high[:, None])
        tags = (key_segment[:, None], query_segment[None], places[:, None], places[None])
        return marks.astype(jnp.int32), tags

    encoder_view = view(source_segment, source_segment, False)
    self_view = view(target_segment, target_segment, True)
    cross_view = view(target_segment, source_segment, False)

    entry_biases = mine(attention_biases[:, :2].reshape(3, 2, count, share), 2)
    exit_biases = attention_biases[:, 2]
    hidden_biases = mine(expander_biases.reshape(2, shards, count, -1), 2).reshape(2, 1, -1)

    def gain(norm):
        return norm_gains[norm : norm + 1]

    def shift(norm):
        return norm_shifts[norm : norm + 1]

    def exit_bias(block):
        return exit_biases[block : block + 1]

    rows = projections.shape[1]
    feed_rows = reducers.shape[1] // count
    if quick():
        piece = share // shards
        line = (me + jnp.arange(count, dtype=jnp.int32)) % count
        table = jnp.concatenate([me[None], line])

        def entry_cut(block, out, top):
            return [
                (0, block, rows, (0, 0), share, (part * model_width, share), 0, out, top, part * share)
                for part in range(3)
            ]

        moves = entry_cut(0, 0, 0) + [
            (1, block, piece, (0, piece), model_width, (0, 0), 1 + i, 1 + i, block * piece, 0)
            for i in range(count)
            for block in range(3)
        ]
        outs = [shape((rows, 3 * share), low)] + [shape((3 * piece, model_width), low)] * count
        first, *deals = cut([projections, combiners], table, moves, outs, "cut_first")
        entry_relay = Relay(first)
        sent = [
            lax.ppermute(deals[step], ("batch", "seq"), line_pairs(step, count, False))
            for step in range(1, count)
        ]
        lanes = expanders.shape[2] // shards
        moves = entry_cut(1, 2, 0) + entry_cut(2, 2, rows)
        for feed in range(2):
            moves += [
                (1, feed, rows, (0, 0), feed_rows, (part * lanes, feed_rows), 0, feed, 0, part * feed_rows)
                for part in range(shards)
            ]
            moves.append(
                (2, feed, feed_rows, (0, feed_rows), model_width, (0, 0), 0, feed, rows, 0)
            )
        outs = [shape((rows + feed_rows, model_width), low)] * 2
        outs += [shape((2 * rows, 3 * share), low)]
        feed_zero, feed_one, entry_rest = cut(
            [projections, expanders, reducers], table, moves, outs, "cut_rest"
        )
        entry_relay.touch()
        source_spread = Spread(hold(source_tokens))
        entry_relay.touch()
        entry_relay.touch()
        place, _ = line_place()
        order, relayed = line_order(), relay_order()
        entry_table = (order * rows)[None]
        whole_rows = shards * rows
        dealt = add_dealt(deals[0], sent, (place == me).astype(jnp.int32)[None])
        leave_relay = Relay(dealt)
        rest_line = gather_line(hold(entry_rest))
        source_pieces = source_spread.finish()
        encoder_entry = assemble(
            entry_relay.pieces(), (relayed * rows)[None], [(0, rows, whole_rows)], rows
        )[0]
        leave_relay.touch()
        target_spread = Spread(hold(target_tokens))
    else:
        entries, leaves, expand, reduce = gather_whole(
            projections, combiners, expanders, reducers
        )
        encoder_entry, decoder_entry, cross_entry = entries
        source_pieces = spread(source_tokens)
        target_spread = Spread(target_tokens)

    encoder_normed, *projected = project_self(
        source_pieces, gain(0), shift(0), encoder_entry, entry_biases[0]
    )
    if quick():
        leave_relay.touch()
    mixture, total = attend_forward(*encoder_view, *projected, heads, False)
    encoder_stored = (*projected, mixture, total)
    target_pieces = target_spread.finish()
    if quick():
        leave_relay.touch()
        feed_line = gather_line(hold(feed_zero))
        one_line = part_rows(rest_line, 2 * rows, 0, rows)
        two_line = part_rows(rest_line, 2 * rows, rows, rows)
        leaves = assemble(
            leave_relay.pieces(),
            jnp.stack([((relayed % 2) * 4 + relayed // 2) * piece] * 3),
            [(i * piece, piece, shards * piece) for i in range(3)],
            3 * piece,
        )
        one_other = to_side(hold(one_line))
    encoder_partials = Collect(project_out(mixture, leaves[0], count))
    encoder_partials.turn()
    if quick():
        decoder_entry = assemble(
            [one_line, one_other], entry_table, [(0, rows, whole_rows)], rows
        )[0]
    decoder_normed, *projected = project_self(
        target_pieces, gain(2), shift(2), decoder_entry, entry_biases[1]
    )
    if quick():
        feed_other = to_side(hold(feed_line))
        last_line = gather_line(hold(feed_one))
    mixture, total = attend_forward(*self_view, *projected, heads, True)
    decoder_stored = (*projected, mixture, total)
    middle, middle_normed = residual_norm(
        source_tokens, encoder_partials.finish(), exit_bias(0), gain(1), shift(1)
    )
    middle_spread = Spread(middle_normed)
    decoder_partials = Collect(project_out(mixture, leaves[1], count))
    decoder_partials.turn()
    target_incoming, target_incoming_low, target_sum = join_gradient(
        target_cotangent, target_keep, []
    )
    self_out, self_normed = residual_norm(
        target_tokens, decoder_partials.finish(), exit_bias(1), gain(3), shift(3)
    )
    self_spread = Spread(self_normed)
    middle_pieces = middle_spread.finish()
    if quick():
        expand, reduce = [None, None], [None, None]
        feed_parts = [(0, rows, whole_rows), (rows, feed_rows, shards * feed_rows)]
        feed_table = jnp.stack([order * rows, order * feed_rows])
        height = rows + feed_rows
        expand[0], reduce[0] = assemble([feed_line, feed_other], feed_table, feed_parts, height)
        two_other = to_side(hold(two_line))
    encoder_active, encoder_slope, partials = feed_forward(
        middle_pieces, expand[0], reduce[0], hidden_biases[0]
    )
    memory_partials = Collect(partials)
    memory_partials.turn()
    if quick():
        cross_entry = assemble(
            [two_line, two_other], entry_table, [(0, rows, whole_rows)], rows
        )[0]
    memory_low = residual_low(middle, memory_partials.finish(), reducer_biases[0:1])
    memory_spread = Spread(memory_low)
    if quick():
        last_other = to_side(hold(last_line))
    memory_pieces = memory_spread.finish()
    self_pieces = self_spread.finish()
    target_incoming_spread = Spread(hold(target_incoming_low))
    cross_projected = project_cross(self_pieces, memory_pieces, cross_entry, entry_biases[2])
    mixture, total = attend_forward(*cross_view, *cross_projected, heads, False)
    cross_stored = (*cross_projected, mixture, total)
    target_incoming_pieces = target_incoming_spread.finish()
    partials = Collect(project_out(mixture, leaves[2], count))
    partials.turn()
    cross_out, cross_normed = residual_norm(
        self_out, partials.finish(), exit_bias(2), gain(4), shift(4)
    )
    cross_spread = Spread(cross_normed)
    if quick():
        expand[1], reduce[1] = assemble([last_line, last_other], feed_table, feed_parts, height)
    cross_pieces = cross_spread.finish()
    decoder_active, decoder_slope, partials = feed_forward(
        cross_pieces, expand[1], reduce[1], hidden_biases[1]
    )
    decoded_partials = Collect(partials)

    order = line_order() if quick() else None

    def feed_gradients(pieces, normed_pieces, hidden, active):
        pairs = [
            (normed_pieces, [hidden], 0, hidden.shape[1]),
            ([active], pieces, 0, model_width),
        ]
        return outer_sums(pairs, order, "feed_weights", True)

    def exit_gradient(stored, pieces):
        pairs = [([stored[3]], pieces, 0, model_width)]
        return outer_sums(pairs, None, "exit_weights")[0]

    def sums_over_batch(blocks):
        if quick():
            return Scatter(blocks)
        return [
            lax.psum_scatter(part, "batch", scatter_dimension=0, tiled=True) for part in blocks
        ]

    hidden, decoder_hidden_sum, partials = feed_backward(
        target_incoming_pieces, expand[1], reduce[1], decoder_slope
    )
    partials = Collect(partials)
    partials.turn()
    decoded_partials.turn()
    decoder_feed_shares = sums_over_batch(
        feed_gradients(target_incoming_pieces, cross_pieces, hidden, decoder_active)
    )
    incoming, incoming_low, norm_four = norm_backward(
        cross_out, gain(4), target_incoming, partials.finish()
    )
    incoming_spread = Spread(incoming_low)
    decoded_low = residual_low(cross_out, decoded_partials.finish(), reducer_biases[1:2])
    incoming_pieces = incoming_spread.finish()
    cross_joined, cross_sums, partials, memory_partials = attend_backward(
        *cross_view, incoming_pieces, leaves[2], cross_entry, cross_stored, heads, False, True
    )
    memory_partials = Collect(memory_partials)
    memory_partials.turn()
    partials = Collect(partials)
    cross_exit = exit_gradient(cross_stored, incoming_pieces)
    cross_shares = sums_over_batch(
        outer_sums(
            [
                (self_pieces, [cross_joined], 0, share),
                (memory_pieces, [cross_joined], share, 2 * share),
            ],
            order,
            "attention_weights",
        )
    )
    source_incoming, source_incoming_low, source_sum = join_gradient(
        source_cotangent, source_keep, memory_partials.finish()
    )
    source_incoming_spread = Spread(source_incoming_low)
    partials.turn()
    source_incoming_pieces = source_incoming_spread.finish()
    if quick():
        decoder_feed_shares.turn()
    hidden, encoder_hidden_sum, feed_partials = feed_backward(
        source_incoming_pieces, expand[0], reduce[0], encoder_slope
    )
    feed_partials = Collect(feed_partials)
    feed_partials.turn()
    self_incoming, self_incoming_low, norm_three = norm_backward(
        self_out, gain(3), incoming, partials.finish()
    )
    self_incoming_spread = Spread(self_incoming_low)
    encoder_feed_shares = sums_over_batch(
        feed_gradients(source_incoming_pieces, middle_pieces, hidden, encoder_active)
    )
    middle_incoming, middle_incoming_low, norm_one = norm_backward(
        middle, gain(1), source_incoming, feed_partials.finish()
    )
    middle_incoming_spread = Spread(middle_incoming_low)
    self_incoming_pieces = self_incoming_spread.finish()
    if quick():
        cross_shares.turn()
    decoder_exit = exit_gradient(decoder_stored, self_incoming_pieces)
    decoder_joined, decoder_sums, decoder_partials, _ = attend_backward(
        *self_view, self_incoming_pieces, leaves[1], decoder_entry, decoder_stored, heads, True, False
    )
    decoder_partials = Collect(decoder_partials)
    decoder_blocks = outer_sums(
        [([decoder_normed], [decoder_joined], 0, 3 * share)], order, "attention_weights"
    )
    middle_incoming_pieces = middle_incoming_spread.finish()
    encoder_exit = exit_gradient(encoder_stored, middle_incoming_pieces)
    exits = [encoder_exit, decoder_exit, cross_exit]
    if quick():
        table = ((order % 2) * 4 + order // 2) * piece
        decoder_shares = Scatter(join_blocks(decoder_blocks, exits, table))
        encoder_feed_shares.turn()
        decoder_feed_share, cross_share = decoder_feed_shares.finish(), cross_shares.finish()
    else:
        decoder_shares = sums_over_batch(decoder_blocks)
    decoder_partials.turn()
    encoder_joined, encoder_sums, encoder_partials, _ = attend_backward(
        *encoder_view,
        middle_incoming_pieces,
        leaves[0],
        encoder_entry,
        encoder_stored,
        heads,
        False,
        False,
    )
    encoder_partials = Collect(encoder_partials)
    encoder_shares = sums_over_batch(
        outer_sums([([encoder_normed], [encoder_joined], 0, 3 * share)], order, "attention_weights")
    )
    encoder_partials.turn()
    if quick():
        decoder_shares.turn()
        encoder_feed_share = encoder_feed_shares.finish()
        decoder_feed_spread = Spread(decoder_feed_share)
    target_gradient, _, norm_two = norm_backward(
        target_tokens, gain(2), self_incoming, decoder_partials.finish()
    )
    source_gradient, _, norm_zero = norm_backward(
        source_tokens, gain(0), middle_incoming, encoder_partials.finish()
    )

    norms = (norm_zero, norm_one, norm_two, norm_three, norm_four)
    if quick():
        owners = me ^ jnp.array(seq_offsets(), jnp.int32)
        entry_moves = [
            ((0, rows), (part * share, share), (0, 0), (part * model_width, share))
            for part in range(3)
        ]
        expand_moves = [
            ((0, rows), (part * feed_rows, feed_rows), (0, 0), (part * lanes, feed_rows))
            for part in range(shards)
        ]
        reduce_moves = [((rows, feed_rows), (0, model_width), (0, feed_rows), (0, 0))]

        def finish_entry(block, shares, former):
            outputs = [(projections.shape, block, entry_moves)]
            return finish(shares, owners, former, outputs, "finish_entry")

        def finish_feed(feed, shares, former):
            outputs = [
                (expanders.shape, feed, expand_moves),
                (reducers.shape, feed, reduce_moves),
            ]
            return finish(shares, owners, former, outputs, "finish_feed")

        laid = lay_sums(
            [*norms, source_sum, target_sum],
            [encoder_sums, decoder_sums, cross_sums],
            [encoder_hidden_sum, decoder_hidden_sum],
            me[None],
            shards,
        )
        summed = Sum(laid)
        encoder_shares.turn()
        cross_spread = Spread(cross_share)
        feeds_whole = finish_feed(1, decoder_feed_spread.finish(), [])
        summed.turn()
        feed_spread = Spread(encoder_feed_share)
        entry_whole = finish_entry(2, cross_spread.finish(), [])
        summed.turn()
        decoder_share, exit_share = part_blocks(
            decoder_shares.finish(), rows, 3, piece, model_width
        )
        feeds_whole = finish_feed(0, feed_spread.finish(), feeds_whole)
        exit_return = Return(exit_share, 3)
        summed.turn()
        decoder_spread = Spread(decoder_share)
        summed.turn()
        exit_return.turn()
        entry_whole = finish_entry(1, decoder_spread.finish(), entry_whole)
        summed.turn()
        summed = summed.values
        exit_return.turn()
        combiners_gradient = exit_return.finish()
        encoder_spread = Spread(encoder_shares.finish())
        entry_whole = finish_entry(0, encoder_spread.finish(), entry_whole)
        projections_gradient = entry_whole[0]
        expanders_gradient, reducers_gradient = feeds_whole
        norm_sums = summed[:15].reshape(5, 3, -1)
        exit_sums = summed[15:17]
        inner = summed[17:23].reshape(3, 2, -1)
        hidden_sums = summed[23 : 23 + 2 * expanders.shape[2] // model_width].reshape(2, -1)
    else:
        wholes = [
            lax.dynamic_update_slice(
                jnp.zeros((count,) + part.shape, low), part[None], (me, 0, 0)
            ).reshape(-1, model_width)
            for part in exits
        ]
        combiners_gradient = jnp.stack([sums_over_batch([part])[0] for part in wholes])
        combiners_gradient = lax.psum(combiners_gradient, "seq").astype(high)
        entry_shares = [encoder_shares[0], decoder_shares[0], jnp.concatenate(cross_shares, 1)]
        feed_shares = [encoder_feed_shares, decoder_feed_shares]

        def whole(part, groups):
            pieces = [p.reshape(rows, groups, -1) for p in spread(part)]
            return spread_order(pieces, 2).reshape(rows, -1).astype(high)

        projections_gradient = jnp.stack([whole(part, 3) for part in entry_shares])
        expanders_gradient = jnp.stack([whole(part[0], shards) for part in feed_shares])
        reducers_gradient = jnp.stack(
            [spread_order(spread(part[1]), 0).reshape(-1, model_width) for part in feed_shares]
        ).astype(high)
        inner = jnp.stack([encoder_sums, decoder_sums, cross_sums])
        inner = lax.dynamic_update_slice(
            jnp.zeros((3, 2, count, share), high), inner[:, :, None], (0, 0, me, 0)
        )
        hidden_sums = jnp.stack([encoder_hidden_sum, decoder_hidden_sum])
        hidden_sums = hidden_sums.reshape(2, shards, 1, -1)
        hidden_sums = lax.dynamic_update_slice(
            jnp.zeros((2, shards, count, hidden_sums.shape[3]), high), hidden_sums, (0, 0, me, 0)
        )
        parts = [jnp.stack(norms), jnp.concatenate([source_sum, target_sum]), inner, hidden_sums]
        summed = lax.psum(parts, ("batch", "seq"))
        norm_sums, exit_sums, inner, hidden_sums = summed
        inner = inner.reshape(3, 2, -1)
        hidden_sums = hidden_sums.reshape(2, -1)
    outer = jnp.stack([norm_sums[1, 2], norm_sums[3, 2], norm_sums[4, 2]])
    return (
        memory_low[None],
        decoded_low[None],
        source_gradient[None],
        target_gradient[None],
        projections_gradient,
        combiners_gradient,
        expanders_gradient,
        reducers_gradient,
        norm_sums[:, 0],
        norm_sums[:, 1],
        jnp.concatenate([inner, outer[:, None]], 1),
        hidden_sums,
        exit_sums,
    )


def solution(mesh):
    in_specs = (
        P("batch", "seq", None),
        P("batch", "seq", None),
        P("batch", None),
        P("batch", None),
        P(None, "batch", None),
        P(None, "batch", None),
        P(None, "batch", None),
        P(None, "batch", None),
        P(),
        P(),
        P(),
        P(),
        P(),
        P("batch", "seq", None),
        P("batch", "seq", None),
    )
    out_specs = (
        P("batch", "seq", None),
        P("batch", "seq", None),
        P("batch", "seq", None),
        P("batch", "seq", None),
        P(None, "batch", None),
        P(None, "batch", None),
        P(None, "batch", None),
        P(None, "batch", None),
        P(),
        P(),
        P(),
        P(),
        P(),
    )
    return jax.shard_map(
        per_device, mesh=mesh, in_specs=in_specs, out_specs=out_specs, check_vma=False
    )
```
